128 devices in a mesh: row: 4 (over x), col: 32 (over z, y, core).
Axes of the slice: x: 4, y: 4, z: 4, core: 2. Of those that a mesh axis runs over, the one named last changes fastest.
Arguments:
- a_tiles: bfloat16 [12288, 3200], P(('row', 'col')), may hold values from -4 to 4
- a_owner: int32 [12288], P(('row', 'col')), may hold values from 0 to 127, as said below
- a_offset: int32 [12288, 2], P(('row', 'col')), may hold values from 0 to 560, as said below
- b_tiles: bfloat16 [12288, 3200], P(('row', 'col')), may hold values from -6 to 6
- b_owner: int32 [12288], P(('row', 'col')), may hold values from 0 to 127, as said below
- b_offset: int32 [12288, 2], P(('row', 'col')), may hold values from 0 to 560, as said below
- patch_valid: int32 [48, 512], P('row', 'col'), may hold values 0 or 1
Outputs:
- flow_field: float32 [2, 48, 512], P(None, 'row', 'col')
- mesh_field: float32 [2, 48, 512], P(None, 'row', 'col')
The draws below stay inside these ranges and needn't reach their ends.
Inputs may be any that keep to these rules, and one draw needn't show every extreme that they name: `a_owner`: each region owner receives exactly 96 first-section tiles, one for every tile position of its region; a device sends either no tile or exactly 1 tiles to one owner. `a_offset`: row offsets are multiples of 40 below 480, column offsets multiples of 80 below 640; each owner's tiles cover its region exactly once. `b_owner`: each region owner receives exactly 96 next-section tiles, one for every tile position of its region; a device sends either no tile or exactly 1 tiles to one owner. `b_offset`: row offsets are multiples of 40 below 480, column offsets multiples of 80 below 640; each owner's tiles cover its region exactly once.
All inputs are finite; a program needn't handle non-finite values. No bound on the sum of `patch_valid` on one device may be relied on, other than what follows from the above.
Results may differ from the reference program's by a relative error of at most 0.004.
Values may be sent and summed in bfloat16 or wider, within the bound.
No kernel may reach another device: no remote copies, remote signals or barrier semaphores. Data moves between devices by JAX's collectives and lax.ppermute only.
A program may use at most 64 MiB of HBM per device.

```python
import math
import jax
import jax.numpy as jnp
from jax import lax

PATCH = 160
STRIDE = 40
TY = 12
TX = 8
SWEEPS = 3
MARGIN = 60
RH = 480
RW = 640
TH = 40
TW = 80
TPR = 96
CAP = 1
NGH = 48
NGW = 512
SH = 1920
SW = 20480
NTILES = 12288


def routing(key, salt):
    salted = jax.random.fold_in(key, salt)
    subkeys = jax.random.split(salted, 5)
    devices = NTILES // TPR
    owners_each = TPR // CAP
    offset_set = jax.random.permutation(subkeys[0], devices)[:owners_each]
    sender_rank = jax.random.permutation(subkeys[1], devices)
    owner_label = jax.random.permutation(subkeys[2], devices)
    tile_perm = jax.vmap(lambda sub: jax.random.permutation(sub, TPR))(jax.random.split(subkeys[3], devices))
    place_perm = jax.vmap(lambda sub: jax.random.permutation(sub, TPR))(jax.random.split(subkeys[4], devices))
    group_index = tile_perm // CAP
    slot_index = tile_perm % CAP
    tile_owner = owner_label[(sender_rank[:, None] + offset_set[group_index]) % devices]
    position = place_perm[tile_owner, group_index * CAP + slot_index]
    row_offset = position // TX * TH
    col_offset = position % TX * TW
    offsets = jnp.stack([row_offset, col_offset], axis=-1)
    return (tile_owner.reshape(-1).astype(jnp.int32), offsets.reshape(-1, 2).astype(jnp.int32))


def textures(key):
    salted = jax.random.fold_in(key, 11)
    subkeys = jax.random.split(salted, 3)
    shifts = jax.random.randint(subkeys[2], (SH // RH, SW // RW, 2), -STRIDE, STRIDE + 1)
    texture = jax.random.truncated_normal(subkeys[0], -4.0, 4.0, (SH, SW), jnp.float32)
    noise_field = jax.random.truncated_normal(subkeys[1], -4.0, 4.0, (SH, SW), jnp.float32)
    pixel_rows = jnp.arange(SH, dtype=jnp.int32)
    pixel_cols = jnp.arange(SW, dtype=jnp.int32)
    region_row = (pixel_rows // RH)[:, None]
    region_col = (pixel_cols // RW)[None, :]
    shift_y = shifts[:, :, 0][region_row, region_col]
    shift_x = shifts[:, :, 1][region_row, region_col]
    source_y = jnp.clip(pixel_rows[:, None] - shift_y, 0, SH - 1)
    source_x = jnp.clip(pixel_cols[None, :] - shift_x, 0, SW - 1)
    section_one = texture
    section_two = texture[source_y, source_x] + 0.5 * noise_field
    return (section_one, section_two)


def cut_tiles(slab, tile_owner, tile_offset):
    region_cols = SW // RW
    block_row = tile_owner // region_cols * TY + tile_offset[:, 0] // TH
    block_col = tile_owner % region_cols * TX + tile_offset[:, 1] // TW
    blocks = slab.reshape(SH // TH, TH, SW // TW, TW).transpose(0, 2, 1, 3)
    return blocks[block_row, block_col].reshape(-1, TH * TW)


def draw_a_owner(key, part):
    return routing(key, 1)[0]


def draw_a_offset(key, part):
    return routing(key, 1)[1]


def draw_b_owner(key, part):
    return routing(key, 2)[0]


def draw_b_offset(key, part):
    return routing(key, 2)[1]


def draw_a_tiles(key, part):
    tile_owner, tile_offset = routing(key, 1)
    section_one, section_two = textures(key)
    return cut_tiles(section_one, tile_owner, tile_offset).astype(jnp.bfloat16)


def draw_b_tiles(key, part):
    tile_owner, tile_offset = routing(key, 2)
    section_one, section_two = textures(key)
    return cut_tiles(section_two, tile_owner, tile_offset).astype(jnp.bfloat16)


def touch_ends(values, own_key, least, top_value):
    index_at = [jax.random.randint(jax.random.fold_in(own_key, axis), (), 0, length) for axis, length in enumerate(values.shape)]
    widest = values.shape.index(max(values.shape))
    next_to = index_at[:widest] + [(index_at[widest] + 1) % values.shape[widest]] + index_at[widest + 1:]
    return values.at[tuple(index_at)].set(least).at[tuple(next_to)].set(top_value)


def setup_inputs(seed: int = 0) -> dict:
    key_list = jax.random.split(jax.random.key(seed), 8)
    return {
        "a_tiles": draw_a_tiles(jax.random.fold_in(key_list[7], 71), 0),
        "a_owner": draw_a_owner(jax.random.fold_in(key_list[7], 71), 0),
        "a_offset": draw_a_offset(jax.random.fold_in(key_list[7], 71), 0),
        "b_tiles": draw_b_tiles(jax.random.fold_in(key_list[7], 71), 0),
        "b_owner": draw_b_owner(jax.random.fold_in(key_list[7], 71), 0),
        "b_offset": draw_b_offset(jax.random.fold_in(key_list[7], 71), 0),
        "patch_valid": touch_ends((jax.random.randint(key_list[6], (NGH, NGW), 0, 4) < 3).astype(jnp.int32), jax.random.fold_in(key_list[6], 1), 0, 1),
    }


stiffness = 1.0
tiny = 1e-06

def dft_tables():
    freq_index = jnp.arange(PATCH, dtype=jnp.int32)
    phase = (freq_index[:, None] * freq_index[None, :] % PATCH).astype(jnp.float32) * (2.0 * math.pi / PATCH)
    return (jnp.cos(phase).astype(jnp.bfloat16), jnp.sin(phase).astype(jnp.bfloat16))

def rounded(values):
    return lax.optimization_barrier(values.astype(jnp.bfloat16)).astype(jnp.float32)

def product(form, left_side, right_side):
    return jnp.einsum(form, left_side.astype(jnp.float32), right_side.astype(jnp.float32), precision=lax.Precision.HIGHEST)

def forward(patches, cosine_table, sine_table):
    right_side = jnp.concatenate([cosine_table, sine_table], axis=1)
    first_segment = rounded(product('nyx,xk->nyk', patches, right_side))
    halves = first_segment.reshape(first_segment.shape[0], PATCH, 2, PATCH)
    left_real = jnp.stack([cosine_table, -sine_table])
    left_imag = jnp.stack([-sine_table, -cosine_table])
    return (product('hky,nyhj->nkj', left_real, halves), product('hky,nyhj->nkj', left_imag, halves))

def inverse(cross_real, cross_imag, cosine_table, sine_table):
    stacked = jnp.stack([cross_real, cross_imag], axis=2)
    right_u = jnp.stack([cosine_table, -sine_table])
    right_v = jnp.stack([sine_table, cosine_table])
    inverse_u = rounded(product('nyhx,hxk->nyk', stacked, right_u))
    inverse_v = rounded(product('nyhx,hxk->nyk', stacked, right_v))
    stacked_uv = jnp.stack([inverse_u, inverse_v], axis=2)
    left_real = jnp.stack([cosine_table, -sine_table])
    return product('hky,nyhj->nkj', left_real, stacked_uv)

def patch_norm(patches):
    values = patches.astype(jnp.float32)
    return PATCH * jnp.sqrt(lax.optimization_barrier(jnp.mean(values * values, axis=(1, 2))) + tiny)

def correlate(patch_a, patch_b, cosine_table, sine_table):
    real_a, imag_a = forward(patch_a, cosine_table, sine_table)
    real_b, imag_b = forward(patch_b, cosine_table, sine_table)
    inv_norms = (1.0 / (patch_norm(patch_a) * patch_norm(patch_b)))[:, None, None]
    cross_real = rounded((real_a * real_b + imag_a * imag_b) * inv_norms)
    cross_imag = rounded((real_a * imag_b - imag_a * real_b) * inv_norms)
    correlation = inverse(cross_real, cross_imag, cosine_table, sine_table) / (PATCH * PATCH)
    weight = correlation * correlation
    weight_sum = lax.optimization_barrier(jnp.sum(weight, axis=(1, 2)))
    freq_index = jnp.arange(PATCH, dtype=jnp.int32)
    shift_units = jnp.where(freq_index < PATCH // 2, freq_index, freq_index - PATCH).astype(jnp.float32) * (16.0 / PATCH)
    flow_y = lax.optimization_barrier(jnp.sum(weight * shift_units[None, :, None], axis=(1, 2))) / (1.0 + weight_sum)
    flow_x = lax.optimization_barrier(jnp.sum(weight * shift_units[None, None, :], axis=(1, 2))) / (1.0 + weight_sum)
    return (flow_y, flow_x, weight_sum / (1.0 + weight_sum))

def assemble(tiles, tile_owner, tile_offset):
    region_cols = SW // RW
    block_row = tile_owner // region_cols * TY + tile_offset[:, 0] // TH
    block_col = tile_owner % region_cols * TX + tile_offset[:, 1] // TW
    blocks = jnp.zeros((SH // TH, SW // TW, TH * TW), tiles.dtype).at[block_row, block_col].set(tiles)
    return blocks.reshape(SH // TH, SW // TW, TH, TW).transpose(0, 2, 1, 3).reshape(SH, SW)

def reference(a_tiles, a_owner, a_offset, b_tiles, b_owner, b_offset, patch_valid):
    cosine_table, sine_table = dft_tables()
    images = jnp.stack([assemble(a_tiles, a_owner, a_offset), assemble(b_tiles, b_owner, b_offset)])
    padded = jnp.pad(images, ((0, 0), (MARGIN, MARGIN), (MARGIN, MARGIN)))

    def one_row(grid_row):
        band_strip = lax.dynamic_slice(padded, (grid_row * 0, grid_row * STRIDE, grid_row * 0), (2, PATCH, padded.shape[2]))
        pieces = [band_strip[:, :, column_step * STRIDE:column_step * STRIDE + NGW * STRIDE] for column_step in range(4)]
        windows = jnp.stack(pieces, 0).reshape(4, 2, PATCH, NGW, STRIDE).transpose(1, 3, 2, 0, 4).reshape(2, NGW, PATCH, PATCH)
        return correlate(windows[0], windows[1], cosine_table, sine_table)
    flow_y, flow_x, confidence = lax.map(one_row, jnp.arange(NGH, dtype=jnp.int32))
    flow_field = jnp.stack([flow_y, flow_x])
    valid_float = patch_valid.astype(jnp.float32)
    strength = valid_float * confidence
    data_pull = strength[None] * flow_field
    mesh_field = valid_float[None] * flow_field
    for sweep_index in range(SWEEPS):
        padded_mesh = jnp.pad(mesh_field, ((0, 0), (1, 1), (1, 1)))
        beside_all = padded_mesh[:, :-2, 1:-1] + padded_mesh[:, 2:, 1:-1] + padded_mesh[:, 1:-1, :-2] + padded_mesh[:, 1:-1, 2:]
        mesh_field = (data_pull + stiffness * beside_all) / (strength[None] + 4.0 * stiffness)
    return (flow_field, mesh_field)
```

```python
import math

import jax
import jax.numpy as jnp
import numpy as np
from jax import lax
from jax.experimental import pallas as pl
from jax.experimental.pallas import tpu as pltpu
from jax.sharding import PartitionSpec as P

PATCH = 160
STRIDE = 40
TY = 12
TX = 8
SWEEPS = 3
MARGIN = 60
HALF = PATCH // 2
FREQ = HALF + 1
WIN = 3
GROUPS = 6
BLOCKS = 11
ROWS = 16 * BLOCKS
IMG_H = 640
IMG_W = 896
FIRST_H = 608

stiffness = 1.0
tiny = 1e-06


def trig():
    k = np.arange(FREQ)
    n = np.arange(PATCH)
    phase = (k[:, None] * n[None, :] % PATCH).astype(np.float64) * (2.0 * math.pi / PATCH)
    cosine, sine = np.cos(phase), np.sin(phase)
    sine[0] = 0.0
    sine[HALF] = 0.0
    return cosine, sine


def tables():
    cosine, sine = trig()
    first = np.zeros((256, 512))
    for w in range(WIN):
        rows = slice(STRIDE * w, STRIDE * w + PATCH)
        first[rows, FREQ * w : FREQ * (w + 1)] = cosine.T
        first[rows, 256 + FREQ * w : 256 + FREQ * (w + 1)] = sine.T
    cos_pad = np.zeros((8 * BLOCKS, PATCH))
    sin_pad = np.zeros((8 * BLOCKS, PATCH))
    cos_pad[:FREQ] = cosine
    sin_pad[:FREQ] = sine
    mixed = np.stack([cos_pad.reshape(BLOCKS, 8, PATCH), sin_pad.reshape(BLOCKS, 8, PATCH)], 1)
    mixed = mixed.reshape(ROWS, PATCH)
    second = np.zeros((2, ROWS, ROWS))
    second[0, :, :PATCH] = mixed
    second[1, :, 8 : 8 + PATCH] = mixed
    half = np.ones((FREQ, 1))
    half[0] = half[HALF] = 0.5
    even = (cosine * half)[:, :HALF].copy()
    even[:, 0] = (cosine * half)[:, HALF]
    odd = sine[:, :HALF].copy()
    rows_inv = np.zeros((PATCH, BLOCKS, 2, 8))
    even_pad = np.zeros((8 * BLOCKS, HALF))
    odd_pad = np.zeros((8 * BLOCKS, HALF))
    even_pad[:FREQ] = even
    odd_pad[:FREQ] = odd
    rows_inv[:HALF, :, 0] = even_pad.T.reshape(HALF, BLOCKS, 8)
    rows_inv[HALF:, :, 1] = odd_pad.T.reshape(HALF, BLOCKS, 8)
    rows_inv[HALF, :, 0] = even_pad.T.reshape(HALF, BLOCKS, 8)[0]
    rows_inv = rows_inv.reshape(PATCH, ROWS)
    cols_even = np.zeros((256, 256))
    cols_odd = np.zeros((256, 256))
    for w in range(WIN):
        cols_even[FREQ * w : FREQ * (w + 1), HALF * w : HALF * (w + 1)] = even
        cols_odd[FREQ * w : FREQ * (w + 1), HALF * w : HALF * (w + 1)] = odd
    select = np.zeros((1280, 128))
    for w in range(WIN):
        lanes = np.arange(FREQ) + FREQ * w
        select[lanes, w] = half[:, 0]
        select[256 + lanes, w] = 1.0
        select[512 + HALF * w + np.arange(HALF), 32 + w] = 1.0
        select[768 + lanes, 64 + w] = half[:, 0]
        select[1024 + lanes, 64 + w] = 1.0
    window = np.zeros((IMG_W, 128))
    for j in range(16):
        for kind in range(3):
            window[STRIDE * j : STRIDE * j + PATCH, 32 * kind + j] = 1.0
    as_bf16 = lambda x: jnp.asarray(x.astype(jnp.bfloat16))
    return tuple(as_bf16(x) for x in (first, second, rows_inv, cols_even, cols_odd, select, window))


def dot(a, b):
    return lax.dot_general(a, b, (((1,), (0,)), ((), ())), preferred_element_type=jnp.float32)


def dot_exact(a, b):
    return lax.dot_general(
        a,
        b,
        (((1,), (0,)), ((), ())),
        preferred_element_type=jnp.float32,
        precision=lax.Precision.HIGHEST,
    )


def window_norms(img_ref, cells_ref, window):
    for c in range(8):
        values = img_ref[80 * c : 80 * c + 80, :].astype(jnp.float32)
        squares = (values * values).reshape(2, 5, 8, IMG_W).sum(axis=1)
        sums = squares.sum(axis=1)
        cells_ref[2 * c : 2 * c + 2, :] = sums
    cells = cells_ref[...]
    row = lax.broadcasted_iota(jnp.int32, (16, 16), 0)
    col = lax.broadcasted_iota(jnp.int32, (16, 16), 1)
    band = ((col >= row) & (col < row + 4)).astype(jnp.float32)
    total = dot_exact(dot_exact(band, cells), window)
    return total / (PATCH * PATCH) + tiny


def correlate_kernel(
    img_a, img_b, first, second, rows_inv, cols_even, cols_odd, select, window, out, fa, fb, cells, raw
):
    window_f32 = window[...].astype(jnp.float32)
    mean_a = window_norms(img_a, cells, window_f32)
    mean_b = window_norms(img_b, cells, window_f32)
    for g in range(GROUPS):
        lo = WIN * STRIDE * g
        for img, dst in ((img_a, fa), (img_b, fb)):
            dst[g] = dot(img[:FIRST_H, lo : lo + 256], first[...]).astype(jnp.bfloat16)

    sub = lax.broadcasted_iota(jnp.int32, (8, 256), 0)
    lane = lax.broadcasted_iota(jnp.int32, (8, 256), 1)
    top_half = jnp.where(sub == 0, 0.5, 1.0)
    top_half2 = jnp.concatenate([top_half, top_half], axis=1)
    slot_zero = lane % HALF == 0
    shift_x = jnp.where(slot_zero, -8.0, 0.4 * (lane % HALF).astype(jnp.float32))[:1]
    sub_f = jnp.concatenate([sub, sub], axis=1).astype(jnp.float32)

    def weighted_rows(x):
        total = x[1, 0] + x[1, 1]
        for t in range(2, BLOCKS - 1):
            total = total + (x[t, 0] + x[t, 1])
        return total + x[0, 1] + (x[0, 0] * (top_half2 if x.shape[-1] == 512 else top_half) + 0.5 * x[BLOCKS - 1, 0])

    def one(g, q, parity):
        start = pl.multiple_of(80 * q + 32 * parity, 16)
        spec = []
        for src in (fa, fb):
            s = dot(second[parity], src[g, pl.ds(start, ROWS), :]).reshape(BLOCKS, 2, 8, 512)
            cc, cs = s[:, 0, :, :256], s[:, 0, :, 256:]
            sc, ss = s[:, 1, :, :256], s[:, 1, :, 256:]
            spec.append((cc - ss, sc + cs, cc + ss, sc - cs))
        (a1, a2, a3, a4), (b1, b2, b3, b4) = spec
        plus_r = a1 * b1 + a2 * b2
        plus_i = a1 * b2 - a2 * b1
        minus_r = a3 * b3 + a4 * b4
        minus_i = a3 * b4 - a4 * b3
        dcc = plus_r + minus_r
        dss = minus_r - plus_r
        dsc = plus_i + minus_i
        dcs = plus_i - minus_i
        d = jnp.stack(
            [jnp.concatenate([dcc, dcs], axis=2), jnp.concatenate([dsc, dss], axis=2)], axis=1
        )
        weight = weighted_rows(d * d)
        d16 = d.reshape(ROWS, 512).astype(jnp.bfloat16)
        inv = dot(rows_inv[...], d16)
        prod = (inv[:HALF] * inv[HALF:]).reshape(10, 8, 512)
        run = prod[9]
        ramp = prod[9]
        for t in range(8, 0, -1):
            run = run + prod[t]
            ramp = ramp + run
        run = run + prod[0]
        flow_y = 3.2 * ramp + 0.4 * sub_f * run
        flow_y = jnp.where(sub_f == 0.0, flow_y - 8.0 * prod[0], flow_y)
        even = dot(d16[:, :256], cols_even[...]).reshape(BLOCKS, 2, 8, 256)
        odd = dot(d16[:, 256:], cols_odd[...]).reshape(BLOCKS, 2, 8, 256)
        flow_x = weighted_rows(even * jnp.where(slot_zero[None, None], even, odd))
        i = 2 * q + parity
        raw[g, pl.ds(i, 1), 0:512] = jnp.sum(flow_y, axis=0, keepdims=True)
        raw[g, pl.ds(i, 1), 512:768] = jnp.sum(flow_x, axis=0, keepdims=True) * shift_x
        raw[g, pl.ds(i, 1), 768:1280] = jnp.sum(weight, axis=0, keepdims=True)

    raw[:, 12:16, :] = jnp.zeros((GROUPS, 4, 1280), jnp.float32)

    def step(n, carry):
        g = n // 6
        q = n % 6
        one(g, q, 0)
        one(g, q, 1)
        return carry

    lax.fori_loop(0, GROUPS * 6, step, 0)
    sums = dot_exact(raw[...].reshape(GROUPS * 16, 1280), select[...].astype(jnp.float32))
    sums = sums.reshape(GROUPS, 16, 128)
    lane128 = lax.broadcasted_iota(jnp.int32, (16, 128), 1) % 32
    total = sums[0]
    for g in range(1, GROUPS):
        piece = sums[g] if g < 5 else jnp.where(lane128 == 0, sums[g], 0.0)
        total = total + pltpu.roll(piece, WIN * g, axis=1)
    scale = (1.0 / (PATCH * PATCH)) / (mean_a * mean_b)
    unit = (2.0 / (PATCH * PATCH)) ** 2 * HALF / (PATCH * PATCH)
    total = total * (scale * unit)
    lane_all = lax.broadcasted_iota(jnp.int32, (16, 128), 1)
    weight = jnp.where(lane_all >= 64, total * HALF, 0.0)
    down = 1.0 + weight + pltpu.roll(weight, 96, axis=1) + pltpu.roll(weight, 64, axis=1)
    out[...] = jnp.where(lane_all >= 64, weight, total) / down


def correlate(img_a, img_b):
    return pl.pallas_call(
        correlate_kernel,
        out_shape=jax.ShapeDtypeStruct((16, 128), jnp.float32),
        scratch_shapes=[
            pltpu.VMEM((GROUPS, FIRST_H, 512), jnp.bfloat16),
            pltpu.VMEM((GROUPS, FIRST_H, 512), jnp.bfloat16),
            pltpu.VMEM((16, IMG_W), jnp.float32),
            pltpu.VMEM((GROUPS, 16, 1280), jnp.float32),
        ],
    )(img_a, img_b, *tables())


def extended_2(block, sides, width):
    for axis, dim in sides:
        count = lax.axis_size(axis)
        forward = [(i, i + 1) for i in range(count - 1)]
        backward = [(target, source) for source, target in forward]
        low = lax.ppermute(
            lax.slice_in_dim(block, block.shape[dim] - width, None, axis=dim), axis, forward
        )
        high = lax.ppermute(lax.slice_in_dim(block, 0, width, axis=dim), axis, backward)
        block = jnp.concatenate([low, block, high], axis=dim)
    return block


def outgoing(tiles, tile_owner, tile_offset, slot_count, tile_h, tile_w):
    select = (jnp.arange(slot_count, dtype=jnp.int32)[:, None] == tile_owner[None, :]).astype(
        jnp.bfloat16
    )
    position = tile_offset[:, 0] // tile_h * TX + tile_offset[:, 1] // tile_w + 1
    sent_tiles = jnp.dot(select, tiles, preferred_element_type=jnp.float32).astype(jnp.bfloat16)
    slot_code = jnp.dot(
        select, position.astype(jnp.bfloat16)[:, None], preferred_element_type=jnp.float32
    ).astype(jnp.bfloat16)
    return (sent_tiles, slot_code)


def incoming(received, slot_code, tile_count, tile_h, tile_w):
    wanted = jnp.arange(1, tile_count + 1, dtype=jnp.int32).astype(jnp.float32)
    select = (slot_code.astype(jnp.float32)[None, :] == wanted[:, None]).astype(jnp.bfloat16)
    blocks = jnp.dot(select, received, preferred_element_type=jnp.float32).astype(jnp.bfloat16)
    return (
        blocks.reshape(TY, TX, tile_h, tile_w)
        .transpose(0, 2, 1, 3)
        .reshape(TY * tile_h, TX * tile_w)
    )


def per_device(a_tiles, a_owner, a_offset, b_tiles, b_owner, b_offset, patch_valid):
    grid_rows, grid_cols = patch_valid.shape
    tile_h = grid_rows * STRIDE // TY
    tile_w = grid_cols * STRIDE // TX
    tile_count, tile_size = a_tiles.shape
    devices = lax.axis_size("row") * lax.axis_size("col")
    send_a, code_a = outgoing(a_tiles, a_owner, a_offset, devices, tile_h, tile_w)
    send_b, code_b = outgoing(b_tiles, b_owner, b_offset, devices, tile_h, tile_w)
    code = jnp.pad(jnp.concatenate([code_a, code_b], axis=1), ((0, 0), (0, 126)))
    packed = jnp.concatenate([send_a, send_b, code], axis=1).reshape(devices, 51, 128)
    got = lax.all_to_all(packed, ("row", "col"), split_axis=0, concat_axis=0, tiled=True)
    got_a = got[:, :25].reshape(devices, tile_size)
    got_b = got[:, 25:50].reshape(devices, tile_size)
    canvas_a = incoming(got_a, got[:, 50, 0], tile_count, tile_h, tile_w)
    canvas_b = incoming(got_b, got[:, 50, 1], tile_count, tile_h, tile_w)
    images = jnp.stack([canvas_a, canvas_b])
    padded = extended_2(images, (("row", 1), ("col", 2)), MARGIN)
    padded = jnp.pad(
        padded, ((0, 0), (0, IMG_H - padded.shape[1]), (0, IMG_W - padded.shape[2]))
    )
    result = correlate(padded[0], padded[1])
    flow_field = jnp.stack([result[:grid_rows, :grid_cols], result[:grid_rows, 32 : 32 + grid_cols]])
    confidence = result[:grid_rows, 64 : 64 + grid_cols]
    valid_float = patch_valid.astype(jnp.float32)
    strength = valid_float * confidence
    start = valid_float[None] * flow_field
    fields = jnp.concatenate([start, (strength + 4.0 * stiffness)[None]])
    fields = extended_2(fields, (("row", 1), ("col", 2)), SWEEPS)
    mesh = fields[:2]
    down = fields[2]
    inside = down > 0.0
    rest = jnp.where(inside, 1.0 / jnp.where(inside, down, 1.0), 0.0)
    pull = mesh * jnp.where(inside, down - 4.0 * stiffness, 0.0)
    for sweep_index in range(SWEEPS):
        around = mesh[:, :-2, 1:-1] + mesh[:, 2:, 1:-1] + mesh[:, 1:-1, :-2] + mesh[:, 1:-1, 2:]
        rest = rest[1:-1, 1:-1]
        pull = pull[:, 1:-1, 1:-1]
        mesh = (pull + stiffness * around) * rest
    return (flow_field, mesh)


def solution(mesh):
    in_specs = (
        P(("row", "col"), None),
        P(("row", "col")),
        P(("row", "col"), None),
        P(("row", "col"), None),
        P(("row", "col")),
        P(("row", "col"), None),
        P("row", "col"),
    )
    out_specs = (P(None, "row", "col"), P(None, "row", "col"))
    return jax.shard_map(
        per_device, mesh=mesh, in_specs=in_specs, out_specs=out_specs, check_vma=False
    )
```

```python
import math

import jax
import jax.numpy as jnp
import numpy as np
from jax import lax
from jax.experimental import pallas as pl
from jax.experimental.pallas import tpu as pltpu
from jax.sharding import PartitionSpec as P

PATCH = 160
STRIDE = 40
TY = 12
TX = 8
SWEEPS = 3
MARGIN = 60
HALF = PATCH // 2
FREQ = HALF + 1
WIN = 3
GROUPS = 6
BLOCKS = 11
ROWS = 16 * BLOCKS
TILE_H = 40
TILE_W = 80
SPLIT = 128 - TILE_W
LANES = 32
SLOT_H = 56
FRAME_H = 608
FORM_H = 488
EDGE_H = 64
TOP = 56
FIRST_H = FRAME_H

stiffness = 1.0
tiny = 1e-06


def trig():
    k = np.arange(FREQ)
    n = np.arange(PATCH)
    phase = (k[:, None] * n[None, :] % PATCH).astype(np.float64) * (2.0 * math.pi / PATCH)
    cosine, sine = np.cos(phase), np.sin(phase)
    sine[0] = 0.0
    sine[HALF] = 0.0
    return cosine, sine


def tables():
    cosine, sine = trig()
    first = np.zeros((256, 512))
    for w in range(WIN):
        rows = slice(STRIDE * w, STRIDE * w + PATCH)
        first[rows, FREQ * w : FREQ * (w + 1)] = cosine.T
        first[rows, 256 + FREQ * w : 256 + FREQ * (w + 1)] = sine.T
    cos_pad = np.zeros((8 * BLOCKS, PATCH))
    sin_pad = np.zeros((8 * BLOCKS, PATCH))
    cos_pad[:FREQ] = cosine
    sin_pad[:FREQ] = sine
    mixed = np.stack([cos_pad.reshape(BLOCKS, 8, PATCH), sin_pad.reshape(BLOCKS, 8, PATCH)], 1)
    mixed = mixed.reshape(ROWS, PATCH)
    second = np.zeros((2, ROWS, ROWS))
    second[0, :, :PATCH] = mixed
    second[1, :, 8 : 8 + PATCH] = mixed
    half = np.ones((FREQ, 1))
    half[0] = half[HALF] = 0.5
    even = (cosine * half)[:, :HALF].copy()
    even[:, 0] = (cosine * half)[:, HALF]
    odd = sine[:, :HALF].copy()
    rows_inv = np.zeros((PATCH, BLOCKS, 2, 8))
    even_pad = np.zeros((8 * BLOCKS, HALF))
    odd_pad = np.zeros((8 * BLOCKS, HALF))
    even_pad[:FREQ] = even
    odd_pad[:FREQ] = odd
    rows_inv[:HALF, :, 0] = even_pad.T.reshape(HALF, BLOCKS, 8)
    rows_inv[HALF:, :, 1] = odd_pad.T.reshape(HALF, BLOCKS, 8)
    rows_inv[HALF, :, 0] = even_pad.T.reshape(HALF, BLOCKS, 8)[0]
    rows_inv = rows_inv.reshape(PATCH, ROWS)
    cols_even = np.zeros((256, 256))
    cols_odd = np.zeros((256, 256))
    for w in range(WIN):
        cols_even[FREQ * w : FREQ * (w + 1), HALF * w : HALF * (w + 1)] = even
        cols_odd[FREQ * w : FREQ * (w + 1), HALF * w : HALF * (w + 1)] = odd
    select = np.zeros((1280, 128))
    for w in range(WIN):
        lanes = np.arange(FREQ) + FREQ * w
        select[lanes, w] = half[:, 0]
        select[256 + lanes, w] = 1.0
        select[512 + HALF * w + np.arange(HALF), 32 + w] = 1.0
        select[768 + lanes, 64 + w] = half[:, 0]
        select[1024 + lanes, 64 + w] = 1.0
    window = np.zeros((256, 128))
    for w in range(WIN):
        for kind in range(3):
            window[STRIDE * w : STRIDE * w + PATCH, 32 * kind + w] = 1.0
    as_bf16 = lambda x: jnp.asarray(x.astype(jnp.bfloat16))
    return tuple(as_bf16(x) for x in (first, second, rows_inv, cols_even, cols_odd, select, window))


def dot(a, b):
    return lax.dot_general(a, b, (((1,), (0,)), ((), ())), preferred_element_type=jnp.float32)


def dot_exact(a, b):
    return lax.dot_general(
        a,
        b,
        (((1,), (0,)), ((), ())),
        preferred_element_type=jnp.float32,
        precision=lax.Precision.HIGHEST,
    )


def spread_groups(sums):
    lane = lax.broadcasted_iota(jnp.int32, (16, 128), 1) % 32
    total = sums[0]
    for g in range(1, GROUPS):
        piece = sums[g] if g < GROUPS - 1 else jnp.where(lane == 0, sums[g], 0.0)
        total = total + pltpu.roll(piece, WIN * g, axis=1)
    return total


def window_means(grp, sec, cells, window):
    row = lax.broadcasted_iota(jnp.int32, (16, 16), 0)
    col = lax.broadcasted_iota(jnp.int32, (16, 16), 1)
    band = ((col >= row) & (col < row + 4)).astype(jnp.float32)
    for g in range(GROUPS):
        for c in range(7):
            values = grp[sec, g, 80 * c : 80 * c + 80, :].astype(jnp.float32)
            squares = (values * values).reshape(2, 5, 8, 256).sum(axis=1)
            cells[2 * c : 2 * c + 2, 256 * g : 256 * g + 256] = squares.sum(axis=1)
        values = grp[sec, g, 560:608, :].astype(jnp.float32)[:40]
        cells[14:15, 256 * g : 256 * g + 256] = (
            (values * values).reshape(5, 8, 256).sum(axis=0).sum(axis=0, keepdims=True)
        )
    cells[15:16, :] = jnp.zeros((1, 256 * GROUPS), jnp.float32)
    sums = dot_exact(band, cells[...])
    stacked = jnp.concatenate([sums[:, 256 * g : 256 * g + 256] for g in range(GROUPS)], axis=0)
    total = dot_exact(stacked, window).reshape(GROUPS, 16, 128)
    return spread_groups(total) / (PATCH * PATCH) + tiny


def pixel_places(sec, odd_group):
    row = lax.broadcasted_iota(jnp.int32, (512, 256), 0)
    col = lax.broadcasted_iota(jnp.int32, (512, 256), 1)
    tile, lane = row // 128, row % 128
    if sec == 0:
        pixel = jnp.where(lane < TILE_W, lane, -1000)
    else:
        tail = jnp.where(lane < LANES, lane + SPLIT, -1000)
        pixel = jnp.where(lane >= TILE_W, lane - TILE_W, tail)
    offset = 20 + 40 * odd_group
    return jnp.where((tile * TILE_W + pixel - offset == col) & (col < 240), 1.0, 0.0).astype(jnp.bfloat16)


def gather_frame(form, top, bottom, left, right, frame):
    for sec in range(2):
        for c in range(10):
            if 1 <= c <= 8:
                t = c - 1
                frame[sec, c, 0:TOP, :] = top[sec, t, 0:TOP, :]
                frame[sec, c, TOP : TOP + FORM_H, :] = form[sec, t]
                frame[sec, c, 544:600, :] = bottom[sec, t, 8:EDGE_H, :]
                frame[sec, c, 600:608, :] = jnp.zeros((8, 128), jnp.bfloat16)
                for dst, own, other in ((TOP, form[sec, t, 0:8, :], top[sec, t, TOP:EDGE_H, :]),
                                        (536, form[sec, t, 480:488, :], bottom[sec, t, 0:8, :])):
                    both = own.astype(jnp.float32) + other.astype(jnp.float32)
                    frame[sec, c, dst : dst + 8, :] = both.astype(jnp.bfloat16)
            else:
                frame[sec, c] = (left if c == 0 else right)[sec]


def correlate_kernel(
    form, top, bottom, left, right, first, second, rows_inv, cols_even, cols_odd, select, window,
    out, frame, grp, fa, fb, cells, raw, cross,
):
    gather_frame(form, top, bottom, left, right, frame)
    for sec, dst in ((0, fa), (1, fb)):
        for odd_group in range(2):
            places = pixel_places(sec, odd_group)
            for g in range(odd_group, GROUPS, 2):
                c = 3 * (g // 2) + odd_group
                count = min(4, 10 - c)
                wide = jnp.concatenate([frame[sec, c + k] for k in range(count)], axis=1)
                pixels = dot(wide, places[: 128 * count]).astype(jnp.bfloat16)
                grp[sec, g] = pixels
                dst[g] = dot(pixels, first[...]).astype(jnp.bfloat16)
    window_f32 = window[...].astype(jnp.float32)
    mean_a = window_means(grp, 0, cells, window_f32)
    mean_b = window_means(grp, 1, cells, window_f32)

    sub = lax.broadcasted_iota(jnp.int32, (8, 256), 0)
    lane = lax.broadcasted_iota(jnp.int32, (8, 256), 1)
    top_half = jnp.where(sub == 0, 0.5, 1.0)
    top_half2 = jnp.concatenate([top_half, top_half], axis=1)
    slot_zero = lane % HALF == 0
    shift_x = jnp.where(slot_zero, -8.0, 0.4 * (lane % HALF).astype(jnp.float32))[:1]
    sub_f = jnp.concatenate([sub, sub], axis=1).astype(jnp.float32)

    def weighted_rows(x):
        total = x[1, 0] + x[1, 1]
        for t in range(2, BLOCKS - 1):
            total = total + (x[t, 0] + x[t, 1])
        return total + x[0, 1] + (x[0, 0] * (top_half2 if x.shape[-1] == 512 else top_half) + 0.5 * x[BLOCKS - 1, 0])

    def spectra(g, q, parity):
        start = pl.multiple_of(80 * q + 32 * parity, 16)
        spec = []
        for src in (fa, fb):
            s = dot(second[parity], src[g, pl.ds(start, ROWS), :]).reshape(BLOCKS, 2, 8, 512)
            cc, cs = s[:, 0, :, :256], s[:, 0, :, 256:]
            sc, ss = s[:, 1, :, :256], s[:, 1, :, 256:]
            spec.append((cc - ss, sc + cs, cc + ss, sc - cs))
        (a1, a2, a3, a4), (b1, b2, b3, b4) = spec
        plus_r = a1 * b1 + a2 * b2
        plus_i = a1 * b2 - a2 * b1
        minus_r = a3 * b3 + a4 * b4
        minus_i = a3 * b4 - a4 * b3
        dcc = plus_r + minus_r
        dss = minus_r - plus_r
        dsc = plus_i + minus_i
        dcs = plus_i - minus_i
        d = jnp.stack(
            [jnp.concatenate([dcc, dcs], axis=2), jnp.concatenate([dsc, dss], axis=2)], axis=1
        )
        weight = weighted_rows(d * d)
        raw[g, pl.ds(2 * q + parity, 1), 768:1280] = jnp.sum(weight, axis=0, keepdims=True)
        cross[parity] = d.reshape(ROWS, 512).astype(jnp.bfloat16)

    def flows(g, q, parity):
        d16 = cross[parity]
        inv = dot(rows_inv[...], d16)
        prod = (inv[:HALF] * inv[HALF:]).reshape(10, 8, 512)
        run = prod[9]
        ramp = prod[9]
        for t in range(8, 0, -1):
            run = run + prod[t]
            ramp = ramp + run
        run = run + prod[0]
        flow_y = 3.2 * ramp + 0.4 * sub_f * run
        flow_y = jnp.where(sub_f == 0.0, flow_y - 8.0 * prod[0], flow_y)
        even = dot(d16[:, :256], cols_even[...]).reshape(BLOCKS, 2, 8, 256)
        odd = dot(d16[:, 256:], cols_odd[...]).reshape(BLOCKS, 2, 8, 256)
        flow_x = weighted_rows(even * jnp.where(slot_zero[None, None], even, odd))
        i = 2 * q + parity
        raw[g, pl.ds(i, 1), 0:512] = jnp.sum(flow_y, axis=0, keepdims=True)
        raw[g, pl.ds(i, 1), 512:768] = jnp.sum(flow_x, axis=0, keepdims=True) * shift_x

    raw[:, 12:16, :] = jnp.zeros((GROUPS, 4, 1280), jnp.float32)

    spectra(0, 0, 0)
    spectra(0, 0, 1)

    def step(n, carry):
        for parity in range(2):
            flows((n - 1) // 6, (n - 1) % 6, parity)
            spectra(n // 6, n % 6, parity)
        return carry

    lax.fori_loop(1, GROUPS * 6, step, 0)
    flows(GROUPS - 1, 5, 0)
    flows(GROUPS - 1, 5, 1)
    sums = dot_exact(raw[...].reshape(GROUPS * 16, 1280), select[...].astype(jnp.float32))
    total = spread_groups(sums.reshape(GROUPS, 16, 128))
    scale = (1.0 / (PATCH * PATCH)) / (mean_a * mean_b)
    unit = (2.0 / (PATCH * PATCH)) ** 2 * HALF / (PATCH * PATCH)
    total = total * (scale * unit)
    lane_all = lax.broadcasted_iota(jnp.int32, (16, 128), 1)
    weight = jnp.where(lane_all >= 64, total * HALF, 0.0)
    down = 1.0 + weight + pltpu.roll(weight, 96, axis=1) + pltpu.roll(weight, 64, axis=1)
    out[...] = jnp.where(lane_all >= 64, weight, total) / down


def correlate(form, top, bottom, left, right):
    return pl.pallas_call(
        correlate_kernel,
        out_shape=jax.ShapeDtypeStruct((16, 128), jnp.float32),
        scratch_shapes=[
            pltpu.VMEM((2, 10, FRAME_H, 128), jnp.bfloat16),
            pltpu.VMEM((2, GROUPS, FRAME_H, 256), jnp.bfloat16),
            pltpu.VMEM((GROUPS, FIRST_H, 512), jnp.bfloat16),
            pltpu.VMEM((GROUPS, FIRST_H, 512), jnp.bfloat16),
            pltpu.VMEM((16, 256 * GROUPS), jnp.float32),
            pltpu.VMEM((GROUPS, 16, 1280), jnp.float32),
            pltpu.VMEM((2, ROWS, 512), jnp.bfloat16),
        ],
    )(form, top, bottom, left, right, *tables())


def pack_kernel(a_tiles, b_tiles, a_owner, b_owner, a_offset, b_offset, out, rows):
    count = a_tiles.shape[0]
    owners = jnp.concatenate([a_owner[...], b_owner[...]], axis=1)
    slot = lax.broadcasted_iota(jnp.int32, (128, 2 * count), 0)
    select = jnp.where(slot == owners, 1.0, 0.0).astype(jnp.bfloat16)
    zero = lambda width: jnp.zeros((count, width), jnp.bfloat16)

    def position(offset):
        row = offset[:, 0:1].astype(jnp.float32)
        col = offset[:, 1:2].astype(jnp.float32)
        code = row * (TX / TILE_H) + col * (1.0 / TILE_W) + 1.0
        return jnp.floor(code + 0.5)

    def piece(tiles, start, width):
        return tiles[:, start : start + width]

    lane = lax.broadcasted_iota(jnp.int32, (count, 128), 1)
    code_a = jnp.where(lane == 64, position(a_offset), 0.0).astype(jnp.bfloat16)
    code_b = jnp.where(lane == 96, position(b_offset), 0.0).astype(jnp.bfloat16)

    def send_row(y):
        if y < TILE_H:
            a_part = jnp.concatenate([piece(a_tiles, TILE_W * y, TILE_W), zero(SPLIT)], axis=1)
            b_part = jnp.concatenate([zero(TILE_W), piece(b_tiles, TILE_W * y, SPLIT)], axis=1)
        elif y < TILE_H + 8:
            u = y - TILE_H
            a_part = zero(128)
            b_part = jnp.concatenate(
                [piece(b_tiles, TILE_W * (8 * k + u) + SPLIT, LANES) for k in range(4)], axis=1
            )
        else:
            u = y - TILE_H - 8
            a_part = code_a
            b_part = jnp.concatenate(
                [piece(b_tiles, TILE_W * (32 + u) + SPLIT, LANES), zero(96)], axis=1
            )
            b_part = b_part + code_b
        return jnp.concatenate([a_part, b_part], axis=0)

    for y in range(0, SLOT_H, 2):
        both = jnp.concatenate([send_row(y), send_row(y + 1)], axis=1)
        sent = dot(select, both)
        rows[pl.ds(y, 128, stride=SLOT_H), :] = sent[:, :128]
        rows[pl.ds(y + 1, 128, stride=SLOT_H), :] = sent[:, 128:]

    def flush(n, carry):
        start = pl.multiple_of(8 * SLOT_H * n, 8)
        block = rows[pl.ds(start, 8 * SLOT_H), :].reshape(8, SLOT_H, 128)
        out[pl.ds(8 * n, 8)] = block.astype(jnp.bfloat16)
        return carry

    lax.fori_loop(0, 16, flush, 0)


def place_kernel(got, form, up, down, rows, plane_a, plane_b):
    def widen(n, carry):
        start = pl.multiple_of(8 * SLOT_H * n, 8)
        block = got[pl.ds(8 * n, 8)].astype(jnp.float32)
        rows[pl.ds(start, 8 * SLOT_H), :] = block.reshape(8 * SLOT_H, 128)
        return carry

    lax.fori_loop(0, 16, widen, 0)
    codes = rows[pl.ds(TILE_H + 8, 128, stride=SLOT_H), :]
    wanted = lax.broadcasted_iota(jnp.int32, (128, 128), 1).astype(jnp.float32) + 1.0
    pick = lambda col: jnp.where(codes[:, col : col + 1] == wanted, 1.0, 0.0).T[:96]
    select_a = pick(64)
    select_b = pick(96)
    select = jnp.concatenate([select_a, select_b], axis=0).astype(jnp.bfloat16)
    select_b = select_b.astype(jnp.bfloat16)

    def slot_row(y):
        return rows[pl.ds(y, 128, stride=SLOT_H), :].astype(jnp.bfloat16)

    for plane in (plane_a, plane_b):
        for t in range(TX):
            plane[FORM_H * t : FORM_H * t + 8, :] = jnp.zeros((8, 128), jnp.float32)
            plane[FORM_H * t + 480 : FORM_H * t + 488, :] = jnp.zeros((8, 128), jnp.float32)
    lane = lax.broadcasted_iota(jnp.int32, (96, 128), 1)
    tail = lane < LANES

    for u in range(0, 8, 2):
        tails = jnp.concatenate([slot_row(TILE_H + u + v + w) for v in range(2) for w in (0, 8)], axis=1)
        tails = dot(select_b, tails)
        mains = {}
        for k in range(5):
            y = 8 * k + u
            main = dot(select, jnp.concatenate([slot_row(y), slot_row(y + 1)], axis=1))
            for v in range(2):
                part_a = main[:96, 128 * v : 128 * v + 128]
                part_b = main[96:, 128 * v : 128 * v + 128]
                rest = tails[:, 256 * v : 256 * v + 128] if k < 4 else tails[:, 256 * v + 128 : 256 * v + 256]
                if 0 < k < 4:
                    rest = pltpu.roll(rest, 128 - LANES * k, axis=1)
                part_b = jnp.where(tail, rest, part_b)
                for ty in range(TY):
                    where = pl.ds(TILE_H * ty + y + v + 4, TX, stride=FORM_H)
                    plane_a[where, :] = part_a[TX * ty : TX * ty + TX]
                    plane_b[where, :] = part_b[TX * ty : TX * ty + TX]

    for sec, plane in ((0, plane_a), (1, plane_b)):
        for t in range(TX):
            block = plane[FORM_H * t : FORM_H * t + FORM_H, :].astype(jnp.bfloat16)
            form[sec, t] = block
            up[sec, t] = plane[FORM_H * t : FORM_H * t + EDGE_H, :].astype(jnp.bfloat16)
            down[sec, t] = plane[FORM_H * t + 424 : FORM_H * t + 488, :].astype(jnp.bfloat16)


def pack(a_tiles, b_tiles, a_owner, b_owner, a_offset, b_offset):
    return pl.pallas_call(
        pack_kernel,
        out_shape=jax.ShapeDtypeStruct((128, SLOT_H, 128), jnp.bfloat16),
        scratch_shapes=[pltpu.VMEM((128 * SLOT_H, 128), jnp.float32)],
    )(a_tiles, b_tiles, a_owner[None], b_owner[None], a_offset, b_offset)


def place(got):
    edge = jax.ShapeDtypeStruct((2, TX, EDGE_H, 128), jnp.bfloat16)
    return pl.pallas_call(
        place_kernel,
        out_shape=(jax.ShapeDtypeStruct((2, TX, FORM_H, 128), jnp.bfloat16), edge, edge),
        scratch_shapes=[
            pltpu.VMEM((128 * SLOT_H, 128), jnp.float32),
            pltpu.VMEM((TX * FORM_H, 128), jnp.float32),
            pltpu.VMEM((TX * FORM_H, 128), jnp.float32),
        ],
    )(got)


def extended_2(block, sides, width):
    for axis, dim in sides:
        count = lax.axis_size(axis)
        forward = [(i, i + 1) for i in range(count - 1)]
        backward = [(target, source) for source, target in forward]
        low = lax.ppermute(
            lax.slice_in_dim(block, block.shape[dim] - width, None, axis=dim), axis, forward
        )
        high = lax.ppermute(lax.slice_in_dim(block, 0, width, axis=dim), axis, backward)
        block = jnp.concatenate([low, block, high], axis=dim)
    return block


def shifted(block, axis, step):
    count = lax.axis_size(axis)
    pairs = [(i, i + step) for i in range(count) if 0 <= i + step < count]
    return lax.ppermute(block, axis, pairs)


def column(form, top, bottom, t):
    grow = lambda x, low, high: jnp.pad(x[:, t], ((0, 0), (low, high), (0, 0)))
    return (
        grow(form, TOP, FRAME_H - TOP - FORM_H)
        + grow(top, 0, FRAME_H - EDGE_H)
        + grow(bottom, 536, FRAME_H - 536 - EDGE_H)
    )


def per_device(a_tiles, a_owner, a_offset, b_tiles, b_owner, b_offset, patch_valid):
    grid_rows, grid_cols = patch_valid.shape
    packed = pack(a_tiles, b_tiles, a_owner, b_owner, a_offset, b_offset)
    got = lax.all_to_all(packed, ("row", "col"), split_axis=0, concat_axis=0, tiled=True)
    form, up, down = place(got)
    top = shifted(down, "row", 1)
    bottom = shifted(up, "row", -1)
    left = shifted(column(form, top, bottom, TX - 1), "col", 1)
    right = shifted(column(form, top, bottom, 0), "col", -1)
    result = correlate(form, top, bottom, left, right)
    flow_field = jnp.stack([result[:grid_rows, :grid_cols], result[:grid_rows, 32 : 32 + grid_cols]])
    confidence = result[:grid_rows, 64 : 64 + grid_cols]
    valid_float = patch_valid.astype(jnp.float32)
    strength = valid_float * confidence
    start = valid_float[None] * flow_field
    fields = jnp.concatenate([start, (strength + 4.0 * stiffness)[None]])
    fields = extended_2(fields, (("row", 1), ("col", 2)), SWEEPS)
    mesh = fields[:2]
    below = fields[2]
    inside = below > 0.0
    rest = jnp.where(inside, 1.0 / jnp.where(inside, below, 1.0), 0.0)
    pull = mesh * jnp.where(inside, below - 4.0 * stiffness, 0.0)
    for sweep_index in range(SWEEPS):
        around = mesh[:, :-2, 1:-1] + mesh[:, 2:, 1:-1] + mesh[:, 1:-1, :-2] + mesh[:, 1:-1, 2:]
        rest = rest[1:-1, 1:-1]
        pull = pull[:, 1:-1, 1:-1]
        mesh = (pull + stiffness * around) * rest
    return (flow_field, mesh)


def solution(mesh):
    in_specs = (
        P(("row", "col"), None),
        P(("row", "col")),
        P(("row", "col"), None),
        P(("row", "col"), None),
        P(("row", "col")),
        P(("row", "col"), None),
        P("row", "col"),
    )
    out_specs = (P(None, "row", "col"), P(None, "row", "col"))
    return jax.shard_map(
        per_device, mesh=mesh, in_specs=in_specs, out_specs=out_specs, check_vma=False
    )
```

```python
import math

import jax
import jax.numpy as jnp
import numpy as np
from jax import lax
from jax.experimental import pallas as pl
from jax.experimental.pallas import tpu as pltpu
from jax.sharding import PartitionSpec as P

PATCH = 160
STRIDE = 40
TY = 12
TX = 8
SWEEPS = 3
MARGIN = 60
HALF = PATCH // 2
FREQ = HALF + 1
WIN = 3
GROUPS = 6
ROWS = PATCH
TILE_H = 40
TILE_W = 80
SPLIT = 128 - TILE_W
LANES = 32
SLOT_H = 56
FRAME_H = 608
FORM_H = 488
EDGE_H = 64
TOP = 56
TMAJOR = True
FIRST_H = FRAME_H

stiffness = 1.0
tiny = 1e-06


def trig():
    k = np.arange(FREQ)
    n = np.arange(PATCH)
    phase = (k[:, None] * n[None, :] % PATCH).astype(np.float64) * (2.0 * math.pi / PATCH)
    cosine, sine = np.cos(phase), np.sin(phase)
    sine[0] = 0.0
    sine[HALF] = 0.0
    return cosine, sine


def tables():
    cosine, sine = trig()
    first = np.zeros((256, 512))
    for w in range(WIN):
        rows = slice(STRIDE * w, STRIDE * w + PATCH)
        first[rows, FREQ * w : FREQ * (w + 1)] = cosine.T
        first[rows, 256 + FREQ * w : 256 + FREQ * (w + 1)] = sine.T
    mixed = np.concatenate([cosine[HALF:], sine[1:HALF], cosine[:HALF]])
    second = np.zeros((2, ROWS, 176))
    for parity in range(2):
        second[parity, :, 8 * parity : 8 * parity + PATCH] = mixed
    half = np.ones((FREQ, 1))
    half[0] = half[HALF] = 0.5
    shift = np.where(np.arange(PATCH) < HALF, np.arange(PATCH), np.arange(PATCH) - PATCH) * (16.0 / PATCH)
    shift[HALF] = 0.0
    rounded = lambda x: x.astype(jnp.bfloat16).astype(np.float64)
    mix = 2.0 * half * ((rounded(cosine) * shift) @ rounded(sine).T)
    sign = half[:, 0] * cosine[:, HALF]
    mix_rows = np.zeros((HALF + 8, ROWS))
    mix_rows[:FREQ, 1:HALF] = mix[:, 1:HALF]
    mix_rows[FREQ, HALF:] = sign[:HALF]
    mix_rows[FREQ, 0] = sign[HALF]
    mix_cols = np.zeros((256, 256))
    sign_cols = np.zeros((16, 256))
    for w in range(WIN):
        mix_cols[FREQ * w : FREQ * (w + 1), FREQ * w : FREQ * (w + 1)] = mix.T
        sign_cols[w, FREQ * w : FREQ * (w + 1)] = sign
    select = np.zeros((1280, 128))
    for w in range(WIN):
        lanes = np.arange(FREQ) + FREQ * w
        select[lanes, w] = half[:, 0]
        select[256 + lanes, w] = 1.0
        select[512 + lanes, 32 + w] = 1.0
        select[768 + lanes, 64 + w] = half[:, 0]
        select[1024 + lanes, 64 + w] = 1.0
    window = np.zeros((256, 128))
    for w in range(WIN):
        for kind in range(3):
            window[STRIDE * w : STRIDE * w + PATCH, 32 * kind + w] = 1.0
    as_bf16 = lambda x: jnp.asarray(x.astype(jnp.bfloat16))
    return tuple(as_bf16(x) for x in (first, second, mix_rows, mix_cols, sign_cols, select, window))


def dot(a, b):
    return lax.dot_general(a, b, (((1,), (0,)), ((), ())), preferred_element_type=jnp.float32)


def dot_exact(a, b):
    return lax.dot_general(
        a,
        b,
        (((1,), (0,)), ((), ())),
        preferred_element_type=jnp.float32,
        precision=lax.Precision.HIGHEST,
    )


def spread_groups(sums):
    lane = lax.broadcasted_iota(jnp.int32, (16, 128), 1) % 32
    total = sums[0]
    for g in range(1, GROUPS):
        piece = sums[g] if g < GROUPS - 1 else jnp.where(lane == 0, sums[g], 0.0)
        total = total + pltpu.roll(piece, WIN * g, axis=1)
    return total


def window_means(grp, sec, cells, window):
    for g in range(GROUPS):
        for c in range(7):
            values = grp[sec, g, 80 * c : 80 * c + 80, :].astype(jnp.float32)
            squares = (values * values).reshape(2, 5, 8, 256).sum(axis=1)
            cells[2 * c : 2 * c + 2, 256 * g : 256 * g + 256] = squares.sum(axis=1)
        values = grp[sec, g, 560:608, :].astype(jnp.float32)[:40]
        cells[14:15, 256 * g : 256 * g + 256] = (
            (values * values).reshape(5, 8, 256).sum(axis=0).sum(axis=0, keepdims=True)
        )
    cells[15:24, :] = jnp.zeros((9, 256 * GROUPS), jnp.float32)
    sums = cells[0:16, :] + cells[1:17, :] + cells[2:18, :] + cells[3:19, :]
    stacked = jnp.concatenate([sums[:, 256 * g : 256 * g + 256] for g in range(GROUPS)], axis=0)
    total = dot_exact(stacked, window).reshape(GROUPS, 16, 128)
    return spread_groups(total) / (PATCH * PATCH) + tiny


def pixel_places(sec, odd_group):
    row = lax.broadcasted_iota(jnp.int32, (512, 256), 0)
    col = lax.broadcasted_iota(jnp.int32, (512, 256), 1)
    tile, lane = row // 128, row % 128
    if sec == 0:
        pixel = jnp.where(lane < TILE_W, lane, -1000)
    else:
        tail = jnp.where(lane < LANES, lane + SPLIT, -1000)
        pixel = jnp.where(lane >= TILE_W, lane - TILE_W, tail)
    offset = 20 + 40 * odd_group
    return jnp.where((tile * TILE_W + pixel - offset == col) & (col < 240), 1.0, 0.0).astype(jnp.bfloat16)


def gather_frame(form, top, bottom, left, right, frame):
    for sec in range(2):
        for c in range(10):
            if 1 <= c <= 8:
                t = c - 1
                frame[sec, c, 0:TOP, :] = top[t, sec, 0:TOP, :]
                frame[sec, c, TOP : TOP + FORM_H, :] = form[t, sec]
                frame[sec, c, 544:600, :] = bottom[t, sec, 8:EDGE_H, :]
                frame[sec, c, 600:608, :] = jnp.zeros((8, 128), jnp.bfloat16)
                for dst, own, other in ((TOP, form[t, sec, 0:8, :], top[t, sec, TOP:EDGE_H, :]),
                                        (536, form[t, sec, 480:488, :], bottom[t, sec, 0:8, :])):
                    both = own.astype(jnp.float32) + other.astype(jnp.float32)
                    frame[sec, c, dst : dst + 8, :] = both.astype(jnp.bfloat16)
            else:
                frame[sec, c] = (left if c == 0 else right)[sec]


def correlate_kernel(
    form, top, bottom, left, right, first, second, mix_rows, mix_cols, sign_cols,
    select, window, out, frame, grp, fa, fb, cells, raw, raw_end, spec, cross, flow_rows, flow_cols,
):
    gather_frame(form, top, bottom, left, right, frame)
    for sec, dst in ((0, fa), (1, fb)):
        for odd_group in range(2):
            places = pixel_places(sec, odd_group)
            for g in range(odd_group, GROUPS, 2):
                c = 3 * (g // 2) + odd_group
                count = min(4, 10 - c)
                wide = jnp.concatenate([frame[sec, c + k] for k in range(count)], axis=1)
                pixels = dot(wide, places[: 128 * count]).astype(jnp.bfloat16)
                grp[sec, g] = pixels
                dst[g] = dot(pixels, first[...]).astype(jnp.bfloat16)
    window_f32 = window[...].astype(jnp.float32)
    mean_a = window_means(grp, 0, cells, window_f32)
    mean_b = window_means(grp, 1, cells, window_f32)

    sub = lax.broadcasted_iota(jnp.int32, (8, 256), 0)
    top = sub == 0
    top_half = jnp.where(top, 0.5, 1.0)
    lane128 = lax.broadcasted_iota(jnp.int32, (8, 128), 1)
    k_lane = lax.broadcasted_iota(jnp.int32, (8, ROWS), 1)
    end_weight = jnp.where((k_lane == 0) | (k_lane == HALF), -4.0, -8.0)

    def row_of(m):
        valid = (m >= 0) & (m < GROUPS * 12)
        near = jnp.clip(m, 0, GROUPS * 12 - 1)
        return near // 12, jnp.where(valid, near % 12, 15), (near % 12) // 2

    def spectra(m, parity):
        g, _, q = row_of(m)
        start = pl.multiple_of(80 * q + 32 * parity, 16)
        spec[parity, 0] = dot(second[parity], fa[g, pl.ds(start, 176), :])
        spec[parity, 1] = dot(second[parity], fb[g, pl.ds(start, 176), :])

    def products(m, parity):
        g, i, _ = row_of(m)
        total = None
        for half in range(2):
            sides = []
            for sec in range(2):
                sides.append([])
                for base in (HALF, 0):
                    for lo in (0, 256):
                        sides[sec].append(
                            spec[parity, sec, base : base + HALF, lo : lo + 256].reshape(10, 8, 256)[5 * half : 5 * half + 5]
                        )
            terms = [(cc - ss, sc + cs, cc + ss, sc - cs) for cc, cs, sc, ss in sides]
            (a1, a2, a3, a4), (b1, b2, b3, b4) = terms
            plus_r = a1 * b1 + a2 * b2
            plus_i = a1 * b2 - a2 * b1
            minus_r = a3 * b3 + a4 * b4
            minus_i = a3 * b4 - a4 * b3
            dcc = plus_r + minus_r
            dss = minus_r - plus_r
            dsc = plus_i + minus_i
            dcs = plus_i - minus_i
            if half == 0:
                (ac, asn, ae, aes), (bc, bsn, be, bes) = [[x[0] for x in side] for side in sides]
                fix = lambda new, old: jnp.concatenate([jnp.where(top, new, old[0])[None], old[1:]], axis=0)
                dcc = fix(2.0 * (ac * bc + asn * bsn), dcc)
                dcs = fix(2.0 * (ac * bsn - asn * bc), dcs)
                dsc = fix(2.0 * (ae * be + aes * bes), dsc)
                dss = fix(2.0 * (ae * bes - aes * be), dss)
            rows = slice(40 * half, 40 * half + 40)
            cos_rows = slice(HALF + 40 * half, HALF + 40 * half + 40)
            cross[parity, rows, 0:256] = dsc.reshape(40, 256).astype(jnp.bfloat16)
            cross[parity, rows, 256:512] = dss.reshape(40, 256).astype(jnp.bfloat16)
            cross[parity, cos_rows, 0:256] = dcc.reshape(40, 256).astype(jnp.bfloat16)
            cross[parity, cos_rows, 256:512] = dcs.reshape(40, 256).astype(jnp.bfloat16)
            low = dcc * dcc + dsc * dsc
            high = dcs * dcs + dss * dss
            if half == 0:
                total = [low[0] * top_half + low[1:].sum(axis=0), high[0] * top_half + high[1:].sum(axis=0)]
            else:
                total = [total[0] + low.sum(axis=0), total[1] + high.sum(axis=0)]
        total = jnp.concatenate(total, axis=1)
        raw[g, pl.ds(i, 1), 768:1280] = jnp.sum(total, axis=0, keepdims=True)

    def flows(m, parity):
        g, i, _ = row_of(m)
        flow_rows[parity] = dot(mix_rows[...], cross[parity])
        flow_cols[parity] = dot(cross[parity, :, 256:512], mix_cols[...])
        end = lax.dot_general(
            sign_cols[...], cross[parity, :, 0:256], (((1,), (1,)), ((), ())), preferred_element_type=jnp.float32
        )[:8]
        end = jnp.sum(end * end * end_weight, axis=1, keepdims=True)
        raw_end[g] = jnp.where(lane128 == i, end, raw_end[g])

    def flow_sums(m, parity):
        g, i, _ = row_of(m)
        cosines = cross[parity, HALF:, :].astype(jnp.float32).reshape(10, 8, 512)
        mixed = flow_rows[parity].reshape(11, 8, 512)
        flow_y = cosines[0] * mixed[0]
        for t in range(1, 10):
            flow_y = flow_y + cosines[t] * mixed[t]
        end = cross[parity, 0:16, :].astype(jnp.float32)[:1] * mixed[10, 0:1] - 8.0 * mixed[10, 1:2] * mixed[10, 1:2]
        raw[g, pl.ds(i, 1), 0:512] = jnp.sum(flow_y, axis=0, keepdims=True) + end
        cosines = cross[parity, :, 0:256].astype(jnp.float32).reshape(20, 8, 256)
        mixed = flow_cols[parity].reshape(20, 8, 256)
        flow_x = (cosines[0] * mixed[0] + cosines[10] * mixed[10]) * top_half
        for t in range(1, 20):
            if t != 10:
                flow_x = flow_x + cosines[t] * mixed[t]
        raw[g, pl.ds(i, 1), 512:768] = jnp.sum(flow_x, axis=0, keepdims=True)

    raw_end[...] = jnp.zeros((GROUPS, 8, 128), jnp.float32)
    raw[:, 12:16, :] = jnp.zeros((GROUPS, 4, 1280), jnp.float32)

    def step(n, carry):
        for parity in range(2):
            m = 2 * n + parity
            flow_sums(m - 3, 1 - parity)
            flows(m - 2, parity)
            products(m - 1, 1 - parity)
            spectra(m, parity)
        return carry

    lax.fori_loop(0, GROUPS * 6 + 2, step, 0)
    sums = dot_exact(raw[...].reshape(GROUPS * 16, 1280), select[...].astype(jnp.float32))
    sums = sums.reshape(GROUPS, 16, 128)
    ends = [
        pltpu.roll(jnp.concatenate([raw_end[g], jnp.zeros((120, 128), jnp.float32)], axis=0).T[:16], 32, axis=1)
        for g in range(GROUPS)
    ]
    total = spread_groups([sums[g] + ends[g] for g in range(GROUPS)])
    scale = (1.0 / (PATCH * PATCH)) / (mean_a * mean_b)
    unit = (2.0 / (PATCH * PATCH)) ** 2 * HALF / (PATCH * PATCH)
    total = total * (scale * unit)
    lane_all = lax.broadcasted_iota(jnp.int32, (16, 128), 1)
    weight = jnp.where(lane_all >= 64, total * HALF, 0.0)
    down = 1.0 + weight + pltpu.roll(weight, 96, axis=1) + pltpu.roll(weight, 64, axis=1)
    out[...] = jnp.where(lane_all >= 64, weight, total) / down


def correlate(form, top, bottom, left, right):
    return pl.pallas_call(
        correlate_kernel,
        out_shape=jax.ShapeDtypeStruct((16, 128), jnp.float32),
        scratch_shapes=[
            pltpu.VMEM((2, 10, FRAME_H, 128), jnp.bfloat16),
            pltpu.VMEM((2, GROUPS, FRAME_H, 256), jnp.bfloat16),
            pltpu.VMEM((GROUPS, FIRST_H, 512), jnp.bfloat16),
            pltpu.VMEM((GROUPS, FIRST_H, 512), jnp.bfloat16),
            pltpu.VMEM((24, 256 * GROUPS), jnp.float32),
            pltpu.VMEM((GROUPS, 16, 1280), jnp.float32),
            pltpu.VMEM((GROUPS, 8, 128), jnp.float32),
            pltpu.VMEM((2, 2, ROWS, 512), jnp.float32),
            pltpu.VMEM((2, ROWS, 512), jnp.bfloat16),
            pltpu.VMEM((2, HALF + 8, 512), jnp.float32),
            pltpu.VMEM((2, ROWS, 256), jnp.float32),
        ],
        compiler_params=pltpu.CompilerParams(vmem_limit_bytes=40 << 20),
    )(form, top, bottom, left, right, *tables())


def pack_kernel(a_tiles, b_tiles, a_owner, b_owner, a_offset, b_offset, out, rows):
    count = a_tiles.shape[0]
    owners = jnp.concatenate([a_owner[...], b_owner[...]], axis=1)
    slot = lax.broadcasted_iota(jnp.int32, (128, 2 * count), 0)
    select = jnp.where(slot == owners, 1.0, 0.0).astype(jnp.bfloat16)
    zero = lambda width: jnp.zeros((count, width), jnp.bfloat16)

    def position(offset):
        row = offset[0:1, :].astype(jnp.float32)
        col = offset[1:2, :].astype(jnp.float32)
        code = jnp.floor(row * (TX / TILE_H) + col * (1.0 / TILE_W) + 1.5)
        code = jnp.concatenate([code, jnp.zeros((1, 128 - count), jnp.float32)], axis=1)
        return jnp.broadcast_to(code, (128, 128)).T[:count]

    def piece(tiles, start, width):
        return tiles[:, start : start + width]

    lane = lax.broadcasted_iota(jnp.int32, (count, 128), 1)
    code_a = jnp.where(lane == 64, position(a_offset), 0.0).astype(jnp.bfloat16)
    code_b = jnp.where(lane == 96, position(b_offset), 0.0).astype(jnp.bfloat16)

    def send_row(y):
        if y < TILE_H:
            a_part = jnp.concatenate([piece(a_tiles, TILE_W * y, TILE_W), zero(SPLIT)], axis=1)
            b_part = jnp.concatenate([zero(TILE_W), piece(b_tiles, TILE_W * y, SPLIT)], axis=1)
        elif y < TILE_H + 8:
            u = y - TILE_H
            a_part = zero(128)
            b_part = jnp.concatenate(
                [piece(b_tiles, TILE_W * (8 * k + u) + SPLIT, LANES) for k in range(4)], axis=1
            )
        else:
            u = y - TILE_H - 8
            a_part = code_a
            b_part = jnp.concatenate(
                [piece(b_tiles, TILE_W * (32 + u) + SPLIT, LANES), zero(96)], axis=1
            )
            b_part = b_part + code_b
        return jnp.concatenate([a_part, b_part], axis=0)

    for y in range(0, SLOT_H, 2):
        both = jnp.concatenate([send_row(y), send_row(y + 1)], axis=1)
        sent = dot(select, both)
        rows[pl.ds(y, 128, stride=SLOT_H), :] = sent[:, :128]
        rows[pl.ds(y + 1, 128, stride=SLOT_H), :] = sent[:, 128:]

    def flush(n, carry):
        start = pl.multiple_of(8 * SLOT_H * n, 8)
        block = rows[pl.ds(start, 8 * SLOT_H), :].reshape(8, SLOT_H, 128)
        out[pl.ds(8 * n, 8)] = block.astype(jnp.bfloat16)
        return carry

    lax.fori_loop(0, 16, flush, 0)


def place_kernel(got, form, up, down, low, high, rows, plane_a, plane_b):
    def widen(n, carry):
        start = pl.multiple_of(8 * SLOT_H * n, 8)
        block = got[pl.ds(8 * n, 8)].astype(jnp.float32)
        rows[pl.ds(start, 8 * SLOT_H), :] = block.reshape(8 * SLOT_H, 128)
        return carry

    lax.fori_loop(0, 16, widen, 0)
    codes = rows[pl.ds(TILE_H + 8, 128, stride=SLOT_H), :]
    wanted = lax.broadcasted_iota(jnp.int32, (128, 128), 1).astype(jnp.float32) + 1.0
    pick = lambda col: jnp.where(codes[:, col : col + 1] == wanted, 1.0, 0.0).T[:96]
    select_a = pick(64)
    select_b = pick(96)
    select = jnp.concatenate([select_a, select_b], axis=0).astype(jnp.bfloat16)
    select_b = select_b.astype(jnp.bfloat16)

    def slot_row(y):
        return rows[pl.ds(y, 128, stride=SLOT_H), :].astype(jnp.bfloat16)

    for plane in (plane_a, plane_b):
        for t in range(TX):
            plane[FORM_H * t : FORM_H * t + 8, :] = jnp.zeros((8, 128), jnp.float32)
            plane[FORM_H * t + 480 : FORM_H * t + 488, :] = jnp.zeros((8, 128), jnp.float32)
    lane = lax.broadcasted_iota(jnp.int32, (96, 128), 1)
    tail = lane < LANES

    for u in range(0, 8, 2):
        tails = jnp.concatenate([slot_row(TILE_H + u + v + w) for v in range(2) for w in (0, 8)], axis=1)
        tails = dot(select_b, tails)
        mains = {}
        for k in range(5):
            y = 8 * k + u
            main = dot(select, jnp.concatenate([slot_row(y), slot_row(y + 1)], axis=1))
            for v in range(2):
                part_a = main[:96, 128 * v : 128 * v + 128]
                part_b = main[96:, 128 * v : 128 * v + 128]
                rest = tails[:, 256 * v : 256 * v + 128] if k < 4 else tails[:, 256 * v + 128 : 256 * v + 256]
                if 0 < k < 4:
                    rest = pltpu.roll(rest, 128 - LANES * k, axis=1)
                part_b = jnp.where(tail, rest, part_b)
                for ty in range(TY):
                    where = pl.ds(TILE_H * ty + y + v + 4, TX, stride=FORM_H)
                    plane_a[where, :] = part_a[TX * ty : TX * ty + TX]
                    plane_b[where, :] = part_b[TX * ty : TX * ty + TX]

    for sec, plane in ((0, plane_a), (1, plane_b)):
        for t in range(TX):
            block = plane[FORM_H * t : FORM_H * t + FORM_H, :].astype(jnp.bfloat16)
            form[t, sec] = block
            for side, at in ((low, 0), (high, TX - 1)):
                if t == at:
                    side[sec, 0:TOP, :] = jnp.zeros((TOP, 128), jnp.bfloat16)
                    side[sec, TOP : TOP + FORM_H, :] = block
                    side[sec, TOP + FORM_H :, :] = jnp.zeros((FRAME_H - TOP - FORM_H, 128), jnp.bfloat16)
            up[t, sec] = plane[FORM_H * t : FORM_H * t + EDGE_H, :].astype(jnp.bfloat16)
            down[t, sec] = plane[FORM_H * t + 424 : FORM_H * t + 488, :].astype(jnp.bfloat16)


VMEM_SPEC = pl.BlockSpec(memory_space=pltpu.VMEM)


def pack(a_tiles, b_tiles, a_owner, b_owner, a_offset, b_offset):
    return pl.pallas_call(
        pack_kernel,
        out_shape=jax.ShapeDtypeStruct((128, SLOT_H, 128), jnp.bfloat16),
        scratch_shapes=[pltpu.VMEM((128 * SLOT_H, 128), jnp.float32)],
        compiler_params=pltpu.CompilerParams(vmem_limit_bytes=16 << 20),
    )(a_tiles, b_tiles, a_owner[None], b_owner[None], a_offset.T, b_offset.T)


def place(got):
    edge = jax.ShapeDtypeStruct((TX, 2, EDGE_H, 128), jnp.bfloat16)
    side = jax.ShapeDtypeStruct((2, FRAME_H, 128), jnp.bfloat16)
    return pl.pallas_call(
        place_kernel,
        out_shape=(jax.ShapeDtypeStruct((TX, 2, FORM_H, 128), jnp.bfloat16), edge, edge, side, side),
        scratch_shapes=[
            pltpu.VMEM((128 * SLOT_H, 128), jnp.float32),
            pltpu.VMEM((TX * FORM_H, 128), jnp.float32),
            pltpu.VMEM((TX * FORM_H, 128), jnp.float32),
        ],
        in_specs=[VMEM_SPEC],
        out_specs=(VMEM_SPEC,) * 5,
        compiler_params=pltpu.CompilerParams(vmem_limit_bytes=24 << 20),
    )(got)


def extended_2(block, sides, width):
    for axis, dim in sides:
        count = lax.axis_size(axis)
        forward = [(i, i + 1) for i in range(count - 1)]
        backward = [(target, source) for source, target in forward]
        low = lax.ppermute(
            lax.slice_in_dim(block, block.shape[dim] - width, None, axis=dim), axis, forward
        )
        high = lax.ppermute(lax.slice_in_dim(block, 0, width, axis=dim), axis, backward)
        block = jnp.concatenate([low, block, high], axis=dim)
    return block


def shifted(block, axis, step):
    count = lax.axis_size(axis)
    pairs = [(i, i + step) for i in range(count) if 0 <= i + step < count]
    return lax.ppermute(block, axis, pairs)


def column(side, top, bottom, t):
    grow = lambda x, low, high: jnp.pad(x[t], ((0, 0), (low, high), (0, 0)))
    return side + grow(top, 0, FRAME_H - EDGE_H) + grow(bottom, 536, FRAME_H - 536 - EDGE_H)


def per_device(a_tiles, a_owner, a_offset, b_tiles, b_owner, b_offset, patch_valid):
    grid_rows, grid_cols = patch_valid.shape
    packed = pack(a_tiles, b_tiles, a_owner, b_owner, a_offset, b_offset)
    got = lax.all_to_all(packed, ("row", "col"), split_axis=0, concat_axis=0, tiled=True)
    form, up, down, low, high = place(got)
    top = shifted(down, "row", 1)
    bottom = shifted(up, "row", -1)
    left = shifted(column(high, top, bottom, TX - 1), "col", 1)
    right = shifted(column(low, top, bottom, 0), "col", -1)
    result = correlate(form, top, bottom, left, right)
    flow_field = jnp.stack([result[:grid_rows, :grid_cols], result[:grid_rows, 32 : 32 + grid_cols]])
    confidence = result[:grid_rows, 64 : 64 + grid_cols]
    valid_float = patch_valid.astype(jnp.float32)
    strength = valid_float * confidence
    start = valid_float[None] * flow_field
    fields = jnp.concatenate([start, (strength + 4.0 * stiffness)[None]])
    fields = extended_2(fields, (("row", 1), ("col", 2)), SWEEPS)
    mesh = fields[:2]
    below = fields[2]
    inside = below > 0.0
    rest = jnp.where(inside, 1.0 / jnp.where(inside, below, 1.0), 0.0)
    pull = mesh * jnp.where(inside, below - 4.0 * stiffness, 0.0)
    for sweep_index in range(SWEEPS):
        around = mesh[:, :-2, 1:-1] + mesh[:, 2:, 1:-1] + mesh[:, 1:-1, :-2] + mesh[:, 1:-1, 2:]
        rest = rest[1:-1, 1:-1]
        pull = pull[:, 1:-1, 1:-1]
        mesh = (pull + stiffness * around) * rest
    return (flow_field, mesh)


def solution(mesh):
    in_specs = (
        P(("row", "col"), None),
        P(("row", "col")),
        P(("row", "col"), None),
        P(("row", "col"), None),
        P(("row", "col")),
        P(("row", "col"), None),
        P("row", "col"),
    )
    out_specs = (P(None, "row", "col"), P(None, "row", "col"))
    return jax.shard_map(
        per_device, mesh=mesh, in_specs=in_specs, out_specs=out_specs, check_vma=False
    )
```

```python
import math

import jax
import jax.numpy as jnp
import numpy as np
from jax import lax
from jax.experimental import pallas as pl
from jax.experimental.pallas import tpu as pltpu
from jax.sharding import PartitionSpec as P

PATCH = 160
STRIDE = 40
TY = 12
TX = 8
SWEEPS = 3
HALF = PATCH // 2
FREQ = HALF + 1
WIN = 3
GROUPS = 6
ROWS = PATCH
TILE_H = 40
TILE_W = 80
SPLIT = 128 - TILE_W
LANES = 32
SLOT_H = 56
FRAME_H = 608
FORM_H = 488
EDGE_H = 64
TOP = 56

VMEM_SPEC = pl.BlockSpec(memory_space=pltpu.VMEM)

stiffness = 1.0
tiny = 1e-06


def trig():
    k = np.arange(FREQ)
    n = np.arange(PATCH)
    phase = (k[:, None] * n[None, :] % PATCH).astype(np.float64) * (2.0 * math.pi / PATCH)
    cosine, sine = np.cos(phase), np.sin(phase)
    sine[0] = 0.0
    sine[HALF] = 0.0
    return cosine, sine


def tables():
    cosine, sine = trig()
    first = np.zeros((256, 512))
    for w in range(WIN):
        rows = slice(STRIDE * w, STRIDE * w + PATCH)
        first[rows, FREQ * w : FREQ * (w + 1)] = cosine.T
        first[rows, 256 + FREQ * w : 256 + FREQ * (w + 1)] = sine.T
    mixed = np.concatenate([cosine[HALF:], sine[1:HALF], cosine[:HALF]])
    second = np.zeros((2, ROWS, 176))
    for parity in range(2):
        second[parity, :, 8 * parity : 8 * parity + PATCH] = mixed
    half = np.ones((FREQ, 1))
    half[0] = half[HALF] = 0.5
    shift = np.where(np.arange(PATCH) < HALF, np.arange(PATCH), np.arange(PATCH) - PATCH) * (16.0 / PATCH)
    shift[HALF] = 0.0
    rounded = lambda x: x.astype(jnp.bfloat16).astype(np.float64)
    mix = 2.0 * half * ((rounded(cosine) * shift) @ rounded(sine).T)
    sign = half[:, 0] * cosine[:, HALF]
    mix_rows = np.zeros((HALF + 8, ROWS))
    mix_rows[:FREQ, 1:HALF] = mix[:, 1:HALF]
    mix_rows[FREQ, HALF:] = sign[:HALF]
    mix_rows[FREQ, 0] = sign[HALF]
    mix_cols = np.zeros((256, 256))
    sign_cols = np.zeros((16, 256))
    for w in range(WIN):
        mix_cols[FREQ * w : FREQ * (w + 1), FREQ * w : FREQ * (w + 1)] = mix.T
        sign_cols[w, FREQ * w : FREQ * (w + 1)] = sign
    select = np.zeros((1280, 128))
    for w in range(WIN):
        lanes = np.arange(FREQ) + FREQ * w
        select[lanes, w] = half[:, 0]
        select[256 + lanes, w] = 1.0
        select[512 + lanes, 32 + w] = 1.0
        select[768 + lanes, 64 + w] = half[:, 0]
        select[1024 + lanes, 64 + w] = 1.0
    window = np.zeros((256, 128))
    for w in range(WIN):
        for kind in range(3):
            window[STRIDE * w : STRIDE * w + PATCH, 32 * kind + w] = 1.0
    as_bf16 = lambda x: jnp.asarray(x.astype(jnp.bfloat16))
    return tuple(as_bf16(x) for x in (first, second, mix_rows, mix_cols, sign_cols, select, window))


def dot(a, b):
    return lax.dot_general(a, b, (((1,), (0,)), ((), ())), preferred_element_type=jnp.float32)


def dot_exact(a, b):
    return lax.dot_general(
        a,
        b,
        (((1,), (0,)), ((), ())),
        preferred_element_type=jnp.float32,
        precision=lax.Precision.HIGHEST,
    )


EDGE_GROUPS = (0, 4, 5)
INNER_GROUPS = (1, 2, 3)
INNER_LO = 64
INNER_HI = 528


def spread_groups(sums, groups):
    lane = lax.broadcasted_iota(jnp.int32, (16, 128), 1) % 32
    total = jnp.zeros((16, 128), jnp.float32)
    for piece, g in zip(sums, groups):
        piece = piece if g < GROUPS - 1 else jnp.where(lane == 0, piece, 0.0)
        total = total + (pltpu.roll(piece, WIN * g, axis=1) if g else piece)
    return total


def cell_squares(grp, sec, n, cells, lo, hi, base):
    for c in range(lo, hi):
        at = STRIDE * c - base
        near = at // 16 * 16
        values = grp[sec, n, near : near + 48, :].astype(jnp.float32)[at - near : at - near + STRIDE]
        squares = (values * values).reshape(5, 8, 256).sum(axis=0)
        cells[sec, c : c + 1, 256 * n : 256 * n + 256] = jnp.sum(squares, axis=0, keepdims=True)


def window_means(cells, sec, window, groups):
    sums = cells[sec, 0:16, :] + cells[sec, 1:17, :] + cells[sec, 2:18, :] + cells[sec, 3:19, :]
    stacked = jnp.concatenate([sums[:, 256 * n : 256 * n + 256] for n in range(WIN)], axis=0)
    total = dot_exact(stacked, window).reshape(WIN, 16, 128)
    return spread_groups([total[n] for n in range(WIN)], groups) / (PATCH * PATCH) + tiny


def group_pixels(tile, sec, g):
    c = 3 * (g // 2) + g % 2
    offset = 20 + 40 * (g % 2)
    pieces = []
    left = 240
    while left > 0 and c < 10:
        values = tile(c)
        width = min(TILE_W - offset, left)
        if sec == 0:
            pieces.append(values[:, offset : offset + width])
        else:
            if offset < SPLIT:
                pieces.append(values[:, TILE_W + offset : TILE_W + min(SPLIT, offset + width)])
            if offset + width > SPLIT:
                pieces.append(values[:, max(0, offset - SPLIT) : offset + width - SPLIT])
        left -= width
        offset = 0
        c += 1
    rows = pieces[0].shape[0]
    pieces.append(jnp.zeros((rows, 256 - 240 + left), pieces[0].dtype))
    return jnp.concatenate(pieces, axis=1)


def frame_column(form, top, bottom, frame, sec, c, upper, lower):
    t = c - 1
    if upper == lower:
        frame[sec, c, TOP : TOP + FORM_H, :] = form[t, sec]
    else:
        frame[sec, c, TOP:upper, :] = form[t, sec, 0 : upper - TOP, :]
        frame[sec, c, lower : TOP + FORM_H, :] = form[t, sec, lower - TOP :, :]
    frame[sec, c, 0:TOP, :] = top[t, sec, 0:TOP, :]
    frame[sec, c, 544:600, :] = bottom[t, sec, 8:EDGE_H, :]
    frame[sec, c, 600:608, :] = jnp.zeros((8, 128), jnp.bfloat16)
    for dst, own, other in (
        (TOP, form[t, sec, 0:8, :], top[t, sec, TOP:EDGE_H, :]),
        (536, form[t, sec, 480:488, :], bottom[t, sec, 0:8, :]),
    ):
        both = own.astype(jnp.float32) + other.astype(jnp.float32)
        frame[sec, c, dst : dst + 8, :] = both.astype(jnp.bfloat16)


def run_steps(step_of, count, base, fa, fb, second, mix_rows, mix_cols, sign_cols, raw, raw_end, work):
    spec, cross, flow_rows, flow_cols = work
    sub = lax.broadcasted_iota(jnp.int32, (8, 256), 0)
    top = sub == 0
    top_half = jnp.where(top, 0.5, 1.0)
    lane128 = lax.broadcasted_iota(jnp.int32, (8, 128), 1)
    k_lane = lax.broadcasted_iota(jnp.int32, (8, ROWS), 1)
    end_weight = jnp.where((k_lane == 0) | (k_lane == HALF), -4.0, -8.0)

    def row_of(m):
        valid = (m >= 0) & (m < count)
        n, i = step_of(jnp.clip(m, 0, count - 1))
        return n, jnp.where(valid, i, 15), i // 2

    def spectra(m, parity):
        g, _, q = row_of(m)
        start = pl.multiple_of(80 * q + (32 * parity - base), 16)
        spec[parity, 0] = dot(second[parity], fa[g, pl.ds(start, 176), :])
        spec[parity, 1] = dot(second[parity], fb[g, pl.ds(start, 176), :])

    def products(m, parity):
        g, i, _ = row_of(m)
        total = None
        for half in range(2):
            sides = []
            for sec in range(2):
                sides.append([])
                for base in (HALF, 0):
                    for lo in (0, 256):
                        sides[sec].append(
                            spec[parity, sec, base : base + HALF, lo : lo + 256].reshape(10, 8, 256)[5 * half : 5 * half + 5]
                        )
            terms = [(cc - ss, sc + cs, cc + ss, sc - cs) for cc, cs, sc, ss in sides]
            (a1, a2, a3, a4), (b1, b2, b3, b4) = terms
            plus_r = a1 * b1 + a2 * b2
            plus_i = a1 * b2 - a2 * b1
            minus_r = a3 * b3 + a4 * b4
            minus_i = a3 * b4 - a4 * b3
            dcc = plus_r + minus_r
            dss = minus_r - plus_r
            dsc = plus_i + minus_i
            dcs = plus_i - minus_i
            if half == 0:
                (ac, asn, ae, aes), (bc, bsn, be, bes) = [[x[0] for x in side] for side in sides]
                fix = lambda new, old: jnp.concatenate([jnp.where(top, new, old[0])[None], old[1:]], axis=0)
                dcc = fix(2.0 * (ac * bc + asn * bsn), dcc)
                dcs = fix(2.0 * (ac * bsn - asn * bc), dcs)
                dsc = fix(2.0 * (ae * be + aes * bes), dsc)
                dss = fix(2.0 * (ae * bes - aes * be), dss)
            rows = slice(40 * half, 40 * half + 40)
            cos_rows = slice(HALF + 40 * half, HALF + 40 * half + 40)
            cross[parity, rows, 0:256] = dsc.reshape(40, 256).astype(jnp.bfloat16)
            cross[parity, rows, 256:512] = dss.reshape(40, 256).astype(jnp.bfloat16)
            cross[parity, cos_rows, 0:256] = dcc.reshape(40, 256).astype(jnp.bfloat16)
            cross[parity, cos_rows, 256:512] = dcs.reshape(40, 256).astype(jnp.bfloat16)
            low = dcc * dcc + dsc * dsc
            high = dcs * dcs + dss * dss
            if half == 0:
                total = [low[0] * top_half + low[1:].sum(axis=0), high[0] * top_half + high[1:].sum(axis=0)]
            else:
                total = [total[0] + low.sum(axis=0), total[1] + high.sum(axis=0)]
        total = jnp.concatenate(total, axis=1)
        raw[g, pl.ds(i, 1), 768:1280] = jnp.sum(total, axis=0, keepdims=True)

    def flows(m, parity):
        g, i, _ = row_of(m)
        flow_rows[parity] = dot(mix_rows[...], cross[parity])
        flow_cols[parity] = dot(cross[parity, :, 256:512], mix_cols[...])
        end = lax.dot_general(
            sign_cols[...], cross[parity, :, 0:256], (((1,), (1,)), ((), ())), preferred_element_type=jnp.float32
        )[:8]
        end = jnp.sum(end * end * end_weight, axis=1, keepdims=True)
        raw_end[g] = jnp.where(lane128 == i, end, raw_end[g])

    def flow_sums(m, parity):
        g, i, _ = row_of(m)
        cosines = cross[parity, HALF:, :].astype(jnp.float32).reshape(10, 8, 512)
        mixed = flow_rows[parity].reshape(11, 8, 512)
        flow_y = cosines[0] * mixed[0]
        for t in range(1, 10):
            flow_y = flow_y + cosines[t] * mixed[t]
        end = cross[parity, 0:16, :].astype(jnp.float32)[:1] * mixed[10, 0:1] - 8.0 * mixed[10, 1:2] * mixed[10, 1:2]
        raw[g, pl.ds(i, 1), 0:512] = jnp.sum(flow_y, axis=0, keepdims=True) + end
        cosines = cross[parity, :, 0:256].astype(jnp.float32).reshape(20, 8, 256)
        mixed = flow_cols[parity].reshape(20, 8, 256)
        flow_x = (cosines[0] * mixed[0] + cosines[10] * mixed[10]) * top_half
        for t in range(1, 20):
            if t != 10:
                flow_x = flow_x + cosines[t] * mixed[t]
        raw[g, pl.ds(i, 1), 512:768] = jnp.sum(flow_x, axis=0, keepdims=True)

    def step(n, carry):
        for parity in range(2):
            m = 2 * n + parity
            flow_sums(m - 3, 1 - parity)
            flows(m - 2, parity)
            products(m - 1, 1 - parity)
            spectra(m, parity)
        return carry

    lax.fori_loop(0, count // 2 + 2, step, 0)


def finish(raw, raw_end, cells, select, window, groups):
    window = window[...].astype(jnp.float32)
    scale = (1.0 / (PATCH * PATCH)) / (
        window_means(cells, 0, window, groups) * window_means(cells, 1, window, groups)
    )
    sums = dot_exact(raw[...].reshape(WIN * 16, 1280), select[...].astype(jnp.float32)).reshape(WIN, 16, 128)
    pad = jnp.zeros((120, 128), jnp.float32)
    ends = [
        pltpu.roll(jnp.concatenate([raw_end[n], pad], axis=0).T[:16], 32, axis=1) for n in range(WIN)
    ]
    total = spread_groups([sums[n] + ends[n] for n in range(WIN)], groups)
    unit = (2.0 / (PATCH * PATCH)) ** 2 * HALF / (PATCH * PATCH)
    total = total * (scale * unit)
    lane_all = lax.broadcasted_iota(jnp.int32, (16, 128), 1)
    weight = jnp.where(lane_all >= 64, total * HALF, 0.0)
    down = 1.0 + weight + pltpu.roll(weight, 96, axis=1) + pltpu.roll(weight, 64, axis=1)
    return jnp.where(lane_all >= 64, weight, total) / down


def clear_sums(raw, raw_end):
    raw[:, 12:16, :] = jnp.zeros((WIN, 4, 1280), jnp.float32)
    raw_end[...] = jnp.zeros((WIN, 8, 128), jnp.float32)


def early_step(m):
    return m // 8, 2 + m % 8


def edge_step(m):
    return m // 12, m % 12


def late_step(m):
    return m // 4, m % 4 + jnp.where(m % 4 >= 2, 8, 0)


def early_kernel(
    form, first, second, mix_rows, mix_cols, sign_cols, select, window, out, grp, fa, fb, cells, raw, raw_end, *work
):
    lo, hi = INNER_LO - TOP, INNER_HI - TOP
    clear_sums(raw, raw_end)
    raw[:, 0:2, :] = jnp.zeros((WIN, 2, 1280), jnp.float32)
    raw[:, 10:12, :] = jnp.zeros((WIN, 2, 1280), jnp.float32)
    for sec, dst in ((0, fa), (1, fb)):
        cells[sec] = jnp.zeros((24, 256 * WIN), jnp.float32)
        for n, g in enumerate(INNER_GROUPS):
            pixels = group_pixels(lambda c: form[c - 1, sec, lo:hi, :], sec, g)
            grp[sec, n] = pixels
            dst[n] = dot(pixels, first[...]).astype(jnp.bfloat16)
            cell_squares(grp, sec, n, cells, 2, 13, INNER_LO)
    run_steps(
        early_step, 24, INNER_LO, fa, fb, second, mix_rows, mix_cols, sign_cols, raw, raw_end, work
    )
    out[...] = finish(raw, raw_end, cells, select, window, INNER_GROUPS)


def mesh_fields(result, valid):
    row = lax.broadcasted_iota(jnp.int32, (16, 128), 0)
    lane = lax.broadcasted_iota(jnp.int32, (16, 128), 1)
    column = lane % 32
    inside = (row < 12) & (lane < 96) & (column >= SWEEPS) & (column < SWEEPS + 16)
    flags = jnp.concatenate([valid[...].astype(jnp.float32), jnp.zeros((12, 112), jnp.float32)], axis=1)
    flags = jnp.concatenate([flags, jnp.zeros((4, 128), jnp.float32)], axis=0)
    flags = sum(pltpu.roll(flags, SWEEPS + 32 * kind, axis=1) for kind in range(3))
    fields = flags * pltpu.roll(jnp.where(row < 12, result, 0.0), SWEEPS, axis=1)
    fields = fields + jnp.where(lane >= 64, 4.0 * stiffness, 0.0)
    return jnp.where(inside, fields, 0.0), column


def edge_kernel(
    form, top, bottom, left, right, valid, first, second, mix_rows, mix_cols, sign_cols, select, window,
    out, to_right, to_left, frame, grp, fa, fb, cells, raw, raw_end, *work,
):
    clear_sums(raw, raw_end)
    for sec, dst in ((0, fa), (1, fb)):
        frame[sec, 0] = left[sec]
        frame[sec, 9] = right[sec]
        for c in (1, 2, 3, 6, 7, 8):
            frame_column(form, top, bottom, frame, sec, c, FRAME_H, FRAME_H)
        for n, g in enumerate(EDGE_GROUPS):
            pixels = group_pixels(lambda c: frame[sec, c], sec, g)
            grp[sec, n] = pixels
            dst[n] = dot(pixels, first[...]).astype(jnp.bfloat16)
            cell_squares(grp, sec, n, cells, 0, 15, 0)
        cells[sec, 15:24, :] = jnp.zeros((9, 256 * WIN), jnp.float32)
    run_steps(edge_step, 36, 0, fa, fb, second, mix_rows, mix_cols, sign_cols, raw, raw_end, work)
    result = finish(raw, raw_end, cells, select, window, EDGE_GROUPS)
    out[...] = result
    fields, column = mesh_fields(result, valid)
    last = jnp.where((column >= 16) & (column < 16 + SWEEPS), fields, 0.0)
    to_right[...] = pltpu.roll(last, 112, axis=1)
    head = jnp.where((column >= SWEEPS) & (column < 2 * SWEEPS), fields, 0.0)
    to_left[...] = pltpu.roll(head, 16, axis=1)


def late_kernel(
    form, top, bottom, early, edge, valid, first, second, mix_rows, mix_cols, sign_cols, select, window,
    out, fields, frame, grp, fa, fb, cells, raw, raw_end, *work,
):
    upper, lower = 208, 400
    clear_sums(raw, raw_end)
    raw[:, 2:10, :] = jnp.zeros((WIN, 8, 1280), jnp.float32)
    for sec, dst in ((0, fa), (1, fb)):
        cells[sec] = jnp.zeros((24, 256 * WIN), jnp.float32)
        for c in range(1, 8):
            frame_column(form, top, bottom, frame, sec, c, upper, lower)
        for n, g in enumerate(INNER_GROUPS):
            for lo, hi in ((0, upper), (lower, FRAME_H)):
                pixels = group_pixels(lambda c: frame[sec, c, lo:hi, :], sec, g)
                grp[sec, n, lo:hi, :] = pixels
                dst[n, lo:hi, :] = dot(pixels, first[...]).astype(jnp.bfloat16)
            cell_squares(grp, sec, n, cells, 0, 5, 0)
            cell_squares(grp, sec, n, cells, 10, 15, 0)
    run_steps(late_step, 12, 0, fa, fb, second, mix_rows, mix_cols, sign_cols, raw, raw_end, work)
    row = lax.broadcasted_iota(jnp.int32, (16, 128), 0)
    lane = lax.broadcasted_iota(jnp.int32, (16, 128), 1) % 32
    own = finish(raw, raw_end, cells, select, window, INNER_GROUPS)
    own = jnp.where((row >= 2) & (row < 10), early[...], own)
    result = jnp.where((lane >= 3) & (lane < 12), own, edge[...])
    out[...] = result
    fields[...] = mesh_fields(result, valid)[0]


def relax_kernel(result, fields, above, beneath, flow, mesh_out):
    frame = jnp.concatenate(
        [above[...][1:4], fields[...][:12], beneath[...][:SWEEPS], jnp.zeros((6, 128), jnp.float32)],
        axis=0,
    )
    lane = lax.broadcasted_iota(jnp.int32, (24, 128), 1)
    below = jnp.where(lane < 32, pltpu.roll(frame, 64, axis=1), pltpu.roll(frame, 96, axis=1))
    inside = (below > 0.0) & (lane < 64)
    rest = jnp.where(inside, 1.0 / jnp.where(inside, below, 1.0), 0.0)
    mesh = jnp.where(lane < 64, frame, 0.0)
    pull = mesh * jnp.where(inside, below - 4.0 * stiffness, 0.0)
    for _ in range(SWEEPS):
        around = (
            pltpu.roll(mesh, 1, axis=0)
            + pltpu.roll(mesh, 23, axis=0)
            + pltpu.roll(mesh, 1, axis=1)
            + pltpu.roll(mesh, 127, axis=1)
        )
        mesh = (pull + stiffness * around) * rest
    for kind in range(2):
        flow[kind] = result[0:12, 32 * kind : 32 * kind + 16]
        mesh_out[kind] = mesh[SWEEPS : SWEEPS + 12, 32 * kind + SWEEPS : 32 * kind + SWEEPS + 16]


def work_shapes():
    return [
        pltpu.VMEM((2, 2, ROWS, 512), jnp.float32),
        pltpu.VMEM((2, ROWS, 512), jnp.bfloat16),
        pltpu.VMEM((2, HALF + 8, 512), jnp.float32),
        pltpu.VMEM((2, ROWS, 256), jnp.float32),
    ]


SUM_SHAPES = (
    ((2, 24, 256 * WIN), jnp.float32),
    ((WIN, 16, 1280), jnp.float32),
    ((WIN, 8, 128), jnp.float32),
)


def sum_shapes(make):
    return [make(*shape) for shape in SUM_SHAPES]


def grow_params(mib):
    return pltpu.CompilerParams(vmem_limit_bytes=mib << 20)


def frame_shapes():
    return [
        pltpu.VMEM((2, 10, FRAME_H, 128), jnp.bfloat16),
        pltpu.VMEM((2, WIN, FRAME_H, 256), jnp.bfloat16),
        pltpu.VMEM((WIN, FRAME_H, 512), jnp.bfloat16),
        pltpu.VMEM((WIN, FRAME_H, 512), jnp.bfloat16),
        *sum_shapes(pltpu.VMEM),
        *work_shapes(),
    ]


SMALL = jax.ShapeDtypeStruct((16, 128), jnp.float32)


def correlate_early(form, consts):
    height = INNER_HI - INNER_LO
    return pl.pallas_call(
        early_kernel,
        out_shape=SMALL,
        in_specs=[VMEM_SPEC] * 8,
        out_specs=VMEM_SPEC,
        scratch_shapes=[
            pltpu.VMEM((2, WIN, height, 256), jnp.bfloat16),
            pltpu.VMEM((WIN, height, 512), jnp.bfloat16),
            pltpu.VMEM((WIN, height, 512), jnp.bfloat16),
            *sum_shapes(pltpu.VMEM),
            *work_shapes(),
        ],
        compiler_params=grow_params(20),
    )(form, *consts)


def correlate_edge(form, top, bottom, left, right, valid, consts):
    return pl.pallas_call(
        edge_kernel,
        out_shape=(SMALL,) * 3,
        in_specs=[VMEM_SPEC] * 13,
        out_specs=(VMEM_SPEC,) * 3,
        scratch_shapes=frame_shapes(),
        compiler_params=grow_params(24),
    )(form, top, bottom, left, right, valid, *consts)


def correlate_late(form, top, bottom, early, edge, valid, consts):
    return pl.pallas_call(
        late_kernel,
        out_shape=(SMALL,) * 2,
        in_specs=[VMEM_SPEC] * 13,
        out_specs=(VMEM_SPEC,) * 2,
        scratch_shapes=frame_shapes(),
        compiler_params=grow_params(24),
    )(form, top, bottom, early, edge, valid, *consts)


def relax(result, fields, above, beneath):
    field = jax.ShapeDtypeStruct((2, 12, 16), jnp.float32)
    return pl.pallas_call(
        relax_kernel,
        out_shape=(field, field),
        in_specs=[VMEM_SPEC] * 4,
        out_specs=(VMEM_SPEC,) * 2,
        compiler_params=grow_params(8),
    )(result, fields, above, beneath)


def pack_kernel(*refs):
    sources, out, rows, held, arrived = refs[:6], refs[6], refs[7], refs[8:14], refs[14]
    copies = [pltpu.make_async_copy(src, dst, arrived.at[n]) for n, (src, dst) in enumerate(zip(sources, held))]
    for copy in copies:
        copy.start()
    for copy in copies:
        copy.wait()
    a_tiles, b_tiles, a_owner, b_owner, a_offset, b_offset = held
    count = a_tiles.shape[0]
    owners = jnp.concatenate([a_owner[...], b_owner[...]], axis=1)
    slot = lax.broadcasted_iota(jnp.int32, (128, 2 * count), 0)
    select = jnp.where(slot == owners, 1.0, 0.0).astype(jnp.bfloat16)
    zero = lambda width: jnp.zeros((count, width), jnp.bfloat16)

    def position(offset):
        row = offset[0:1, :].astype(jnp.float32)
        col = offset[1:2, :].astype(jnp.float32)
        code = jnp.floor(row * (TX / TILE_H) + col * (1.0 / TILE_W) + 1.5)
        code = jnp.concatenate([code, jnp.zeros((1, 128 - count), jnp.float32)], axis=1)
        return jnp.broadcast_to(code, (128, 128)).T[:count]

    def piece(tiles, start, width):
        return tiles[:, start : start + width]

    lane = lax.broadcasted_iota(jnp.int32, (count, 128), 1)
    code_a = jnp.where(lane == 64, position(a_offset), 0.0).astype(jnp.bfloat16)
    code_b = jnp.where(lane == 96, position(b_offset), 0.0).astype(jnp.bfloat16)

    def send_row(y):
        if y < TILE_H:
            a_part = jnp.concatenate([piece(a_tiles, TILE_W * y, TILE_W), zero(SPLIT)], axis=1)
            b_part = jnp.concatenate([zero(TILE_W), piece(b_tiles, TILE_W * y, SPLIT)], axis=1)
        elif y < TILE_H + 8:
            u = y - TILE_H
            a_part = zero(128)
            b_part = jnp.concatenate(
                [piece(b_tiles, TILE_W * (8 * k + u) + SPLIT, LANES) for k in range(4)], axis=1
            )
        else:
            u = y - TILE_H - 8
            a_part = code_a
            b_part = jnp.concatenate(
                [piece(b_tiles, TILE_W * (32 + u) + SPLIT, LANES), zero(96)], axis=1
            )
            b_part = b_part + code_b
        return jnp.concatenate([a_part, b_part], axis=0)

    for y in range(0, SLOT_H, 2):
        both = jnp.concatenate([send_row(y), send_row(y + 1)], axis=1)
        sent = dot(select, both)
        rows[pl.ds(y, 128, stride=SLOT_H), :] = sent[:, :128]
        rows[pl.ds(y + 1, 128, stride=SLOT_H), :] = sent[:, 128:]

    def flush(n, carry):
        start = pl.multiple_of(8 * SLOT_H * n, 8)
        block = rows[pl.ds(start, 8 * SLOT_H), :].reshape(8, SLOT_H, 128)
        out[pl.ds(8 * n, 8)] = block.astype(jnp.bfloat16)
        return carry

    lax.fori_loop(0, 16, flush, 0)


def place_kernel(got, form, up, down, low, high, rows, plane_a, plane_b):
    def widen(n, carry):
        start = pl.multiple_of(8 * SLOT_H * n, 8)
        block = got[pl.ds(8 * n, 8)].astype(jnp.float32)
        rows[pl.ds(start, 8 * SLOT_H), :] = block.reshape(8 * SLOT_H, 128)
        return carry

    lax.fori_loop(0, 16, widen, 0)
    codes = rows[pl.ds(TILE_H + 8, 128, stride=SLOT_H), :]
    wanted = lax.broadcasted_iota(jnp.int32, (128, 128), 1).astype(jnp.float32) + 1.0
    pick = lambda col: jnp.where(codes[:, col : col + 1] == wanted, 1.0, 0.0).T[:96]
    select_a = pick(64)
    select_b = pick(96)
    select = jnp.concatenate([select_a, select_b], axis=0).astype(jnp.bfloat16)
    select_b = select_b.astype(jnp.bfloat16)

    def slot_row(y):
        return rows[pl.ds(y, 128, stride=SLOT_H), :].astype(jnp.bfloat16)

    for plane in (plane_a, plane_b):
        for t in range(TX):
            plane[FORM_H * t : FORM_H * t + 8, :] = jnp.zeros((8, 128), jnp.float32)
            plane[FORM_H * t + 480 : FORM_H * t + 488, :] = jnp.zeros((8, 128), jnp.float32)
    lane = lax.broadcasted_iota(jnp.int32, (96, 128), 1)
    tail = lane < LANES

    for u in range(0, 8, 2):
        tails = jnp.concatenate([slot_row(TILE_H + u + v + w) for v in range(2) for w in (0, 8)], axis=1)
        tails = dot(select_b, tails)
        for k in range(5):
            y = 8 * k + u
            main = dot(select, jnp.concatenate([slot_row(y), slot_row(y + 1)], axis=1))
            for v in range(2):
                part_a = main[:96, 128 * v : 128 * v + 128]
                part_b = main[96:, 128 * v : 128 * v + 128]
                rest = tails[:, 256 * v : 256 * v + 128] if k < 4 else tails[:, 256 * v + 128 : 256 * v + 256]
                if 0 < k < 4:
                    rest = pltpu.roll(rest, 128 - LANES * k, axis=1)
                part_b = jnp.where(tail, rest, part_b)
                for ty in range(TY):
                    where = pl.ds(TILE_H * ty + y + v + 4, TX, stride=FORM_H)
                    plane_a[where, :] = part_a[TX * ty : TX * ty + TX]
                    plane_b[where, :] = part_b[TX * ty : TX * ty + TX]

    for sec, plane in ((0, plane_a), (1, plane_b)):
        for t in range(TX):
            block = plane[FORM_H * t : FORM_H * t + FORM_H, :].astype(jnp.bfloat16)
            form[t, sec] = block
            for side, at in ((low, 0), (high, TX - 1)):
                if t == at:
                    side[sec, 0:TOP, :] = jnp.zeros((TOP, 128), jnp.bfloat16)
                    side[sec, TOP : TOP + FORM_H, :] = block
                    side[sec, TOP + FORM_H :, :] = jnp.zeros((FRAME_H - TOP - FORM_H, 128), jnp.bfloat16)
            up[t, sec] = plane[FORM_H * t : FORM_H * t + EDGE_H, :].astype(jnp.bfloat16)
            down[t, sec] = plane[FORM_H * t + 424 : FORM_H * t + 488, :].astype(jnp.bfloat16)


def pack(*arrays):
    return pl.pallas_call(
        pack_kernel,
        out_shape=jax.ShapeDtypeStruct((128, SLOT_H, 128), jnp.bfloat16),
        in_specs=[pl.BlockSpec(memory_space=pltpu.HBM)] * 6,
        out_specs=VMEM_SPEC,
        scratch_shapes=[
            pltpu.VMEM((128 * SLOT_H, 128), jnp.float32),
            *[pltpu.VMEM(x.shape, x.dtype) for x in arrays],
            pltpu.SemaphoreType.DMA((6,)),
        ],
        compiler_params=pltpu.CompilerParams(vmem_limit_bytes=60 << 20),
    )(*arrays)


def place(got):
    edge = jax.ShapeDtypeStruct((TX, 2, EDGE_H, 128), jnp.bfloat16)
    side = jax.ShapeDtypeStruct((2, FRAME_H, 128), jnp.bfloat16)
    return pl.pallas_call(
        place_kernel,
        out_shape=(jax.ShapeDtypeStruct((TX, 2, FORM_H, 128), jnp.bfloat16), edge, edge, side, side),
        scratch_shapes=[
            pltpu.VMEM((128 * SLOT_H, 128), jnp.float32),
            pltpu.VMEM((TX * FORM_H, 128), jnp.float32),
            pltpu.VMEM((TX * FORM_H, 128), jnp.float32),
        ],
        in_specs=[VMEM_SPEC],
        out_specs=(VMEM_SPEC,) * 5,
        compiler_params=pltpu.CompilerParams(vmem_limit_bytes=24 << 20),
    )(got)


def shifted(block, axis, step):
    count = lax.axis_size(axis)
    pairs = [(i, i + step) for i in range(count) if 0 <= i + step < count]
    return lax.ppermute(block, axis, pairs)


def column(side, top, bottom, t):
    grow = lambda x, low, high: jnp.pad(x[t], ((0, 0), (low, high), (0, 0)))
    return side + grow(top, 0, FRAME_H - EDGE_H) + grow(bottom, 536, FRAME_H - 536 - EDGE_H)


def per_device(a_tiles, a_owner, a_offset, b_tiles, b_owner, b_offset, patch_valid):
    packed = pack(a_tiles, b_tiles, a_owner[None], b_owner[None], a_offset.T, b_offset.T)
    got = lax.all_to_all(packed, ("row", "col"), split_axis=0, concat_axis=0, tiled=True)
    form, up, down, low, high = place(got)
    consts = tables()
    top = shifted(down, "row", 1)
    bottom = shifted(up, "row", -1)
    early = correlate_early(form, consts)
    left = shifted(column(high, top, bottom, TX - 1), "col", 1)
    right = shifted(column(low, top, bottom, 0), "col", -1)
    edge, to_right, to_left = correlate_edge(form, top, bottom, left, right, patch_valid, consts)
    from_left = shifted(to_right, "col", 1)
    from_right = shifted(to_left, "col", -1)
    result, fields = correlate_late(form, top, bottom, early, edge, patch_valid, consts)
    fields = fields + from_left + from_right
    above = shifted(fields[8:16], "row", 1)
    beneath = shifted(fields[0:8], "row", -1)
    return relax(result, fields, above, beneath)


def solution(mesh):
    in_specs = (
        P(("row", "col"), None),
        P(("row", "col")),
        P(("row", "col"), None),
        P(("row", "col"), None),
        P(("row", "col")),
        P(("row", "col"), None),
        P("row", "col"),
    )
    out_specs = (P(None, "row", "col"), P(None, "row", "col"))
    return jax.shard_map(
        per_device, mesh=mesh, in_specs=in_specs, out_specs=out_specs, check_vma=False
    )
```

```python
import math

import jax
import jax.numpy as jnp
import numpy as np
from jax import lax
from jax.experimental import pallas as pl
from jax.experimental.pallas import tpu as pltpu
from jax.sharding import PartitionSpec as P

PATCH = 160
STRIDE = 40
TY = 12
TX = 8
SWEEPS = 3
HALF = PATCH // 2
FREQ = HALF + 1
WIN = 3
GROUPS = 6
ROWS = PATCH
PAIR_H = 208
TILE_H = 40
TILE_W = 80
SPLIT = 128 - TILE_W
LANES = 32
SLOT_H = 56
FRAME_H = 608
FORM_H = 488
EDGE_H = 64
TOP = 56

VMEM_SPEC = pl.BlockSpec(memory_space=pltpu.VMEM)

stiffness = 1.0
tiny = 1e-06


def trig():
    k = np.arange(FREQ)
    n = np.arange(PATCH)
    phase = (k[:, None] * n[None, :] % PATCH).astype(np.float64) * (2.0 * math.pi / PATCH)
    cosine, sine = np.cos(phase), np.sin(phase)
    sine[0] = 0.0
    sine[HALF] = 0.0
    return cosine, sine


def tables():
    cosine, sine = trig()
    first = np.zeros((256, 512))
    for w in range(WIN):
        rows = slice(STRIDE * w, STRIDE * w + PATCH)
        first[rows, FREQ * w : FREQ * (w + 1)] = cosine.T
        first[rows, 256 + FREQ * w : 256 + FREQ * (w + 1)] = sine.T
    mixed = np.concatenate([cosine[HALF:], sine[1:HALF], cosine[:HALF]])
    second = np.zeros((2, ROWS, PAIR_H))
    for parity in range(2):
        second[parity, :, STRIDE * parity : STRIDE * parity + PATCH] = mixed
    second = second.reshape(2 * ROWS, PAIR_H)
    half = np.ones((FREQ, 1))
    half[0] = half[HALF] = 0.5
    shift = np.where(np.arange(PATCH) < HALF, np.arange(PATCH), np.arange(PATCH) - PATCH) * (16.0 / PATCH)
    shift[HALF] = 0.0
    rounded = lambda x: x.astype(jnp.bfloat16).astype(np.float64)
    mix = 2.0 * half * ((rounded(cosine) * shift) @ rounded(sine).T)
    sign = half[:, 0] * cosine[:, HALF]
    mix_rows = np.zeros((HALF + 8, ROWS))
    mix_rows[:FREQ, 1:HALF] = mix[:, 1:HALF]
    mix_rows[FREQ, HALF:] = sign[:HALF]
    mix_rows[FREQ, 0] = sign[HALF]
    mix_cols = np.zeros((256, 256))
    sign_cols = np.zeros((16, 256))
    for w in range(WIN):
        mix_cols[FREQ * w : FREQ * (w + 1), FREQ * w : FREQ * (w + 1)] = mix.T
        sign_cols[w, FREQ * w : FREQ * (w + 1)] = sign
    select = np.zeros((1280, 128))
    for w in range(WIN):
        lanes = np.arange(FREQ) + FREQ * w
        select[lanes, w] = half[:, 0]
        select[256 + lanes, w] = 1.0
        select[512 + lanes, 32 + w] = 1.0
        select[768 + lanes, 64 + w] = half[:, 0]
        select[1024 + lanes, 64 + w] = 1.0
    window = np.zeros((256, 128))
    for w in range(WIN):
        for kind in range(3):
            window[STRIDE * w : STRIDE * w + PATCH, 32 * kind + w] = 1.0
    as_bf16 = lambda x: jnp.asarray(x.astype(jnp.bfloat16))
    return tuple(as_bf16(x) for x in (first, second, mix_rows, mix_cols, sign_cols, select, window))


def dot(a, b):
    return lax.dot_general(a, b, (((1,), (0,)), ((), ())), preferred_element_type=jnp.float32)


def dot_exact(a, b):
    return lax.dot_general(
        a,
        b,
        (((1,), (0,)), ((), ())),
        preferred_element_type=jnp.float32,
        precision=lax.Precision.HIGHEST,
    )


EDGE_GROUPS = (0, 4, 5)
INNER_GROUPS = (1, 2, 3)
INNER_LO = 64
INNER_HI = 528


def spread_groups(sums, groups):
    lane = lax.broadcasted_iota(jnp.int32, (16, 128), 1) % 32
    total = jnp.zeros((16, 128), jnp.float32)
    for piece, g in zip(sums, groups):
        piece = piece if g < GROUPS - 1 else jnp.where(lane == 0, piece, 0.0)
        total = total + (pltpu.roll(piece, WIN * g, axis=1) if g else piece)
    return total


def cell_squares(grp, sec, n, cells, lo, hi, base):
    for c in range(lo, hi):
        at = STRIDE * c - base
        near = at // 16 * 16
        values = grp[sec, n, near : near + 48, :].astype(jnp.float32)[at - near : at - near + STRIDE]
        squares = (values * values).reshape(5, 8, 256).sum(axis=0)
        cells[sec, c : c + 1, 256 * n : 256 * n + 256] = jnp.sum(squares, axis=0, keepdims=True)


def window_means(cells, sec, window, groups):
    sums = cells[sec, 0:16, :] + cells[sec, 1:17, :] + cells[sec, 2:18, :] + cells[sec, 3:19, :]
    stacked = jnp.concatenate([sums[:, 256 * n : 256 * n + 256] for n in range(WIN)], axis=0)
    total = dot_exact(stacked, window).reshape(WIN, 16, 128)
    return spread_groups([total[n] for n in range(WIN)], groups) / (PATCH * PATCH) + tiny


def group_pixels(tile, sec, g):
    c = 3 * (g // 2) + g % 2
    offset = 20 + 40 * (g % 2)
    pieces = []
    left = 240
    while left > 0 and c < 10:
        values = tile(c)
        width = min(TILE_W - offset, left)
        if sec == 0:
            pieces.append(values[:, offset : offset + width])
        else:
            if offset < SPLIT:
                pieces.append(values[:, TILE_W + offset : TILE_W + min(SPLIT, offset + width)])
            if offset + width > SPLIT:
                pieces.append(values[:, max(0, offset - SPLIT) : offset + width - SPLIT])
        left -= width
        offset = 0
        c += 1
    rows = pieces[0].shape[0]
    pieces.append(jnp.zeros((rows, 256 - 240 + left), pieces[0].dtype))
    return jnp.concatenate(pieces, axis=1)


def frame_column(form, top, bottom, frame, sec, c, upper, lower):
    t = c - 1
    if upper == lower:
        frame[sec, c, TOP : TOP + FORM_H, :] = form[t, sec]
    else:
        frame[sec, c, TOP:upper, :] = form[t, sec, 0 : upper - TOP, :]
        frame[sec, c, lower : TOP + FORM_H, :] = form[t, sec, lower - TOP :, :]
    frame[sec, c, 0:TOP, :] = top[t, sec, 0:TOP, :]
    frame[sec, c, 544:600, :] = bottom[t, sec, 8:EDGE_H, :]
    frame[sec, c, 600:608, :] = jnp.zeros((8, 128), jnp.bfloat16)
    for dst, own, other in (
        (TOP, form[t, sec, 0:8, :], top[t, sec, TOP:EDGE_H, :]),
        (536, form[t, sec, 480:488, :], bottom[t, sec, 0:8, :]),
    ):
        both = own.astype(jnp.float32) + other.astype(jnp.float32)
        frame[sec, c, dst : dst + 8, :] = both.astype(jnp.bfloat16)


def run_steps(step_of, pairs, base, fa, fb, second, mix_rows, mix_cols, sign_cols, raw, raw_end, work):
    spec, cross, flow_rows, flow_cols = work
    sub = lax.broadcasted_iota(jnp.int32, (8, 256), 0)
    top = sub == 0
    top_half = jnp.where(top, 0.5, 1.0)
    lane128 = lax.broadcasted_iota(jnp.int32, (8, 128), 1)
    k_lane = lax.broadcasted_iota(jnp.int32, (8, ROWS), 1)
    end_weight = jnp.where((k_lane == 0) | (k_lane == HALF), -4.0, -8.0)

    def spectra(pair, buf):
        n, q = step_of(pair)
        start = 80 * q - base
        if not isinstance(start, int):
            start = pl.multiple_of(start, 16)
        for sec, src in ((0, fa), (1, fb)):
            spec[buf, sec] = dot(second[...], src[n, pl.ds(start, PAIR_H), :])

    def products(pair, buf, parity):
        n, q = step_of(pair)
        shift = ROWS * parity
        totals = []
        top16 = lax.broadcasted_iota(jnp.int32, (16, 128), 0) == 0
        for lane in (0, 128):
            low = high = None
            for r in range(0, HALF, 16):
                sides = [
                    [
                        spec[buf, sec, shift + at + r : shift + at + r + 16, lo + lane : lo + lane + 128]
                        for at in (HALF, 0)
                        for lo in (0, 256)
                    ]
                    for sec in range(2)
                ]
                (a1, a2, a3, a4), (b1, b2, b3, b4) = [
                    (cc - ss, sc + cs, cc + ss, sc - cs) for cc, cs, sc, ss in sides
                ]
                plus_r = a1 * b1 + a2 * b2
                plus_i = a1 * b2 - a2 * b1
                minus_r = a3 * b3 + a4 * b4
                minus_i = a3 * b4 - a4 * b3
                dcc = plus_r + minus_r
                dss = minus_r - plus_r
                dsc = plus_i + minus_i
                dcs = plus_i - minus_i
                if r == 0:
                    (ac, asn, ae, aes), (bc, bsn, be, bes) = sides
                    dcc = jnp.where(top16, 2.0 * (ac * bc + asn * bsn), dcc)
                    dcs = jnp.where(top16, 2.0 * (ac * bsn - asn * bc), dcs)
                    dsc = jnp.where(top16, 2.0 * (ae * be + aes * bes), dsc)
                    dss = jnp.where(top16, 2.0 * (ae * bes - aes * be), dss)
                cross[buf, shift + r : shift + r + 16, lane : lane + 128] = dsc.astype(jnp.bfloat16)
                cross[buf, shift + r : shift + r + 16, 256 + lane : 384 + lane] = dss.astype(jnp.bfloat16)
                cross[buf, shift + HALF + r : shift + HALF + r + 16, lane : lane + 128] = dcc.astype(jnp.bfloat16)
                cross[buf, shift + HALF + r : shift + HALF + r + 16, 256 + lane : 384 + lane] = dcs.astype(jnp.bfloat16)
                near = dcc * dcc + dsc * dsc
                far = dcs * dcs + dss * dss
                if r == 0:
                    near = jnp.where(top16, 0.5 * near, near)
                    far = jnp.where(top16, 0.5 * far, far)
                low = near[:8] + near[8:] if low is None else low + (near[:8] + near[8:])
                high = far[:8] + far[8:] if high is None else high + (far[:8] + far[8:])
            totals.append((low, high))
        total = jnp.concatenate([totals[0][0], totals[1][0], totals[0][1], totals[1][1]], axis=1)
        raw[n, pl.ds(2 * q + parity, 1), 768:1280] = jnp.sum(total, axis=0, keepdims=True)

    def flows(pair, buf):
        n, q = step_of(pair)
        flow_cols[buf] = dot(cross[buf, :, 256:512], mix_cols[...])
        for parity in range(2):
            rows = slice(ROWS * parity, ROWS * parity + ROWS)
            flow_rows[buf, parity] = dot(mix_rows[...], cross[buf, rows, :])
            end = lax.dot_general(
                sign_cols[...], cross[buf, rows, 0:256], (((1,), (1,)), ((), ())), preferred_element_type=jnp.float32
            )[:8]
            end = jnp.sum(end * end * end_weight, axis=1, keepdims=True)
            raw_end[n] = jnp.where(lane128 == 2 * q + parity, end, raw_end[n])

    def flow_sums(pair, buf, parity):
        n, q = step_of(pair)
        shift = ROWS * parity
        where = pl.ds(2 * q + parity, 1)
        cosines = cross[buf, shift + HALF : shift + ROWS, :].astype(jnp.float32).reshape(10, 8, 512)
        mixed = flow_rows[buf, parity].reshape(11, 8, 512)
        flow_y = cosines[0] * mixed[0]
        for t in range(1, 10):
            flow_y = flow_y + cosines[t] * mixed[t]
        last = cross[buf, shift : shift + 16, :].astype(jnp.float32)[:1]
        end = last * mixed[10, 0:1] - 8.0 * mixed[10, 1:2] * mixed[10, 1:2]
        raw[n, where, 0:512] = jnp.sum(flow_y, axis=0, keepdims=True) + end
        cosines = cross[buf, shift : shift + ROWS, 0:256].astype(jnp.float32).reshape(20, 8, 256)
        mixed = flow_cols[buf, shift : shift + ROWS].reshape(20, 8, 256)
        flow_x = (cosines[0] * mixed[0] + cosines[10] * mixed[10]) * top_half
        for t in range(1, 20):
            if t != 10:
                flow_x = flow_x + cosines[t] * mixed[t]
        raw[n, where, 512:768] = jnp.sum(flow_x, axis=0, keepdims=True)

    def body(t, buf, stages):
        if 3 in stages:
            for parity in range(2):
                flow_sums(t - 3, 1 - buf, parity)
        if 2 in stages:
            flows(t - 2, buf)
        if 1 in stages:
            for parity in range(2):
                products(t - 1, 1 - buf, parity)
        if 0 in stages:
            spectra(t, buf)

    def some(t):
        body(t, t % 2, [k for k in range(4) if 0 <= t - k < pairs])

    begin = 3 + (pairs - 3) % 2
    for t in range(begin):
        some(t)

    def step(k, carry):
        body(begin + 2 * k, begin % 2, range(4))
        body(begin + 2 * k + 1, 1 - begin % 2, range(4))
        return carry

    lax.fori_loop(0, (pairs - begin) // 2, step, 0)
    for t in range(pairs, pairs + 3):
        some(t)


def finish(raw, raw_end, cells, select, window, groups):
    window = window[...].astype(jnp.float32)
    scale = (1.0 / (PATCH * PATCH)) / (
        window_means(cells, 0, window, groups) * window_means(cells, 1, window, groups)
    )
    sums = dot_exact(raw[...].reshape(WIN * 16, 1280), select[...].astype(jnp.float32)).reshape(WIN, 16, 128)
    pad = jnp.zeros((120, 128), jnp.float32)
    ends = [
        pltpu.roll(jnp.concatenate([raw_end[n], pad], axis=0).T[:16], 32, axis=1) for n in range(WIN)
    ]
    total = spread_groups([sums[n] + ends[n] for n in range(WIN)], groups)
    unit = (2.0 / (PATCH * PATCH)) ** 2 * HALF / (PATCH * PATCH)
    total = total * (scale * unit)
    lane_all = lax.broadcasted_iota(jnp.int32, (16, 128), 1)
    weight = jnp.where(lane_all >= 64, total * HALF, 0.0)
    down = 1.0 + weight + pltpu.roll(weight, 96, axis=1) + pltpu.roll(weight, 64, axis=1)
    return jnp.where(lane_all >= 64, weight, total) / down


def clear_sums(raw, raw_end):
    raw[:, 12:16, :] = jnp.zeros((WIN, 4, 1280), jnp.float32)
    raw_end[...] = jnp.zeros((WIN, 8, 128), jnp.float32)


def early_step(pair):
    return pair // 4, 1 + pair % 4


def edge_step(pair):
    return pair // 6, pair % 6


def late_step(pair):
    return pair // 2, 5 * (pair % 2)


def early_kernel(
    form, first, second, mix_rows, mix_cols, sign_cols, select, window, out, grp, fa, fb, cells, raw, raw_end, *work
):
    lo, hi = INNER_LO - TOP, INNER_HI - TOP
    clear_sums(raw, raw_end)
    raw[:, 0:2, :] = jnp.zeros((WIN, 2, 1280), jnp.float32)
    raw[:, 10:12, :] = jnp.zeros((WIN, 2, 1280), jnp.float32)
    for sec, dst in ((0, fa), (1, fb)):
        cells[sec] = jnp.zeros((24, 256 * WIN), jnp.float32)
        for n, g in enumerate(INNER_GROUPS):
            pixels = group_pixels(lambda c: form[c - 1, sec, lo:hi, :], sec, g)
            grp[sec, n] = pixels
            dst[n] = dot(pixels, first[...]).astype(jnp.bfloat16)
            cell_squares(grp, sec, n, cells, 2, 13, INNER_LO)
    run_steps(
        early_step, 12, INNER_LO, fa, fb, second, mix_rows, mix_cols, sign_cols, raw, raw_end, work
    )
    out[...] = finish(raw, raw_end, cells, select, window, INNER_GROUPS)


def mesh_fields(result, valid):
    row = lax.broadcasted_iota(jnp.int32, (16, 128), 0)
    lane = lax.broadcasted_iota(jnp.int32, (16, 128), 1)
    column = lane % 32
    inside = (row < 12) & (lane < 96) & (column >= SWEEPS) & (column < SWEEPS + 16)
    flags = jnp.concatenate([valid[...].astype(jnp.float32), jnp.zeros((12, 112), jnp.float32)], axis=1)
    flags = jnp.concatenate([flags, jnp.zeros((4, 128), jnp.float32)], axis=0)
    flags = sum(pltpu.roll(flags, SWEEPS + 32 * kind, axis=1) for kind in range(3))
    fields = flags * pltpu.roll(jnp.where(row < 12, result, 0.0), SWEEPS, axis=1)
    fields = fields + jnp.where(lane >= 64, 4.0 * stiffness, 0.0)
    return jnp.where(inside, fields, 0.0), column


def edge_kernel(
    form, top, bottom, left, right, valid, first, second, mix_rows, mix_cols, sign_cols, select, window,
    out, to_right, to_left, frame, grp, fa, fb, cells, raw, raw_end, *work,
):
    clear_sums(raw, raw_end)
    for sec, dst in ((0, fa), (1, fb)):
        frame[sec, 0] = left[sec]
        frame[sec, 9] = right[sec]
        for c in (1, 2, 3, 6, 7, 8):
            frame_column(form, top, bottom, frame, sec, c, FRAME_H, FRAME_H)
        for n, g in enumerate(EDGE_GROUPS):
            pixels = group_pixels(lambda c: frame[sec, c], sec, g)
            grp[sec, n] = pixels
            dst[n] = dot(pixels, first[...]).astype(jnp.bfloat16)
            cell_squares(grp, sec, n, cells, 0, 15, 0)
        cells[sec, 15:24, :] = jnp.zeros((9, 256 * WIN), jnp.float32)
    run_steps(edge_step, 18, 0, fa, fb, second, mix_rows, mix_cols, sign_cols, raw, raw_end, work)
    result = finish(raw, raw_end, cells, select, window, EDGE_GROUPS)
    out[...] = result
    fields, column = mesh_fields(result, valid)
    last = jnp.where((column >= 16) & (column < 16 + SWEEPS), fields, 0.0)
    to_right[...] = pltpu.roll(last, 112, axis=1)
    head = jnp.where((column >= SWEEPS) & (column < 2 * SWEEPS), fields, 0.0)
    to_left[...] = pltpu.roll(head, 16, axis=1)


def late_kernel(
    form, top, bottom, early, edge, valid, first, second, mix_rows, mix_cols, sign_cols, select, window,
    out, fields, frame, grp, fa, fb, cells, raw, raw_end, *work,
):
    upper, lower = 208, 400
    clear_sums(raw, raw_end)
    raw[:, 2:10, :] = jnp.zeros((WIN, 8, 1280), jnp.float32)
    for sec, dst in ((0, fa), (1, fb)):
        cells[sec] = jnp.zeros((24, 256 * WIN), jnp.float32)
        for c in range(1, 8):
            frame_column(form, top, bottom, frame, sec, c, upper, lower)
        for n, g in enumerate(INNER_GROUPS):
            for lo, hi in ((0, upper), (lower, FRAME_H)):
                pixels = group_pixels(lambda c: frame[sec, c, lo:hi, :], sec, g)
                grp[sec, n, lo:hi, :] = pixels
                dst[n, lo:hi, :] = dot(pixels, first[...]).astype(jnp.bfloat16)
            cell_squares(grp, sec, n, cells, 0, 5, 0)
            cell_squares(grp, sec, n, cells, 10, 15, 0)
    run_steps(late_step, 6, 0, fa, fb, second, mix_rows, mix_cols, sign_cols, raw, raw_end, work)
    row = lax.broadcasted_iota(jnp.int32, (16, 128), 0)
    lane = lax.broadcasted_iota(jnp.int32, (16, 128), 1) % 32
    own = finish(raw, raw_end, cells, select, window, INNER_GROUPS)
    own = jnp.where((row >= 2) & (row < 10), early[...], own)
    result = jnp.where((lane >= 3) & (lane < 12), own, edge[...])
    out[...] = result
    fields[...] = mesh_fields(result, valid)[0]


def relax_kernel(result, fields, above, beneath, flow, mesh_out):
    frame = jnp.concatenate(
        [above[...][1:4], fields[...][:12], beneath[...][:SWEEPS], jnp.zeros((6, 128), jnp.float32)],
        axis=0,
    )
    lane = lax.broadcasted_iota(jnp.int32, (24, 128), 1)
    below = jnp.where(lane < 32, pltpu.roll(frame, 64, axis=1), pltpu.roll(frame, 96, axis=1))
    inside = (below > 0.0) & (lane < 64)
    rest = jnp.where(inside, 1.0 / jnp.where(inside, below, 1.0), 0.0)
    mesh = jnp.where(lane < 64, frame, 0.0)
    pull = mesh * jnp.where(inside, below - 4.0 * stiffness, 0.0)
    for _ in range(SWEEPS):
        around = (
            pltpu.roll(mesh, 1, axis=0)
            + pltpu.roll(mesh, 23, axis=0)
            + pltpu.roll(mesh, 1, axis=1)
            + pltpu.roll(mesh, 127, axis=1)
        )
        mesh = (pull + stiffness * around) * rest
    for kind in range(2):
        flow[kind] = result[0:12, 32 * kind : 32 * kind + 16]
        mesh_out[kind] = mesh[SWEEPS : SWEEPS + 12, 32 * kind + SWEEPS : 32 * kind + SWEEPS + 16]


def work_shapes():
    return [
        pltpu.VMEM((2, 2, 2 * ROWS, 512), jnp.float32),
        pltpu.VMEM((2, 2 * ROWS, 512), jnp.bfloat16),
        pltpu.VMEM((2, 2, HALF + 8, 512), jnp.float32),
        pltpu.VMEM((2, 2 * ROWS, 256), jnp.float32),
    ]


SUM_SHAPES = (
    ((2, 24, 256 * WIN), jnp.float32),
    ((WIN, 16, 1280), jnp.float32),
    ((WIN, 8, 128), jnp.float32),
)


def sum_shapes(make):
    return [make(*shape) for shape in SUM_SHAPES]


def grow_params(mib):
    return pltpu.CompilerParams(vmem_limit_bytes=mib << 20)


def frame_shapes():
    return [
        pltpu.VMEM((2, 10, FRAME_H, 128), jnp.bfloat16),
        pltpu.VMEM((2, WIN, FRAME_H, 256), jnp.bfloat16),
        pltpu.VMEM((WIN, FRAME_H, 512), jnp.bfloat16),
        pltpu.VMEM((WIN, FRAME_H, 512), jnp.bfloat16),
        *sum_shapes(pltpu.VMEM),
        *work_shapes(),
    ]


SMALL = jax.ShapeDtypeStruct((16, 128), jnp.float32)


def correlate_early(form, consts):
    height = INNER_HI - INNER_LO
    return pl.pallas_call(
        early_kernel,
        out_shape=SMALL,
        in_specs=[VMEM_SPEC] * 8,
        out_specs=VMEM_SPEC,
        scratch_shapes=[
            pltpu.VMEM((2, WIN, height, 256), jnp.bfloat16),
            pltpu.VMEM((WIN, height, 512), jnp.bfloat16),
            pltpu.VMEM((WIN, height, 512), jnp.bfloat16),
            *sum_shapes(pltpu.VMEM),
            *work_shapes(),
        ],
        compiler_params=grow_params(20),
    )(form, *consts)


def correlate_edge(form, top, bottom, left, right, valid, consts):
    return pl.pallas_call(
        edge_kernel,
        out_shape=(SMALL,) * 3,
        in_specs=[VMEM_SPEC] * 13,
        out_specs=(VMEM_SPEC,) * 3,
        scratch_shapes=frame_shapes(),
        compiler_params=grow_params(24),
    )(form, top, bottom, left, right, valid, *consts)


def correlate_late(form, top, bottom, early, edge, valid, consts):
    return pl.pallas_call(
        late_kernel,
        out_shape=(SMALL,) * 2,
        in_specs=[VMEM_SPEC] * 13,
        out_specs=(VMEM_SPEC,) * 2,
        scratch_shapes=frame_shapes(),
        compiler_params=grow_params(24),
    )(form, top, bottom, early, edge, valid, *consts)


def relax(result, fields, above, beneath):
    field = jax.ShapeDtypeStruct((2, 12, 16), jnp.float32)
    return pl.pallas_call(
        relax_kernel,
        out_shape=(field, field),
        in_specs=[VMEM_SPEC] * 4,
        out_specs=(VMEM_SPEC,) * 2,
        compiler_params=grow_params(8),
    )(result, fields, above, beneath)


def pack_kernel(*refs):
    sources, out, rows, held, arrived = refs[:6], refs[6], refs[7], refs[8:14], refs[14]
    copies = [pltpu.make_async_copy(src, dst, arrived.at[n]) for n, (src, dst) in enumerate(zip(sources, held))]
    for copy in copies:
        copy.start()
    for copy in copies:
        copy.wait()
    a_tiles, b_tiles, a_owner, b_owner, a_offset, b_offset = held
    count = a_tiles.shape[0]
    owners = jnp.concatenate([a_owner[...], b_owner[...]], axis=1)
    slot = lax.broadcasted_iota(jnp.int32, (128, 2 * count), 0)
    select = jnp.where(slot == owners, 1.0, 0.0).astype(jnp.bfloat16)
    zero = lambda width: jnp.zeros((count, width), jnp.bfloat16)

    def position(offset):
        row = offset[0:1, :].astype(jnp.float32)
        col = offset[1:2, :].astype(jnp.float32)
        code = jnp.floor(row * (TX / TILE_H) + col * (1.0 / TILE_W) + 1.5)
        code = jnp.concatenate([code, jnp.zeros((1, 128 - count), jnp.float32)], axis=1)
        return jnp.broadcast_to(code, (128, 128)).T[:count]

    def piece(tiles, start, width):
        return tiles[:, start : start + width]

    lane = lax.broadcasted_iota(jnp.int32, (count, 128), 1)
    code_a = jnp.where(lane == 64, position(a_offset), 0.0).astype(jnp.bfloat16)
    code_b = jnp.where(lane == 96, position(b_offset), 0.0).astype(jnp.bfloat16)

    def send_row(y):
        if y < TILE_H:
            a_part = jnp.concatenate([piece(a_tiles, TILE_W * y, TILE_W), zero(SPLIT)], axis=1)
            b_part = jnp.concatenate([zero(TILE_W), piece(b_tiles, TILE_W * y, SPLIT)], axis=1)
        elif y < TILE_H + 8:
            u = y - TILE_H
            a_part = zero(128)
            b_part = jnp.concatenate(
                [piece(b_tiles, TILE_W * (8 * k + u) + SPLIT, LANES) for k in range(4)], axis=1
            )
        else:
            u = y - TILE_H - 8
            a_part = code_a
            b_part = jnp.concatenate(
                [piece(b_tiles, TILE_W * (32 + u) + SPLIT, LANES), zero(96)], axis=1
            )
            b_part = b_part + code_b
        return jnp.concatenate([a_part, b_part], axis=0)

    for y in range(0, SLOT_H, 2):
        both = jnp.concatenate([send_row(y), send_row(y + 1)], axis=1)
        sent = dot(select, both)
        rows[pl.ds(y, 128, stride=SLOT_H), :] = sent[:, :128]
        rows[pl.ds(y + 1, 128, stride=SLOT_H), :] = sent[:, 128:]

    def flush(n, carry):
        start = pl.multiple_of(8 * SLOT_H * n, 8)
        block = rows[pl.ds(start, 8 * SLOT_H), :].reshape(8, SLOT_H, 128)
        out[pl.ds(8 * n, 8)] = block.astype(jnp.bfloat16)
        return carry

    lax.fori_loop(0, 16, flush, 0)


def place_kernel(got, form, up, down, low, high, rows, plane_a, plane_b):
    def widen(n, carry):
        start = pl.multiple_of(8 * SLOT_H * n, 8)
        block = got[pl.ds(8 * n, 8)].astype(jnp.float32)
        rows[pl.ds(start, 8 * SLOT_H), :] = block.reshape(8 * SLOT_H, 128)
        return carry

    lax.fori_loop(0, 16, widen, 0)
    codes = rows[pl.ds(TILE_H + 8, 128, stride=SLOT_H), :]
    wanted = lax.broadcasted_iota(jnp.int32, (128, 128), 1).astype(jnp.float32) + 1.0
    pick = lambda col: jnp.where(codes[:, col : col + 1] == wanted, 1.0, 0.0).T[:96]
    select_a = pick(64)
    select_b = pick(96)
    select = jnp.concatenate([select_a, select_b], axis=0).astype(jnp.bfloat16)
    select_b = select_b.astype(jnp.bfloat16)

    def slot_row(y):
        return rows[pl.ds(y, 128, stride=SLOT_H), :].astype(jnp.bfloat16)

    for plane in (plane_a, plane_b):
        for t in range(TX):
            plane[FORM_H * t : FORM_H * t + 8, :] = jnp.zeros((8, 128), jnp.float32)
            plane[FORM_H * t + 480 : FORM_H * t + 488, :] = jnp.zeros((8, 128), jnp.float32)
    lane = lax.broadcasted_iota(jnp.int32, (96, 128), 1)
    tail = lane < LANES

    for u in range(0, 8, 2):
        tails = jnp.concatenate([slot_row(TILE_H + u + v + w) for v in range(2) for w in (0, 8)], axis=1)
        tails = dot(select_b, tails)
        for k in range(5):
            y = 8 * k + u
            main = dot(select, jnp.concatenate([slot_row(y), slot_row(y + 1)], axis=1))
            for v in range(2):
                part_a = main[:96, 128 * v : 128 * v + 128]
                part_b = main[96:, 128 * v : 128 * v + 128]
                rest = tails[:, 256 * v : 256 * v + 128] if k < 4 else tails[:, 256 * v + 128 : 256 * v + 256]
                if 0 < k < 4:
                    rest = pltpu.roll(rest, 128 - LANES * k, axis=1)
                part_b = jnp.where(tail, rest, part_b)
                for ty in range(TY):
                    where = pl.ds(TILE_H * ty + y + v + 4, TX, stride=FORM_H)
                    plane_a[where, :] = part_a[TX * ty : TX * ty + TX]
                    plane_b[where, :] = part_b[TX * ty : TX * ty + TX]

    for sec, plane in ((0, plane_a), (1, plane_b)):
        for t in range(TX):
            block = plane[FORM_H * t : FORM_H * t + FORM_H, :].astype(jnp.bfloat16)
            form[t, sec] = block
            for side, at in ((low, 0), (high, TX - 1)):
                if t == at:
                    side[sec, 0:TOP, :] = jnp.zeros((TOP, 128), jnp.bfloat16)
                    side[sec, TOP : TOP + FORM_H, :] = block
                    side[sec, TOP + FORM_H :, :] = jnp.zeros((FRAME_H - TOP - FORM_H, 128), jnp.bfloat16)
            up[t, sec] = plane[FORM_H * t : FORM_H * t + EDGE_H, :].astype(jnp.bfloat16)
            down[t, sec] = plane[FORM_H * t + 424 : FORM_H * t + 488, :].astype(jnp.bfloat16)


def pack(*arrays):
    return pl.pallas_call(
        pack_kernel,
        out_shape=jax.ShapeDtypeStruct((128, SLOT_H, 128), jnp.bfloat16),
        in_specs=[pl.BlockSpec(memory_space=pltpu.HBM)] * 6,
        out_specs=VMEM_SPEC,
        scratch_shapes=[
            pltpu.VMEM((128 * SLOT_H, 128), jnp.float32),
            *[pltpu.VMEM(x.shape, x.dtype) for x in arrays],
            pltpu.SemaphoreType.DMA((6,)),
        ],
        compiler_params=pltpu.CompilerParams(vmem_limit_bytes=60 << 20),
    )(*arrays)


def place(got):
    edge = jax.ShapeDtypeStruct((TX, 2, EDGE_H, 128), jnp.bfloat16)
    side = jax.ShapeDtypeStruct((2, FRAME_H, 128), jnp.bfloat16)
    return pl.pallas_call(
        place_kernel,
        out_shape=(jax.ShapeDtypeStruct((TX, 2, FORM_H, 128), jnp.bfloat16), edge, edge, side, side),
        scratch_shapes=[
            pltpu.VMEM((128 * SLOT_H, 128), jnp.float32),
            pltpu.VMEM((TX * FORM_H, 128), jnp.float32),
            pltpu.VMEM((TX * FORM_H, 128), jnp.float32),
        ],
        in_specs=[VMEM_SPEC],
        out_specs=(VMEM_SPEC,) * 5,
        compiler_params=pltpu.CompilerParams(vmem_limit_bytes=24 << 20),
    )(got)


def shifted(block, axis, step):
    count = lax.axis_size(axis)
    pairs = [(i, i + step) for i in range(count) if 0 <= i + step < count]
    return lax.ppermute(block, axis, pairs)


def column(side, top, bottom, t):
    grow = lambda x, low, high: jnp.pad(x[t], ((0, 0), (low, high), (0, 0)))
    return side + grow(top, 0, FRAME_H - EDGE_H) + grow(bottom, 536, FRAME_H - 536 - EDGE_H)


def per_device(a_tiles, a_owner, a_offset, b_tiles, b_owner, b_offset, patch_valid):
    packed = pack(a_tiles, b_tiles, a_owner[None], b_owner[None], a_offset.T, b_offset.T)
    got = lax.all_to_all(packed, ("row", "col"), split_axis=0, concat_axis=0, tiled=True)
    form, up, down, low, high = place(got)
    consts = tables()
    top = shifted(down, "row", 1)
    bottom = shifted(up, "row", -1)
    early = correlate_early(form, consts)
    left = shifted(column(high, top, bottom, TX - 1), "col", 1)
    right = shifted(column(low, top, bottom, 0), "col", -1)
    edge, to_right, to_left = correlate_edge(form, top, bottom, left, right, patch_valid, consts)
    from_left = shifted(to_right, "col", 1)
    from_right = shifted(to_left, "col", -1)
    result, fields = correlate_late(form, top, bottom, early, edge, patch_valid, consts)
    fields = fields + from_left + from_right
    above = shifted(fields[8:16], "row", 1)
    beneath = shifted(fields[0:8], "row", -1)
    return relax(result, fields, above, beneath)


def solution(mesh):
    in_specs = (
        P(("row", "col"), None),
        P(("row", "col")),
        P(("row", "col"), None),
        P(("row", "col"), None),
        P(("row", "col")),
        P(("row", "col"), None),
        P("row", "col"),
    )
    out_specs = (P(None, "row", "col"), P(None, "row", "col"))
    return jax.shard_map(
        per_device, mesh=mesh, in_specs=in_specs, out_specs=out_specs, check_vma=False
    )
```

```python
import math

import jax
import jax.numpy as jnp
import numpy as np
from jax import lax
from jax.experimental import pallas as pl
from jax.experimental.pallas import tpu as pltpu
from jax.sharding import PartitionSpec as P

PATCH = 160
STRIDE = 40
TY = 12
TX = 8
SWEEPS = 3
HALF = PATCH // 2
FREQ = HALF + 1
WIN = 3
GROUPS = 6
ROWS = PATCH
PAIR_H = 208
TILE_H = 40
TILE_W = 80
SPLIT = 128 - TILE_W
LANES = 32
SLOT_H = 56
FRAME_H = 608
FORM_H = 488
EDGE_H = 64
TOP = 56

VMEM_SPEC = pl.BlockSpec(memory_space=pltpu.VMEM)

stiffness = 1.0
tiny = 1e-06


def trig():
    k = np.arange(FREQ)
    n = np.arange(PATCH)
    phase = (k[:, None] * n[None, :] % PATCH).astype(np.float64) * (2.0 * math.pi / PATCH)
    cosine, sine = np.cos(phase), np.sin(phase)
    sine[0] = 0.0
    sine[HALF] = 0.0
    return cosine, sine


def tables():
    cosine, sine = trig()
    first = np.zeros((256, 512))
    for w in range(WIN):
        rows = slice(STRIDE * w, STRIDE * w + PATCH)
        first[rows, FREQ * w : FREQ * (w + 1)] = cosine.T
        first[rows, 256 + FREQ * w : 256 + FREQ * (w + 1)] = sine.T
    mixed = np.concatenate([cosine[HALF:], sine[1:HALF], cosine[:HALF]])
    second = np.zeros((2, ROWS, PAIR_H))
    for parity in range(2):
        second[parity, :, STRIDE * parity : STRIDE * parity + PATCH] = mixed
    second = second.reshape(2 * ROWS, PAIR_H)
    half = np.ones((FREQ, 1))
    half[0] = half[HALF] = 0.5
    shift = np.where(np.arange(PATCH) < HALF, np.arange(PATCH), np.arange(PATCH) - PATCH) * (16.0 / PATCH)
    shift[HALF] = 0.0
    rounded = lambda x: x.astype(jnp.bfloat16).astype(np.float64)
    mix = 2.0 * half * ((rounded(cosine) * shift) @ rounded(sine).T)
    sign = half[:, 0] * cosine[:, HALF]
    mix_rows = np.zeros((HALF + 8, ROWS))
    mix_rows[:FREQ, 1:HALF] = mix[:, 1:HALF]
    mix_rows[FREQ, HALF:] = sign[:HALF]
    mix_rows[FREQ, 0] = sign[HALF]
    mix_cols = np.zeros((256, 256))
    sign_cols = np.zeros((16, 256))
    for w in range(WIN):
        mix_cols[FREQ * w : FREQ * (w + 1), FREQ * w : FREQ * (w + 1)] = mix.T
        sign_cols[w, FREQ * w : FREQ * (w + 1)] = sign
    select = np.zeros((1280, 128))
    for w in range(WIN):
        lanes = np.arange(FREQ) + FREQ * w
        select[lanes, w] = half[:, 0]
        select[256 + lanes, w] = 1.0
        select[512 + lanes, 32 + w] = 1.0
        select[768 + lanes, 64 + w] = half[:, 0]
        select[1024 + lanes, 64 + w] = 1.0
    window = np.zeros((256, 128))
    for w in range(WIN):
        for kind in range(3):
            window[STRIDE * w : STRIDE * w + PATCH, 32 * kind + w] = 1.0
    as_bf16 = lambda x: jnp.asarray(x.astype(jnp.bfloat16))
    return tuple(as_bf16(x) for x in (first, second, mix_rows, mix_cols, sign_cols, select, window))


def dot(a, b):
    return lax.dot_general(a, b, (((1,), (0,)), ((), ())), preferred_element_type=jnp.float32)


def dot_exact(a, b):
    return lax.dot_general(
        a,
        b,
        (((1,), (0,)), ((), ())),
        preferred_element_type=jnp.float32,
        precision=lax.Precision.HIGHEST,
    )


EDGE_GROUPS = (0, 4, 5)
INNER_GROUPS = (1, 2, 3)
INNER_LO = 64
INNER_HI = 528


def spread_groups(sums, groups):
    lane = lax.broadcasted_iota(jnp.int32, (16, 128), 1) % 32
    total = jnp.zeros((16, 128), jnp.float32)
    for piece, g in zip(sums, groups):
        piece = piece if g < GROUPS - 1 else jnp.where(lane == 0, piece, 0.0)
        total = total + (pltpu.roll(piece, WIN * g, axis=1) if g else piece)
    return total


def cell_squares(grp, sec, n, cells, lo, hi, base):
    for c in range(lo, hi):
        at = STRIDE * c - base
        near = at // 16 * 16
        values = grp[sec, n, near : near + 48, :].astype(jnp.float32)[at - near : at - near + STRIDE]
        squares = (values * values).reshape(5, 8, 256).sum(axis=0)
        cells[sec, c : c + 1, 256 * n : 256 * n + 256] = jnp.sum(squares, axis=0, keepdims=True)


def window_means(cells, sec, window, groups):
    sums = cells[sec, 0:16, :] + cells[sec, 1:17, :] + cells[sec, 2:18, :] + cells[sec, 3:19, :]
    stacked = jnp.concatenate([sums[:, 256 * n : 256 * n + 256] for n in range(WIN)], axis=0)
    total = dot_exact(stacked, window).reshape(WIN, 16, 128)
    return spread_groups([total[n] for n in range(WIN)], groups) / (PATCH * PATCH) + tiny


def group_pixels(tile, sec, g):
    c = 3 * (g // 2) + g % 2
    offset = 20 + 40 * (g % 2)
    pieces = []
    left = 240
    while left > 0 and c < 10:
        values = tile(c)
        width = min(TILE_W - offset, left)
        if sec == 0:
            pieces.append(values[:, offset : offset + width])
        else:
            if offset < SPLIT:
                pieces.append(values[:, TILE_W + offset : TILE_W + min(SPLIT, offset + width)])
            if offset + width > SPLIT:
                pieces.append(values[:, max(0, offset - SPLIT) : offset + width - SPLIT])
        left -= width
        offset = 0
        c += 1
    rows = pieces[0].shape[0]
    pieces.append(jnp.zeros((rows, 256 - 240 + left), pieces[0].dtype))
    return jnp.concatenate(pieces, axis=1)


def frame_column(form, top, bottom, frame, sec, c, upper, lower):
    t = c - 1
    if upper == lower:
        frame[sec, c, TOP : TOP + FORM_H, :] = form[t, sec]
    else:
        frame[sec, c, TOP:upper, :] = form[t, sec, 0 : upper - TOP, :]
        frame[sec, c, lower : TOP + FORM_H, :] = form[t, sec, lower - TOP :, :]
    frame[sec, c, 0:TOP, :] = top[t, sec, 0:TOP, :]
    frame[sec, c, 544:600, :] = bottom[t, sec, 8:EDGE_H, :]
    frame[sec, c, 600:608, :] = jnp.zeros((8, 128), jnp.bfloat16)
    for dst, own, other in (
        (TOP, form[t, sec, 0:8, :], top[t, sec, TOP:EDGE_H, :]),
        (536, form[t, sec, 480:488, :], bottom[t, sec, 0:8, :]),
    ):
        both = own.astype(jnp.float32) + other.astype(jnp.float32)
        frame[sec, c, dst : dst + 8, :] = both.astype(jnp.bfloat16)


def run_steps(step_of, pairs, base, fa, fb, second, mix_rows, mix_cols, sign_cols, raw, raw_end, work):
    spec, cross, flow_rows, flow_cols = work
    sub = lax.broadcasted_iota(jnp.int32, (8, 256), 0)
    top = sub == 0
    top_half = jnp.where(top, 0.5, 1.0)
    lane128 = lax.broadcasted_iota(jnp.int32, (8, 128), 1)
    k_lane = lax.broadcasted_iota(jnp.int32, (8, ROWS), 1)
    end_weight = jnp.where((k_lane == 0) | (k_lane == HALF), -4.0, -8.0)

    def spectra(pair, buf):
        n, q = step_of(pair)
        start = 80 * q - base
        if not isinstance(start, int):
            start = pl.multiple_of(start, 16)
        for sec, src in ((0, fa), (1, fb)):
            spec[buf, sec] = dot(second[...], src[n, pl.ds(start, PAIR_H), :])

    def products(pair, buf, parity):
        n, q = step_of(pair)
        shift = ROWS * parity
        totals = []
        top16 = lax.broadcasted_iota(jnp.int32, (16, 128), 0) == 0
        for lane in (0, 128):
            low = high = None
            for r in range(0, HALF, 16):
                sides = [
                    [
                        spec[buf, sec, shift + at + r : shift + at + r + 16, lo + lane : lo + lane + 128]
                        for at in (HALF, 0)
                        for lo in (0, 256)
                    ]
                    for sec in range(2)
                ]
                (a1, a2, a3, a4), (b1, b2, b3, b4) = [
                    (cc - ss, sc + cs, cc + ss, sc - cs) for cc, cs, sc, ss in sides
                ]
                plus_r = a1 * b1 + a2 * b2
                plus_i = a1 * b2 - a2 * b1
                minus_r = a3 * b3 + a4 * b4
                minus_i = a3 * b4 - a4 * b3
                dcc = plus_r + minus_r
                dss = minus_r - plus_r
                dsc = plus_i + minus_i
                dcs = plus_i - minus_i
                if r == 0:
                    (ac, asn, ae, aes), (bc, bsn, be, bes) = sides
                    dcc = jnp.where(top16, 2.0 * (ac * bc + asn * bsn), dcc)
                    dcs = jnp.where(top16, 2.0 * (ac * bsn - asn * bc), dcs)
                    dsc = jnp.where(top16, 2.0 * (ae * be + aes * bes), dsc)
                    dss = jnp.where(top16, 2.0 * (ae * bes - aes * be), dss)
                cross[buf, shift + r : shift + r + 16, lane : lane + 128] = dsc.astype(jnp.bfloat16)
                cross[buf, shift + r : shift + r + 16, 256 + lane : 384 + lane] = dss.astype(jnp.bfloat16)
                cross[buf, shift + HALF + r : shift + HALF + r + 16, lane : lane + 128] = dcc.astype(jnp.bfloat16)
                cross[buf, shift + HALF + r : shift + HALF + r + 16, 256 + lane : 384 + lane] = dcs.astype(jnp.bfloat16)
                near = dcc * dcc + dsc * dsc
                far = dcs * dcs + dss * dss
                if r == 0:
                    near = jnp.where(top16, 0.5 * near, near)
                    far = jnp.where(top16, 0.5 * far, far)
                low = near[:8] + near[8:] if low is None else low + (near[:8] + near[8:])
                high = far[:8] + far[8:] if high is None else high + (far[:8] + far[8:])
            totals.append((low, high))
        total = jnp.concatenate([totals[0][0], totals[1][0], totals[0][1], totals[1][1]], axis=1)
        raw[n, pl.ds(2 * q + parity, 1), 768:1280] = jnp.sum(total, axis=0, keepdims=True)

    def flows(pair, buf):
        n, q = step_of(pair)
        flow_cols[buf] = dot(cross[buf, :, 256:512], mix_cols[...])
        for parity in range(2):
            rows = slice(ROWS * parity, ROWS * parity + ROWS)
            flow_rows[buf, parity] = dot(mix_rows[...], cross[buf, rows, :])
            end = lax.dot_general(
                sign_cols[...], cross[buf, rows, 0:256], (((1,), (1,)), ((), ())), preferred_element_type=jnp.float32
            )[:8]
            end = jnp.sum(end * end * end_weight, axis=1, keepdims=True)
            raw_end[n] = jnp.where(lane128 == 2 * q + parity, end, raw_end[n])

    def flow_sums(pair, buf, parity):
        n, q = step_of(pair)
        shift = ROWS * parity
        where = pl.ds(2 * q + parity, 1)
        cosines = cross[buf, shift + HALF : shift + ROWS, :].astype(jnp.float32).reshape(10, 8, 512)
        mixed = flow_rows[buf, parity].reshape(11, 8, 512)
        flow_y = cosines[0] * mixed[0]
        for t in range(1, 10):
            flow_y = flow_y + cosines[t] * mixed[t]
        last = cross[buf, shift : shift + 16, :].astype(jnp.float32)[:1]
        end = last * mixed[10, 0:1] - 8.0 * mixed[10, 1:2] * mixed[10, 1:2]
        raw[n, where, 0:512] = jnp.sum(flow_y, axis=0, keepdims=True) + end
        cosines = cross[buf, shift : shift + ROWS, 0:256].astype(jnp.float32).reshape(20, 8, 256)
        mixed = flow_cols[buf, shift : shift + ROWS].reshape(20, 8, 256)
        flow_x = (cosines[0] * mixed[0] + cosines[10] * mixed[10]) * top_half
        for t in range(1, 20):
            if t != 10:
                flow_x = flow_x + cosines[t] * mixed[t]
        raw[n, where, 512:768] = jnp.sum(flow_x, axis=0, keepdims=True)

    def body(t, buf, stages):
        if 3 in stages:
            for parity in range(2):
                flow_sums(t - 3, 1 - buf, parity)
        if 2 in stages:
            flows(t - 2, buf)
        if 1 in stages:
            for parity in range(2):
                products(t - 1, 1 - buf, parity)
        if 0 in stages:
            spectra(t, buf)

    def some(t):
        body(t, t % 2, [k for k in range(4) if 0 <= t - k < pairs])

    begin = 3 + (pairs - 3) % 2
    for t in range(begin):
        some(t)

    def step(k, carry):
        body(begin + 2 * k, begin % 2, range(4))
        body(begin + 2 * k + 1, 1 - begin % 2, range(4))
        return carry

    lax.fori_loop(0, (pairs - begin) // 2, step, 0)
    for t in range(pairs, pairs + 3):
        some(t)


def finish(raw, raw_end, cells, select, window, groups):
    window = window[...].astype(jnp.float32)
    scale = (1.0 / (PATCH * PATCH)) / (
        window_means(cells, 0, window, groups) * window_means(cells, 1, window, groups)
    )
    sums = dot_exact(raw[...].reshape(WIN * 16, 1280), select[...].astype(jnp.float32)).reshape(WIN, 16, 128)
    pad = jnp.zeros((120, 128), jnp.float32)
    ends = [
        pltpu.roll(jnp.concatenate([raw_end[n], pad], axis=0).T[:16], 32, axis=1) for n in range(WIN)
    ]
    total = spread_groups([sums[n] + ends[n] for n in range(WIN)], groups)
    unit = (2.0 / (PATCH * PATCH)) ** 2 * HALF / (PATCH * PATCH)
    total = total * (scale * unit)
    lane_all = lax.broadcasted_iota(jnp.int32, (16, 128), 1)
    weight = jnp.where(lane_all >= 64, total * HALF, 0.0)
    down = 1.0 + weight + pltpu.roll(weight, 96, axis=1) + pltpu.roll(weight, 64, axis=1)
    return jnp.where(lane_all >= 64, weight, total) / down


def clear_sums(raw, raw_end):
    raw[:, 12:16, :] = jnp.zeros((WIN, 4, 1280), jnp.float32)
    raw_end[...] = jnp.zeros((WIN, 8, 128), jnp.float32)


def early_step(pair):
    return pair // 4, 1 + pair % 4


def tail_step(pair):
    return 2, 1 + pair


def edge_step(pair):
    return pair // 6, pair % 6


def late_step(pair):
    return pair // 2, 5 * (pair % 2)


def inner_rows(
    members, step_of, pairs, form, first, second, mix_rows, mix_cols, sign_cols, select, window,
    grp, fa, fb, cells, raw, raw_end, *work,
):
    lo, hi = INNER_LO - TOP, INNER_HI - TOP
    raw[...] = jnp.zeros((WIN, 16, 1280), jnp.float32)
    raw_end[...] = jnp.zeros((WIN, 8, 128), jnp.float32)
    for sec, dst in ((0, fa), (1, fb)):
        cells[sec] = jnp.zeros((24, 256 * WIN), jnp.float32)
        for n in members:
            pixels = group_pixels(lambda c: form[c - 1, sec, lo:hi, :], sec, INNER_GROUPS[n])
            grp[sec, n] = pixels
            dst[n] = dot(pixels, first[...]).astype(jnp.bfloat16)
            cell_squares(grp, sec, n, cells, 2, 13, INNER_LO)
    run_steps(step_of, pairs, INNER_LO, fa, fb, second, mix_rows, mix_cols, sign_cols, raw, raw_end, work)
    return finish(raw, raw_end, cells, select, window, INNER_GROUPS)


def early_kernel(*refs):
    out = refs[8]
    out[...] = inner_rows((0, 1), early_step, 8, *refs[:8], *refs[9:])


def tail_kernel(early, late, edge, valid, *refs):
    out, fields = refs[8:10]
    row = lax.broadcasted_iota(jnp.int32, (16, 128), 0)
    lane = lax.broadcasted_iota(jnp.int32, (16, 128), 1) % 32
    own = inner_rows((2,), tail_step, 4, *refs[:8], *refs[10:])
    own = jnp.where(lane < 9, early[...], own)
    own = jnp.where((row >= 2) & (row < 10), own, late[...])
    result = jnp.where((lane >= 3) & (lane < 12), own, edge[...])
    out[...] = result
    fields[...] = mesh_fields(result, valid)[0]


def mesh_fields(result, valid):
    row = lax.broadcasted_iota(jnp.int32, (16, 128), 0)
    lane = lax.broadcasted_iota(jnp.int32, (16, 128), 1)
    column = lane % 32
    inside = (row < 12) & (lane < 96) & (column >= SWEEPS) & (column < SWEEPS + 16)
    flags = jnp.concatenate([valid[...].astype(jnp.float32), jnp.zeros((12, 112), jnp.float32)], axis=1)
    flags = jnp.concatenate([flags, jnp.zeros((4, 128), jnp.float32)], axis=0)
    flags = sum(pltpu.roll(flags, SWEEPS + 32 * kind, axis=1) for kind in range(3))
    fields = flags * pltpu.roll(jnp.where(row < 12, result, 0.0), SWEEPS, axis=1)
    fields = fields + jnp.where(lane >= 64, 4.0 * stiffness, 0.0)
    return jnp.where(inside, fields, 0.0), column


def edge_kernel(
    form, top, bottom, left, right, valid, first, second, mix_rows, mix_cols, sign_cols, select, window,
    out, to_right, to_left, frame, grp, fa, fb, cells, raw, raw_end, *work,
):
    clear_sums(raw, raw_end)
    for sec, dst in ((0, fa), (1, fb)):
        frame[sec, 0] = left[sec]
        frame[sec, 9] = right[sec]
        for c in (1, 2, 3, 6, 7, 8):
            frame_column(form, top, bottom, frame, sec, c, FRAME_H, FRAME_H)
        for n, g in enumerate(EDGE_GROUPS):
            pixels = group_pixels(lambda c: frame[sec, c], sec, g)
            grp[sec, n] = pixels
            dst[n] = dot(pixels, first[...]).astype(jnp.bfloat16)
            cell_squares(grp, sec, n, cells, 0, 15, 0)
        cells[sec, 15:24, :] = jnp.zeros((9, 256 * WIN), jnp.float32)
    run_steps(edge_step, 18, 0, fa, fb, second, mix_rows, mix_cols, sign_cols, raw, raw_end, work)
    result = finish(raw, raw_end, cells, select, window, EDGE_GROUPS)
    out[...] = result
    fields, column = mesh_fields(result, valid)
    last = jnp.where((column >= 16) & (column < 16 + SWEEPS), fields, 0.0)
    to_right[...] = pltpu.roll(last, 112, axis=1)
    head = jnp.where((column >= SWEEPS) & (column < 2 * SWEEPS), fields, 0.0)
    to_left[...] = pltpu.roll(head, 16, axis=1)


def late_kernel(
    form, top, bottom, first, second, mix_rows, mix_cols, sign_cols, select, window,
    out, frame, grp, fa, fb, cells, raw, raw_end, *work,
):
    upper, lower = 208, 400
    clear_sums(raw, raw_end)
    raw[:, 2:10, :] = jnp.zeros((WIN, 8, 1280), jnp.float32)
    for sec, dst in ((0, fa), (1, fb)):
        cells[sec] = jnp.zeros((24, 256 * WIN), jnp.float32)
        for c in range(1, 8):
            frame_column(form, top, bottom, frame, sec, c, upper, lower)
        for n, g in enumerate(INNER_GROUPS):
            for lo, hi in ((0, upper), (lower, FRAME_H)):
                pixels = group_pixels(lambda c: frame[sec, c, lo:hi, :], sec, g)
                grp[sec, n, lo:hi, :] = pixels
                dst[n, lo:hi, :] = dot(pixels, first[...]).astype(jnp.bfloat16)
            cell_squares(grp, sec, n, cells, 0, 5, 0)
            cell_squares(grp, sec, n, cells, 10, 15, 0)
    run_steps(late_step, 6, 0, fa, fb, second, mix_rows, mix_cols, sign_cols, raw, raw_end, work)
    out[...] = finish(raw, raw_end, cells, select, window, INNER_GROUPS)


def relax_kernel(result, fields, above, beneath, flow, mesh_out):
    frame = jnp.concatenate(
        [above[...][1:4], fields[...][:12], beneath[...][:SWEEPS], jnp.zeros((6, 128), jnp.float32)],
        axis=0,
    )
    lane = lax.broadcasted_iota(jnp.int32, (24, 128), 1)
    below = jnp.where(lane < 32, pltpu.roll(frame, 64, axis=1), pltpu.roll(frame, 96, axis=1))
    inside = (below > 0.0) & (lane < 64)
    rest = jnp.where(inside, 1.0 / jnp.where(inside, below, 1.0), 0.0)
    mesh = jnp.where(lane < 64, frame, 0.0)
    pull = mesh * jnp.where(inside, below - 4.0 * stiffness, 0.0)
    for _ in range(SWEEPS):
        around = (
            pltpu.roll(mesh, 1, axis=0)
            + pltpu.roll(mesh, 23, axis=0)
            + pltpu.roll(mesh, 1, axis=1)
            + pltpu.roll(mesh, 127, axis=1)
        )
        mesh = (pull + stiffness * around) * rest
    for kind in range(2):
        flow[:, kind, :] = result[0:12, 32 * kind : 32 * kind + 16]
        mesh_out[:, kind, :] = mesh[SWEEPS : SWEEPS + 12, 32 * kind + SWEEPS : 32 * kind + SWEEPS + 16]


def work_shapes():
    return [
        pltpu.VMEM((2, 2, 2 * ROWS, 512), jnp.float32),
        pltpu.VMEM((2, 2 * ROWS, 512), jnp.bfloat16),
        pltpu.VMEM((2, 2, HALF + 8, 512), jnp.float32),
        pltpu.VMEM((2, 2 * ROWS, 256), jnp.float32),
    ]


SUM_SHAPES = (
    ((2, 24, 256 * WIN), jnp.float32),
    ((WIN, 16, 1280), jnp.float32),
    ((WIN, 8, 128), jnp.float32),
)


def sum_shapes(make):
    return [make(*shape) for shape in SUM_SHAPES]


def grow_params(mib):
    return pltpu.CompilerParams(vmem_limit_bytes=mib << 20)


def frame_shapes():
    return [
        pltpu.VMEM((2, 10, FRAME_H, 128), jnp.bfloat16),
        pltpu.VMEM((2, WIN, FRAME_H, 256), jnp.bfloat16),
        pltpu.VMEM((WIN, FRAME_H, 512), jnp.bfloat16),
        pltpu.VMEM((WIN, FRAME_H, 512), jnp.bfloat16),
        *sum_shapes(pltpu.VMEM),
        *work_shapes(),
    ]


SMALL = jax.ShapeDtypeStruct((16, 128), jnp.float32)


def inner_shapes():
    height = INNER_HI - INNER_LO
    return [
        pltpu.VMEM((2, WIN, height, 256), jnp.bfloat16),
        pltpu.VMEM((WIN, height, 512), jnp.bfloat16),
        pltpu.VMEM((WIN, height, 512), jnp.bfloat16),
        *sum_shapes(pltpu.VMEM),
        *work_shapes(),
    ]


def correlate_early(form, consts):
    return pl.pallas_call(
        early_kernel,
        out_shape=SMALL,
        in_specs=[VMEM_SPEC] * 8,
        out_specs=VMEM_SPEC,
        scratch_shapes=inner_shapes(),
        compiler_params=grow_params(20),
    )(form, *consts)


def correlate_tail(early, late, edge, valid, form, consts):
    return pl.pallas_call(
        tail_kernel,
        out_shape=(SMALL,) * 2,
        in_specs=[VMEM_SPEC] * 12,
        out_specs=(VMEM_SPEC,) * 2,
        scratch_shapes=inner_shapes(),
        compiler_params=grow_params(20),
    )(early, late, edge, valid, form, *consts)


def correlate_edge(form, top, bottom, left, right, valid, consts):
    return pl.pallas_call(
        edge_kernel,
        out_shape=(SMALL,) * 3,
        in_specs=[VMEM_SPEC] * 13,
        out_specs=(VMEM_SPEC,) * 3,
        scratch_shapes=frame_shapes(),
        compiler_params=grow_params(24),
    )(form, top, bottom, left, right, valid, *consts)


def correlate_late(form, top, bottom, consts):
    return pl.pallas_call(
        late_kernel,
        out_shape=SMALL,
        in_specs=[VMEM_SPEC] * 10,
        out_specs=VMEM_SPEC,
        scratch_shapes=frame_shapes(),
        compiler_params=grow_params(24),
    )(form, top, bottom, *consts)


def relax(result, fields, above, beneath):
    field = jax.ShapeDtypeStruct((12, 2, 16), jnp.float32)
    flow, mesh = pl.pallas_call(
        relax_kernel,
        out_shape=(field, field),
        in_specs=[VMEM_SPEC] * 4,
        compiler_params=grow_params(8),
    )(result, fields, above, beneath)
    return flow.transpose(1, 0, 2), mesh.transpose(1, 0, 2)


def pack_kernel(*refs):
    sources, out, rows, held, arrived = refs[:6], refs[6], refs[7], refs[8:14], refs[14]
    copies = [pltpu.make_async_copy(sources[n], held[n], arrived.at[n]) for n in range(2, 6)]
    pieces = []
    for k in range(5):
        lanes = pl.ds(8 * TILE_W * k, 8 * TILE_W)
        pieces.append(
            [
                pltpu.make_async_copy(sources[n].at[:, lanes], held[n].at[:, lanes], arrived.at[6 + 2 * k + n])
                for n in range(2)
            ]
        )
    for copy in copies + sum(pieces, []):
        copy.start()
    for copy in copies:
        copy.wait()
    a_tiles, b_tiles, a_owner, b_owner, a_offset, b_offset = held
    count = a_tiles.shape[0]
    owners = jnp.concatenate([a_owner[...], b_owner[...]], axis=1)
    slot = lax.broadcasted_iota(jnp.int32, (128, 2 * count), 0)
    select = jnp.where(slot == owners, 1.0, 0.0).astype(jnp.bfloat16)
    zero = lambda width: jnp.zeros((count, width), jnp.bfloat16)

    def position(offset):
        row = offset[0:1, :].astype(jnp.float32)
        col = offset[1:2, :].astype(jnp.float32)
        code = jnp.floor(row * (TX / TILE_H) + col * (1.0 / TILE_W) + 1.5)
        code = jnp.concatenate([code, jnp.zeros((1, 128 - count), jnp.float32)], axis=1)
        return jnp.broadcast_to(code, (128, 128)).T[:count]

    def piece(tiles, start, width):
        return tiles[:, start : start + width]

    lane = lax.broadcasted_iota(jnp.int32, (count, 128), 1)
    code_a = jnp.where(lane == 64, position(a_offset), 0.0).astype(jnp.bfloat16)
    code_b = jnp.where(lane == 96, position(b_offset), 0.0).astype(jnp.bfloat16)

    def send_row(y):
        if y < TILE_H:
            a_part = jnp.concatenate([piece(a_tiles, TILE_W * y, TILE_W), zero(SPLIT)], axis=1)
            b_part = jnp.concatenate([zero(TILE_W), piece(b_tiles, TILE_W * y, SPLIT)], axis=1)
        elif y < TILE_H + 8:
            u = y - TILE_H
            a_part = zero(128)
            b_part = jnp.concatenate(
                [piece(b_tiles, TILE_W * (8 * k + u) + SPLIT, LANES) for k in range(4)], axis=1
            )
        else:
            u = y - TILE_H - 8
            a_part = code_a
            b_part = jnp.concatenate(
                [piece(b_tiles, TILE_W * (32 + u) + SPLIT, LANES), zero(96)], axis=1
            )
            b_part = b_part + code_b
        return jnp.concatenate([a_part, b_part], axis=0)

    for y in range(0, SLOT_H, 2):
        if y % 8 == 0 and y < TILE_H:
            for copy in pieces[y // 8]:
                copy.wait()
        both = jnp.concatenate([send_row(y), send_row(y + 1)], axis=1)
        sent = dot(select, both)
        rows[pl.ds(y, 128, stride=SLOT_H), :] = sent[:, :128]
        rows[pl.ds(y + 1, 128, stride=SLOT_H), :] = sent[:, 128:]

    def flush(n, carry):
        start = pl.multiple_of(8 * SLOT_H * n, 8)
        block = rows[pl.ds(start, 8 * SLOT_H), :].reshape(8, SLOT_H, 128)
        out[pl.ds(8 * n, 8)] = block.astype(jnp.bfloat16)
        return carry

    lax.fori_loop(0, 16, flush, 0)


def place_kernel(got, form, up, down, low, high, rows, plane_a, plane_b):
    def widen(n, carry):
        start = pl.multiple_of(8 * SLOT_H * n, 8)
        block = got[pl.ds(8 * n, 8)].astype(jnp.float32)
        rows[pl.ds(start, 8 * SLOT_H), :] = block.reshape(8 * SLOT_H, 128)
        return carry

    lax.fori_loop(0, 16, widen, 0)
    codes = rows[pl.ds(TILE_H + 8, 128, stride=SLOT_H), :]
    wanted = lax.broadcasted_iota(jnp.int32, (128, 128), 1).astype(jnp.float32) + 1.0
    pick = lambda col: jnp.where(codes[:, col : col + 1] == wanted, 1.0, 0.0).T[:96]
    select_a = pick(64)
    select_b = pick(96)
    select = jnp.concatenate([select_a, select_b], axis=0).astype(jnp.bfloat16)
    select_b = select_b.astype(jnp.bfloat16)

    def slot_row(y):
        return rows[pl.ds(y, 128, stride=SLOT_H), :].astype(jnp.bfloat16)

    for plane in (plane_a, plane_b):
        for t in range(TX):
            plane[FORM_H * t : FORM_H * t + 8, :] = jnp.zeros((8, 128), jnp.float32)
            plane[FORM_H * t + 480 : FORM_H * t + 488, :] = jnp.zeros((8, 128), jnp.float32)
    lane = lax.broadcasted_iota(jnp.int32, (96, 128), 1)
    tail = lane < LANES

    for u in range(0, 8, 2):
        tails = jnp.concatenate([slot_row(TILE_H + u + v + w) for v in range(2) for w in (0, 8)], axis=1)
        tails = dot(select_b, tails)
        for k in range(5):
            y = 8 * k + u
            main = dot(select, jnp.concatenate([slot_row(y), slot_row(y + 1)], axis=1))
            for v in range(2):
                part_a = main[:96, 128 * v : 128 * v + 128]
                part_b = main[96:, 128 * v : 128 * v + 128]
                rest = tails[:, 256 * v : 256 * v + 128] if k < 4 else tails[:, 256 * v + 128 : 256 * v + 256]
                if 0 < k < 4:
                    rest = pltpu.roll(rest, 128 - LANES * k, axis=1)
                part_b = jnp.where(tail, rest, part_b)
                for ty in range(TY):
                    where = pl.ds(TILE_H * ty + y + v + 4, TX, stride=FORM_H)
                    plane_a[where, :] = part_a[TX * ty : TX * ty + TX]
                    plane_b[where, :] = part_b[TX * ty : TX * ty + TX]

    for sec, plane in ((0, plane_a), (1, plane_b)):
        for t in range(TX):
            block = plane[FORM_H * t : FORM_H * t + FORM_H, :].astype(jnp.bfloat16)
            form[t, sec] = block
            for side, at in ((low, 0), (high, TX - 1)):
                if t == at:
                    side[sec, 0:TOP, :] = jnp.zeros((TOP, 128), jnp.bfloat16)
                    side[sec, TOP : TOP + FORM_H, :] = block
                    side[sec, TOP + FORM_H :, :] = jnp.zeros((FRAME_H - TOP - FORM_H, 128), jnp.bfloat16)
            up[t, sec] = plane[FORM_H * t : FORM_H * t + EDGE_H, :].astype(jnp.bfloat16)
            down[t, sec] = plane[FORM_H * t + 424 : FORM_H * t + 488, :].astype(jnp.bfloat16)


def pack(*arrays):
    return pl.pallas_call(
        pack_kernel,
        out_shape=jax.ShapeDtypeStruct((128, SLOT_H, 128), jnp.bfloat16),
        in_specs=[pl.BlockSpec(memory_space=pltpu.HBM)] * 6,
        out_specs=VMEM_SPEC,
        scratch_shapes=[
            pltpu.VMEM((128 * SLOT_H, 128), jnp.float32),
            *[pltpu.VMEM(x.shape, x.dtype) for x in arrays],
            pltpu.SemaphoreType.DMA((16,)),
        ],
        compiler_params=pltpu.CompilerParams(vmem_limit_bytes=60 << 20),
    )(*arrays)


def place(got):
    edge = jax.ShapeDtypeStruct((TX, 2, EDGE_H, 128), jnp.bfloat16)
    side = jax.ShapeDtypeStruct((2, FRAME_H, 128), jnp.bfloat16)
    return pl.pallas_call(
        place_kernel,
        out_shape=(jax.ShapeDtypeStruct((TX, 2, FORM_H, 128), jnp.bfloat16), edge, edge, side, side),
        scratch_shapes=[
            pltpu.VMEM((128 * SLOT_H, 128), jnp.float32),
            pltpu.VMEM((TX * FORM_H, 128), jnp.float32),
            pltpu.VMEM((TX * FORM_H, 128), jnp.float32),
        ],
        in_specs=[VMEM_SPEC],
        out_specs=(VMEM_SPEC,) * 5,
        compiler_params=pltpu.CompilerParams(vmem_limit_bytes=24 << 20),
    )(got)


def shifted(block, axis, step):
    count = lax.axis_size(axis)
    pairs = [(i, i + step) for i in range(count) if 0 <= i + step < count]
    return lax.ppermute(block, axis, pairs)


def column(side, top, bottom, t):
    grow = lambda x, low, high: jnp.pad(x[t], ((0, 0), (low, high), (0, 0)))
    return side + grow(top, 0, FRAME_H - EDGE_H) + grow(bottom, 536, FRAME_H - 536 - EDGE_H)


def per_device(a_tiles, a_owner, a_offset, b_tiles, b_owner, b_offset, patch_valid):
    packed = pack(a_tiles, b_tiles, a_owner[None], b_owner[None], a_offset.T, b_offset.T)
    got = lax.all_to_all(packed, ("row", "col"), split_axis=0, concat_axis=0, tiled=True)
    form, up, down, low, high = place(got)
    consts = tables()
    top = shifted(down, "row", 1)
    bottom = shifted(up, "row", -1)
    early = correlate_early(form, consts)
    left = shifted(column(high, top, bottom, TX - 1), "col", 1)
    right = shifted(column(low, top, bottom, 0), "col", -1)
    late = correlate_late(form, top, bottom, consts)
    edge, to_right, to_left = correlate_edge(form, top, bottom, left, right, patch_valid, consts)
    from_left = shifted(to_right, "col", 1)
    from_right = shifted(to_left, "col", -1)
    result, fields = correlate_tail(early, late, edge, patch_valid, form, consts)
    fields = fields + from_left + from_right
    above = shifted(fields[8:16], "row", 1)
    beneath = shifted(fields[0:8], "row", -1)
    return relax(result, fields, above, beneath)


def solution(mesh):
    in_specs = (
        P(("row", "col"), None),
        P(("row", "col")),
        P(("row", "col"), None),
        P(("row", "col"), None),
        P(("row", "col")),
        P(("row", "col"), None),
        P("row", "col"),
    )
    out_specs = (P(None, "row", "col"), P(None, "row", "col"))
    return jax.shard_map(
        per_device, mesh=mesh, in_specs=in_specs, out_specs=out_specs, check_vma=False
    )
```

```python
import math

import jax
import jax.numpy as jnp
import numpy as np
from jax import lax
from jax.experimental import pallas as pl
from jax.experimental.pallas import tpu as pltpu
from jax.sharding import PartitionSpec as P

PATCH = 160
STRIDE = 40
TY = 12
TX = 8
SWEEPS = 3
HALF = PATCH // 2
FREQ = HALF + 1
WIN = 3
GROUPS = 6
ROWS = PATCH
PAIR_H = 208
TILE_H = 40
TILE_W = 80
SPLIT = 128 - TILE_W
LANES = 32
SLOT_H = 56
FRAME_H = 608
FORM_H = 488
EDGE_H = 64
TOP = 56

VMEM_SPEC = pl.BlockSpec(memory_space=pltpu.VMEM)

stiffness = 1.0
tiny = 1e-06


def trig():
    k = np.arange(FREQ)
    n = np.arange(PATCH)
    phase = (k[:, None] * n[None, :] % PATCH).astype(np.float64) * (2.0 * math.pi / PATCH)
    cosine, sine = np.cos(phase), np.sin(phase)
    sine[0] = 0.0
    sine[HALF] = 0.0
    return cosine, sine


def tables():
    cosine, sine = trig()
    first = np.zeros((256, 512))
    for w in range(WIN):
        rows = slice(STRIDE * w, STRIDE * w + PATCH)
        first[rows, FREQ * w : FREQ * (w + 1)] = cosine.T
        first[rows, 256 + FREQ * w : 256 + FREQ * (w + 1)] = sine.T
    mixed = np.concatenate([cosine[HALF:], sine[1:HALF], cosine[:HALF]])
    second = np.zeros((2, ROWS, PAIR_H))
    for parity in range(2):
        second[parity, :, STRIDE * parity : STRIDE * parity + PATCH] = mixed
    second = second.reshape(2 * ROWS, PAIR_H)
    half = np.ones((FREQ, 1))
    half[0] = half[HALF] = 0.5
    shift = np.where(np.arange(PATCH) < HALF, np.arange(PATCH), np.arange(PATCH) - PATCH) * (16.0 / PATCH)
    shift[HALF] = 0.0
    rounded = lambda x: x.astype(jnp.bfloat16).astype(np.float64)
    mix = 2.0 * half * ((rounded(cosine) * shift) @ rounded(sine).T)
    sign = half[:, 0] * cosine[:, HALF]
    mix_rows = np.zeros((HALF + 8, ROWS))
    mix_rows[:FREQ, 1:HALF] = mix[:, 1:HALF]
    mix_rows[FREQ, HALF:] = sign[:HALF]
    mix_rows[FREQ, 0] = sign[HALF]
    mix_cols = np.zeros((256, 256))
    sign_cols = np.zeros((16, 256))
    for w in range(WIN):
        mix_cols[FREQ * w : FREQ * (w + 1), FREQ * w : FREQ * (w + 1)] = mix.T
        sign_cols[w, FREQ * w : FREQ * (w + 1)] = sign
    select = np.zeros((1280, 128))
    for w in range(WIN):
        lanes = np.arange(FREQ) + FREQ * w
        select[lanes, w] = half[:, 0]
        select[256 + lanes, w] = 1.0
        select[512 + lanes, 32 + w] = 1.0
        select[768 + lanes, 64 + w] = half[:, 0]
        select[1024 + lanes, 64 + w] = 1.0
    window = np.zeros((256, 128))
    for w in range(WIN):
        for kind in range(3):
            window[STRIDE * w : STRIDE * w + PATCH, 32 * kind + w] = 1.0
    as_bf16 = lambda x: jnp.asarray(x.astype(jnp.bfloat16))
    return tuple(as_bf16(x) for x in (first, second, mix_rows, mix_cols, sign_cols, select, window))


def dot(a, b):
    return lax.dot_general(a, b, (((1,), (0,)), ((), ())), preferred_element_type=jnp.float32)


def dot_exact(a, b):
    parts = []
    for _ in range(3):
        parts.append(a.astype(jnp.bfloat16))
        a = a - parts[-1].astype(jnp.float32)
    rows = a.shape[0]
    both = dot(jnp.concatenate(parts, axis=0), b)
    return both[:rows] + (both[rows : 2 * rows] + both[2 * rows :])


EDGE_GROUPS = (0, 4, 5)
INNER_GROUPS = (1, 2, 3)
INNER_LO = 64
INNER_HI = 528


def spread_groups(sums, groups):
    lane = lax.broadcasted_iota(jnp.int32, (16, 128), 1) % 32
    total = jnp.zeros((16, 128), jnp.float32)
    for piece, g in zip(sums, groups):
        piece = piece if g < GROUPS - 1 else jnp.where(lane == 0, piece, 0.0)
        total = total + (pltpu.roll(piece, WIN * g, axis=1) if g else piece)
    return total


def cell_squares(grp, sec, n, cells, lo, hi, base):
    for c in range(lo, hi):
        at = STRIDE * c - base
        near = at // 16 * 16
        values = grp[sec, n, near : near + 48, :].astype(jnp.float32)[at - near : at - near + STRIDE]
        squares = (values * values).reshape(5, 8, 256).sum(axis=0)
        cells[sec, c : c + 1, 256 * n : 256 * n + 256] = jnp.sum(squares, axis=0, keepdims=True)


def window_means(cells, sec, window, groups):
    sums = cells[sec, 0:16, :] + cells[sec, 1:17, :] + cells[sec, 2:18, :] + cells[sec, 3:19, :]
    stacked = jnp.concatenate([sums[:, 256 * n : 256 * n + 256] for n in range(WIN)], axis=0)
    total = dot_exact(stacked, window).reshape(WIN, 16, 128)
    return spread_groups([total[n] for n in range(WIN)], groups) / (PATCH * PATCH) + tiny


def group_pixels(tile, sec, g):
    c = 3 * (g // 2) + g % 2
    offset = 20 + 40 * (g % 2)
    pieces = []
    left = 240
    while left > 0 and c < 10:
        values = tile(c)
        width = min(TILE_W - offset, left)
        if sec == 0:
            pieces.append(values[:, offset : offset + width])
        else:
            if offset < SPLIT:
                pieces.append(values[:, TILE_W + offset : TILE_W + min(SPLIT, offset + width)])
            if offset + width > SPLIT:
                pieces.append(values[:, max(0, offset - SPLIT) : offset + width - SPLIT])
        left -= width
        offset = 0
        c += 1
    rows = pieces[0].shape[0]
    pieces.append(jnp.zeros((rows, 256 - 240 + left), pieces[0].dtype))
    return jnp.concatenate(pieces, axis=1)


def frame_column(form, top, bottom, frame, sec, c, upper, lower):
    t = c - 1
    if upper == lower:
        frame[sec, c, TOP : TOP + FORM_H, :] = form[t, sec]
    else:
        frame[sec, c, TOP:upper, :] = form[t, sec, 0 : upper - TOP, :]
        frame[sec, c, lower : TOP + FORM_H, :] = form[t, sec, lower - TOP :, :]
    frame[sec, c, 0:TOP, :] = top[t, sec, 0:TOP, :]
    frame[sec, c, 544:600, :] = bottom[t, sec, 8:EDGE_H, :]
    frame[sec, c, 600:608, :] = jnp.zeros((8, 128), jnp.bfloat16)
    for dst, own, other in (
        (TOP, form[t, sec, 0:8, :], top[t, sec, TOP:EDGE_H, :]),
        (536, form[t, sec, 480:488, :], bottom[t, sec, 0:8, :]),
    ):
        both = own.astype(jnp.float32) + other.astype(jnp.float32)
        frame[sec, c, dst : dst + 8, :] = both.astype(jnp.bfloat16)


def run_steps(step_of, pairs, base, fa, fb, second, mix_rows, mix_cols, sign_cols, raw, raw_end, work):
    spec, cross, flow_rows, flow_cols = work
    sub = lax.broadcasted_iota(jnp.int32, (8, 256), 0)
    top = sub == 0
    top_half = jnp.where(top, 0.5, 1.0)
    lane128 = lax.broadcasted_iota(jnp.int32, (8, 128), 1)
    k_lane = lax.broadcasted_iota(jnp.int32, (8, ROWS), 1)
    end_weight = jnp.where((k_lane == 0) | (k_lane == HALF), -4.0, -8.0)

    def spectra(pair, buf):
        n, q = step_of(pair)
        start = 80 * q - base
        if not isinstance(start, int):
            start = pl.multiple_of(start, 16)
        for sec, src in ((0, fa), (1, fb)):
            spec[buf, sec] = dot(second[...], src[n, pl.ds(start, PAIR_H), :])

    def products(pair, buf, parity):
        n, q = step_of(pair)
        shift = ROWS * parity
        totals = []
        top16 = lax.broadcasted_iota(jnp.int32, (16, 128), 0) == 0
        for lane in (0, 128):
            low = high = None
            for r in range(0, HALF, 16):
                sides = [
                    [
                        spec[buf, sec, shift + at + r : shift + at + r + 16, lo + lane : lo + lane + 128]
                        for at in (HALF, 0)
                        for lo in (0, 256)
                    ]
                    for sec in range(2)
                ]
                (a1, a2, a3, a4), (b1, b2, b3, b4) = [
                    (cc - ss, sc + cs, cc + ss, sc - cs) for cc, cs, sc, ss in sides
                ]
                plus_r = a1 * b1 + a2 * b2
                plus_i = a1 * b2 - a2 * b1
                minus_r = a3 * b3 + a4 * b4
                minus_i = a3 * b4 - a4 * b3
                dcc = plus_r + minus_r
                dss = minus_r - plus_r
                dsc = plus_i + minus_i
                dcs = plus_i - minus_i
                if r == 0:
                    (ac, asn, ae, aes), (bc, bsn, be, bes) = sides
                    dcc = jnp.where(top16, 2.0 * (ac * bc + asn * bsn), dcc)
                    dcs = jnp.where(top16, 2.0 * (ac * bsn - asn * bc), dcs)
                    dsc = jnp.where(top16, 2.0 * (ae * be + aes * bes), dsc)
                    dss = jnp.where(top16, 2.0 * (ae * bes - aes * be), dss)
                cross[buf, shift + r : shift + r + 16, lane : lane + 128] = dsc.astype(jnp.bfloat16)
                cross[buf, shift + r : shift + r + 16, 256 + lane : 384 + lane] = dss.astype(jnp.bfloat16)
                cross[buf, shift + HALF + r : shift + HALF + r + 16, lane : lane + 128] = dcc.astype(jnp.bfloat16)
                cross[buf, shift + HALF + r : shift + HALF + r + 16, 256 + lane : 384 + lane] = dcs.astype(jnp.bfloat16)
                near = dcc * dcc + dsc * dsc
                far = dcs * dcs + dss * dss
                if r == 0:
                    near = jnp.where(top16, 0.5 * near, near)
                    far = jnp.where(top16, 0.5 * far, far)
                low = near[:8] + near[8:] if low is None else low + (near[:8] + near[8:])
                high = far[:8] + far[8:] if high is None else high + (far[:8] + far[8:])
            totals.append((low, high))
        total = jnp.concatenate([totals[0][0], totals[1][0], totals[0][1], totals[1][1]], axis=1)
        raw[n, pl.ds(2 * q + parity, 1), 768:1280] = jnp.sum(total, axis=0, keepdims=True)

    def flows(pair, buf):
        n, q = step_of(pair)
        flow_cols[buf] = dot(cross[buf, :, 256:512], mix_cols[...])
        for parity in range(2):
            rows = slice(ROWS * parity, ROWS * parity + ROWS)
            flow_rows[buf, parity] = dot(mix_rows[...], cross[buf, rows, :])
            end = lax.dot_general(
                sign_cols[...], cross[buf, rows, 0:256], (((1,), (1,)), ((), ())), preferred_element_type=jnp.float32
            )[:8]
            end = jnp.sum(end * end * end_weight, axis=1, keepdims=True)
            raw_end[n] = jnp.where(lane128 == 2 * q + parity, end, raw_end[n])

    def flow_sums(pair, buf, parity):
        n, q = step_of(pair)
        shift = ROWS * parity
        where = pl.ds(2 * q + parity, 1)
        cosines = cross[buf, shift + HALF : shift + ROWS, :].astype(jnp.float32).reshape(10, 8, 512)
        mixed = flow_rows[buf, parity].reshape(11, 8, 512)
        flow_y = cosines[0] * mixed[0]
        for t in range(1, 10):
            flow_y = flow_y + cosines[t] * mixed[t]
        last = cross[buf, shift : shift + 16, :].astype(jnp.float32)[:1]
        end = last * mixed[10, 0:1] - 8.0 * mixed[10, 1:2] * mixed[10, 1:2]
        raw[n, where, 0:512] = jnp.sum(flow_y, axis=0, keepdims=True) + end
        cosines = cross[buf, shift : shift + ROWS, 0:256].astype(jnp.float32).reshape(20, 8, 256)
        mixed = flow_cols[buf, shift : shift + ROWS].reshape(20, 8, 256)
        flow_x = (cosines[0] * mixed[0] + cosines[10] * mixed[10]) * top_half
        for t in range(1, 20):
            if t != 10:
                flow_x = flow_x + cosines[t] * mixed[t]
        raw[n, where, 512:768] = jnp.sum(flow_x, axis=0, keepdims=True)

    def body(t, buf, stages):
        if 3 in stages:
            for parity in range(2):
                flow_sums(t - 3, 1 - buf, parity)
        if 2 in stages:
            flows(t - 2, buf)
        if 1 in stages:
            for parity in range(2):
                products(t - 1, 1 - buf, parity)
        if 0 in stages:
            spectra(t, buf)

    def some(t):
        body(t, t % 2, [k for k in range(4) if 0 <= t - k < pairs])

    begin = 3 + (pairs - 3) % 2
    for t in range(begin):
        some(t)

    def step(k, carry):
        body(begin + 2 * k, begin % 2, range(4))
        body(begin + 2 * k + 1, 1 - begin % 2, range(4))
        return carry

    lax.fori_loop(0, (pairs - begin) // 2, step, 0)
    for t in range(pairs, pairs + 3):
        some(t)


def finish(raw, raw_end, cells, select, window, groups):
    window = window[...]
    scale = (1.0 / (PATCH * PATCH)) / (
        window_means(cells, 0, window, groups) * window_means(cells, 1, window, groups)
    )
    sums = dot_exact(raw[...].reshape(WIN * 16, 1280), select[...]).reshape(WIN, 16, 128)
    pad = jnp.zeros((120, 128), jnp.float32)
    ends = [
        pltpu.roll(jnp.concatenate([raw_end[n], pad], axis=0).T[:16], 32, axis=1) for n in range(WIN)
    ]
    total = spread_groups([sums[n] + ends[n] for n in range(WIN)], groups)
    unit = (2.0 / (PATCH * PATCH)) ** 2 * HALF / (PATCH * PATCH)
    total = total * (scale * unit)
    lane_all = lax.broadcasted_iota(jnp.int32, (16, 128), 1)
    weight = jnp.where(lane_all >= 64, total * HALF, 0.0)
    down = 1.0 + weight + pltpu.roll(weight, 96, axis=1) + pltpu.roll(weight, 64, axis=1)
    return jnp.where(lane_all >= 64, weight, total) / down


def clear_sums(raw, raw_end):
    raw[:, 12:16, :] = jnp.zeros((WIN, 4, 1280), jnp.float32)
    raw_end[...] = jnp.zeros((WIN, 8, 128), jnp.float32)


def early_step(pair):
    return pair // 4, 1 + pair % 4


def tail_step(pair):
    return 2, 1 + pair


def edge_step(pair):
    return pair // 6, pair % 6


def late_step(pair):
    return pair // 2, 5 * (pair % 2)


def inner_rows(
    members, step_of, pairs, form, first, second, mix_rows, mix_cols, sign_cols, select, window,
    grp, fa, fb, cells, raw, raw_end, *work,
):
    lo, hi = INNER_LO - TOP, INNER_HI - TOP
    raw[...] = jnp.zeros((WIN, 16, 1280), jnp.float32)
    raw_end[...] = jnp.zeros((WIN, 8, 128), jnp.float32)
    for sec, dst in ((0, fa), (1, fb)):
        cells[sec] = jnp.zeros((24, 256 * WIN), jnp.float32)
        for n in members:
            pixels = group_pixels(lambda c: form[c - 1, sec, lo:hi, :], sec, INNER_GROUPS[n])
            grp[sec, n] = pixels
            dst[n] = dot(pixels, first[...]).astype(jnp.bfloat16)
            cell_squares(grp, sec, n, cells, 2, 13, INNER_LO)
    run_steps(step_of, pairs, INNER_LO, fa, fb, second, mix_rows, mix_cols, sign_cols, raw, raw_end, work)
    return finish(raw, raw_end, cells, select, window, INNER_GROUPS)


def early_kernel(*refs):
    out = refs[8]
    out[...] = inner_rows((0, 1), early_step, 8, *refs[:8], *refs[9:])


def tail_kernel(early, late, edge, valid, *refs):
    out, fields = refs[8:10]
    row = lax.broadcasted_iota(jnp.int32, (16, 128), 0)
    lane = lax.broadcasted_iota(jnp.int32, (16, 128), 1) % 32
    own = inner_rows((2,), tail_step, 4, *refs[:8], *refs[10:])
    own = jnp.where(lane < 9, early[...], own)
    own = jnp.where((row >= 2) & (row < 10), own, late[...])
    result = jnp.where((lane >= 3) & (lane < 12), own, edge[...])
    out[...] = result
    fields[...] = mesh_fields(result, valid)[0]


def mesh_fields(result, valid):
    row = lax.broadcasted_iota(jnp.int32, (16, 128), 0)
    lane = lax.broadcasted_iota(jnp.int32, (16, 128), 1)
    column = lane % 32
    inside = (row < 12) & (lane < 96) & (column >= SWEEPS) & (column < SWEEPS + 16)
    flags = jnp.concatenate([valid[...].astype(jnp.float32), jnp.zeros((12, 112), jnp.float32)], axis=1)
    flags = jnp.concatenate([flags, jnp.zeros((4, 128), jnp.float32)], axis=0)
    flags = sum(pltpu.roll(flags, SWEEPS + 32 * kind, axis=1) for kind in range(3))
    fields = flags * pltpu.roll(jnp.where(row < 12, result, 0.0), SWEEPS, axis=1)
    fields = fields + jnp.where(lane >= 64, 4.0 * stiffness, 0.0)
    return jnp.where(inside, fields, 0.0), column


def edge_kernel(
    form, top, bottom, left, right, valid, first, second, mix_rows, mix_cols, sign_cols, select, window,
    out, to_right, to_left, frame, grp, fa, fb, cells, raw, raw_end, *work,
):
    clear_sums(raw, raw_end)
    for sec, dst in ((0, fa), (1, fb)):
        frame[sec, 0] = left[sec]
        frame[sec, 9] = right[sec]
        for c in (1, 2, 3, 6, 7, 8):
            frame_column(form, top, bottom, frame, sec, c, FRAME_H, FRAME_H)
        for n, g in enumerate(EDGE_GROUPS):
            pixels = group_pixels(lambda c: frame[sec, c], sec, g)
            grp[sec, n] = pixels
            dst[n] = dot(pixels, first[...]).astype(jnp.bfloat16)
            cell_squares(grp, sec, n, cells, 0, 15, 0)
        cells[sec, 15:24, :] = jnp.zeros((9, 256 * WIN), jnp.float32)
    run_steps(edge_step, 18, 0, fa, fb, second, mix_rows, mix_cols, sign_cols, raw, raw_end, work)
    result = finish(raw, raw_end, cells, select, window, EDGE_GROUPS)
    out[...] = result
    fields, column = mesh_fields(result, valid)
    last = jnp.where((column >= 16) & (column < 16 + SWEEPS), fields, 0.0)
    to_right[...] = pltpu.roll(last, 112, axis=1)
    head = jnp.where((column >= SWEEPS) & (column < 2 * SWEEPS), fields, 0.0)
    to_left[...] = pltpu.roll(head, 16, axis=1)


def late_kernel(
    form, top, bottom, first, second, mix_rows, mix_cols, sign_cols, select, window,
    out, frame, grp, fa, fb, cells, raw, raw_end, *work,
):
    upper, lower = 208, 400
    clear_sums(raw, raw_end)
    raw[:, 2:10, :] = jnp.zeros((WIN, 8, 1280), jnp.float32)
    for sec, dst in ((0, fa), (1, fb)):
        cells[sec] = jnp.zeros((24, 256 * WIN), jnp.float32)
        for c in range(1, 8):
            frame_column(form, top, bottom, frame, sec, c, upper, lower)
        for n, g in enumerate(INNER_GROUPS):
            for lo, hi in ((0, upper), (lower, FRAME_H)):
                pixels = group_pixels(lambda c: frame[sec, c, lo:hi, :], sec, g)
                grp[sec, n, lo:hi, :] = pixels
                dst[n, lo:hi, :] = dot(pixels, first[...]).astype(jnp.bfloat16)
            cell_squares(grp, sec, n, cells, 0, 5, 0)
            cell_squares(grp, sec, n, cells, 10, 15, 0)
    run_steps(late_step, 6, 0, fa, fb, second, mix_rows, mix_cols, sign_cols, raw, raw_end, work)
    out[...] = finish(raw, raw_end, cells, select, window, INNER_GROUPS)


def relax_kernel(result, fields, above, beneath, flow, mesh_out):
    frame = jnp.concatenate(
        [above[...][1:4], fields[...][:12], beneath[...][:SWEEPS], jnp.zeros((6, 128), jnp.float32)],
        axis=0,
    )
    lane = lax.broadcasted_iota(jnp.int32, (24, 128), 1)
    below = jnp.where(lane < 32, pltpu.roll(frame, 64, axis=1), pltpu.roll(frame, 96, axis=1))
    inside = (below > 0.0) & (lane < 64)
    rest = jnp.where(inside, 1.0 / jnp.where(inside, below, 1.0), 0.0)
    mesh = jnp.where(lane < 64, frame, 0.0)
    pull = mesh * jnp.where(inside, below - 4.0 * stiffness, 0.0)
    for _ in range(SWEEPS):
        around = (
            pltpu.roll(mesh, 1, axis=0)
            + pltpu.roll(mesh, 23, axis=0)
            + pltpu.roll(mesh, 1, axis=1)
            + pltpu.roll(mesh, 127, axis=1)
        )
        mesh = (pull + stiffness * around) * rest
    for kind in range(2):
        flow[:, kind, :] = result[0:12, 32 * kind : 32 * kind + 16]
        mesh_out[:, kind, :] = mesh[SWEEPS : SWEEPS + 12, 32 * kind + SWEEPS : 32 * kind + SWEEPS + 16]


def work_shapes():
    return [
        pltpu.VMEM((2, 2, 2 * ROWS, 512), jnp.float32),
        pltpu.VMEM((2, 2 * ROWS, 512), jnp.bfloat16),
        pltpu.VMEM((2, 2, HALF + 8, 512), jnp.float32),
        pltpu.VMEM((2, 2 * ROWS, 256), jnp.float32),
    ]


SUM_SHAPES = (
    ((2, 24, 256 * WIN), jnp.float32),
    ((WIN, 16, 1280), jnp.float32),
    ((WIN, 8, 128), jnp.float32),
)


def sum_shapes(make):
    return [make(*shape) for shape in SUM_SHAPES]


def grow_params(mib):
    return pltpu.CompilerParams(vmem_limit_bytes=mib << 20)


def frame_shapes():
    return [
        pltpu.VMEM((2, 10, FRAME_H, 128), jnp.bfloat16),
        pltpu.VMEM((2, WIN, FRAME_H, 256), jnp.bfloat16),
        pltpu.VMEM((WIN, FRAME_H, 512), jnp.bfloat16),
        pltpu.VMEM((WIN, FRAME_H, 512), jnp.bfloat16),
        *sum_shapes(pltpu.VMEM),
        *work_shapes(),
    ]


SMALL = jax.ShapeDtypeStruct((16, 128), jnp.float32)


def inner_shapes():
    height = INNER_HI - INNER_LO
    return [
        pltpu.VMEM((2, WIN, height, 256), jnp.bfloat16),
        pltpu.VMEM((WIN, height, 512), jnp.bfloat16),
        pltpu.VMEM((WIN, height, 512), jnp.bfloat16),
        *sum_shapes(pltpu.VMEM),
        *work_shapes(),
    ]


def correlate_early(form, consts):
    return pl.pallas_call(
        early_kernel,
        out_shape=SMALL,
        in_specs=[VMEM_SPEC] * 8,
        out_specs=VMEM_SPEC,
        scratch_shapes=inner_shapes(),
        compiler_params=grow_params(20),
    )(form, *consts)


def correlate_tail(early, late, edge, valid, form, consts):
    return pl.pallas_call(
        tail_kernel,
        out_shape=(SMALL,) * 2,
        in_specs=[VMEM_SPEC] * 12,
        out_specs=(VMEM_SPEC,) * 2,
        scratch_shapes=inner_shapes(),
        compiler_params=grow_params(20),
    )(early, late, edge, valid, form, *consts)


def correlate_edge(form, top, bottom, left, right, valid, consts):
    return pl.pallas_call(
        edge_kernel,
        out_shape=(SMALL,) * 3,
        in_specs=[VMEM_SPEC] * 13,
        out_specs=(VMEM_SPEC,) * 3,
        scratch_shapes=frame_shapes(),
        compiler_params=grow_params(24),
    )(form, top, bottom, left, right, valid, *consts)


def correlate_late(form, top, bottom, consts):
    return pl.pallas_call(
        late_kernel,
        out_shape=SMALL,
        in_specs=[VMEM_SPEC] * 10,
        out_specs=VMEM_SPEC,
        scratch_shapes=frame_shapes(),
        compiler_params=grow_params(24),
    )(form, top, bottom, *consts)


def relax(result, fields, above, beneath):
    field = jax.ShapeDtypeStruct((12, 2, 16), jnp.float32)
    flow, mesh = pl.pallas_call(
        relax_kernel,
        out_shape=(field, field),
        in_specs=[VMEM_SPEC] * 4,
        compiler_params=grow_params(8),
    )(result, fields, above, beneath)
    return flow.transpose(1, 0, 2), mesh.transpose(1, 0, 2)


def pack_kernel(*refs):
    sources, out, rows, held, arrived = refs[:6], refs[6], refs[7], refs[8:14], refs[14]
    copies = [pltpu.make_async_copy(src, dst, arrived.at[n]) for n, (src, dst) in enumerate(zip(sources, held))]
    for copy in copies:
        copy.start()
    for copy in copies:
        copy.wait()
    a_tiles, b_tiles, a_owner, b_owner, a_offset, b_offset = held
    count = a_tiles.shape[0]
    owners = jnp.concatenate([a_owner[...], b_owner[...]], axis=1)
    slot = lax.broadcasted_iota(jnp.int32, (128, 2 * count), 0)
    select = jnp.where(slot == owners, 1.0, 0.0).astype(jnp.bfloat16)
    zero = lambda width: jnp.zeros((count, width), jnp.bfloat16)

    def position(offset):
        row = offset[0:1, :].astype(jnp.float32)
        col = offset[1:2, :].astype(jnp.float32)
        code = jnp.floor(row * (TX / TILE_H) + col * (1.0 / TILE_W) + 1.5)
        code = jnp.concatenate([code, jnp.zeros((1, 128 - count), jnp.float32)], axis=1)
        return jnp.broadcast_to(code, (128, 128)).T[:count]

    def piece(tiles, start, width):
        return tiles[:, start : start + width]

    lane = lax.broadcasted_iota(jnp.int32, (count, 128), 1)
    code_a = jnp.where(lane == 64, position(a_offset), 0.0).astype(jnp.bfloat16)
    code_b = jnp.where(lane == 96, position(b_offset), 0.0).astype(jnp.bfloat16)

    def send_row(y):
        if y < TILE_H:
            a_part = jnp.concatenate([piece(a_tiles, TILE_W * y, TILE_W), zero(SPLIT)], axis=1)
            b_part = jnp.concatenate([zero(TILE_W), piece(b_tiles, TILE_W * y, SPLIT)], axis=1)
        elif y < TILE_H + 8:
            u = y - TILE_H
            a_part = zero(128)
            b_part = jnp.concatenate(
                [piece(b_tiles, TILE_W * (8 * k + u) + SPLIT, LANES) for k in range(4)], axis=1
            )
        else:
            u = y - TILE_H - 8
            a_part = code_a
            b_part = jnp.concatenate(
                [piece(b_tiles, TILE_W * (32 + u) + SPLIT, LANES), zero(96)], axis=1
            )
            b_part = b_part + code_b
        return jnp.concatenate([a_part, b_part], axis=0)

    for y in range(0, SLOT_H, 2):
        both = jnp.concatenate([send_row(y), send_row(y + 1)], axis=1)
        sent = dot(select, both)
        rows[pl.ds(y, 128, stride=SLOT_H), :] = sent[:, :128]
        rows[pl.ds(y + 1, 128, stride=SLOT_H), :] = sent[:, 128:]

    def flush(n, carry):
        start = pl.multiple_of(8 * SLOT_H * n, 8)
        block = rows[pl.ds(start, 8 * SLOT_H), :].reshape(8, SLOT_H, 128)
        out[pl.ds(8 * n, 8)] = block.astype(jnp.bfloat16)
        return carry

    lax.fori_loop(0, 16, flush, 0)


def place_kernel(got, form, up, down, low, high, rows, plane_a, plane_b):
    def widen(n, carry):
        start = pl.multiple_of(8 * SLOT_H * n, 8)
        block = got[pl.ds(8 * n, 8)].astype(jnp.float32)
        rows[pl.ds(start, 8 * SLOT_H), :] = block.reshape(8 * SLOT_H, 128)
        return carry

    lax.fori_loop(0, 16, widen, 0)
    codes = rows[pl.ds(TILE_H + 8, 128, stride=SLOT_H), :]
    wanted = lax.broadcasted_iota(jnp.int32, (128, 128), 1).astype(jnp.float32) + 1.0
    pick = lambda col: jnp.where(codes[:, col : col + 1] == wanted, 1.0, 0.0).T[:96]
    select_a = pick(64)
    select_b = pick(96)
    select = jnp.concatenate([select_a, select_b], axis=0).astype(jnp.bfloat16)
    select_b = select_b.astype(jnp.bfloat16)

    def slot_row(y):
        return rows[pl.ds(y, 128, stride=SLOT_H), :].astype(jnp.bfloat16)

    for plane in (plane_a, plane_b):
        for t in range(TX):
            plane[FORM_H * t : FORM_H * t + 8, :] = jnp.zeros((8, 128), jnp.float32)
            plane[FORM_H * t + 480 : FORM_H * t + 488, :] = jnp.zeros((8, 128), jnp.float32)
    lane = lax.broadcasted_iota(jnp.int32, (96, 128), 1)
    tail = lane < LANES

    for u in range(0, 8, 2):
        tails = jnp.concatenate([slot_row(TILE_H + u + v + w) for v in range(2) for w in (0, 8)], axis=1)
        tails = dot(select_b, tails)
        for k in range(5):
            y = 8 * k + u
            main = dot(select, jnp.concatenate([slot_row(y), slot_row(y + 1)], axis=1))
            for v in range(2):
                part_a = main[:96, 128 * v : 128 * v + 128]
                part_b = main[96:, 128 * v : 128 * v + 128]
                rest = tails[:, 256 * v : 256 * v + 128] if k < 4 else tails[:, 256 * v + 128 : 256 * v + 256]
                if 0 < k < 4:
                    rest = pltpu.roll(rest, 128 - LANES * k, axis=1)
                part_b = jnp.where(tail, rest, part_b)
                for ty in range(TY):
                    where = pl.ds(TILE_H * ty + y + v + 4, TX, stride=FORM_H)
                    plane_a[where, :] = part_a[TX * ty : TX * ty + TX]
                    plane_b[where, :] = part_b[TX * ty : TX * ty + TX]

    for sec, plane in ((0, plane_a), (1, plane_b)):
        for t in range(TX):
            block = plane[FORM_H * t : FORM_H * t + FORM_H, :].astype(jnp.bfloat16)
            form[t, sec] = block
            for side, at in ((low, 0), (high, TX - 1)):
                if t == at:
                    side[sec, 0:TOP, :] = jnp.zeros((TOP, 128), jnp.bfloat16)
                    side[sec, TOP : TOP + FORM_H, :] = block
                    side[sec, TOP + FORM_H :, :] = jnp.zeros((FRAME_H - TOP - FORM_H, 128), jnp.bfloat16)
            up[t, sec] = plane[FORM_H * t : FORM_H * t + EDGE_H, :].astype(jnp.bfloat16)
            down[t, sec] = plane[FORM_H * t + 424 : FORM_H * t + 488, :].astype(jnp.bfloat16)


def pack(*arrays):
    return pl.pallas_call(
        pack_kernel,
        out_shape=jax.ShapeDtypeStruct((128, SLOT_H, 128), jnp.bfloat16),
        in_specs=[pl.BlockSpec(memory_space=pltpu.HBM)] * 6,
        out_specs=VMEM_SPEC,
        scratch_shapes=[
            pltpu.VMEM((128 * SLOT_H, 128), jnp.float32),
            *[pltpu.VMEM(x.shape, x.dtype) for x in arrays],
            pltpu.SemaphoreType.DMA((6,)),
        ],
        compiler_params=pltpu.CompilerParams(vmem_limit_bytes=60 << 20),
    )(*arrays)


def place(got):
    edge = jax.ShapeDtypeStruct((TX, 2, EDGE_H, 128), jnp.bfloat16)
    side = jax.ShapeDtypeStruct((2, FRAME_H, 128), jnp.bfloat16)
    return pl.pallas_call(
        place_kernel,
        out_shape=(jax.ShapeDtypeStruct((TX, 2, FORM_H, 128), jnp.bfloat16), edge, edge, side, side),
        scratch_shapes=[
            pltpu.VMEM((128 * SLOT_H, 128), jnp.float32),
            pltpu.VMEM((TX * FORM_H, 128), jnp.float32),
            pltpu.VMEM((TX * FORM_H, 128), jnp.float32),
        ],
        in_specs=[VMEM_SPEC],
        out_specs=(VMEM_SPEC,) * 5,
        compiler_params=pltpu.CompilerParams(vmem_limit_bytes=24 << 20),
    )(got)


def shifted(block, axis, step):
    count = lax.axis_size(axis)
    pairs = [(i, i + step) for i in range(count) if 0 <= i + step < count]
    return lax.ppermute(block, axis, pairs)


def column(side, top, bottom, t):
    grow = lambda x, low, high: jnp.pad(x[t], ((0, 0), (low, high), (0, 0)))
    return side + grow(top, 0, FRAME_H - EDGE_H) + grow(bottom, 536, FRAME_H - 536 - EDGE_H)


def per_device(a_tiles, a_owner, a_offset, b_tiles, b_owner, b_offset, patch_valid):
    packed = pack(a_tiles, b_tiles, a_owner[None], b_owner[None], a_offset.T, b_offset.T)
    got = lax.all_to_all(packed, ("row", "col"), split_axis=0, concat_axis=0, tiled=True)
    form, up, down, low, high = place(got)
    consts = tables()
    top = shifted(down, "row", 1)
    bottom = shifted(up, "row", -1)
    early = correlate_early(form, consts)
    left = shifted(column(high, top, bottom, TX - 1), "col", 1)
    right = shifted(column(low, top, bottom, 0), "col", -1)
    late = correlate_late(form, top, bottom, consts)
    edge, to_right, to_left = correlate_edge(form, top, bottom, left, right, patch_valid, consts)
    from_left = shifted(to_right, "col", 1)
    from_right = shifted(to_left, "col", -1)
    result, fields = correlate_tail(early, late, edge, patch_valid, form, consts)
    fields = fields + from_left + from_right
    above = shifted(fields[8:16], "row", 1)
    beneath = shifted(fields[0:8], "row", -1)
    return relax(result, fields, above, beneath)


def solution(mesh):
    in_specs = (
        P(("row", "col"), None),
        P(("row", "col")),
        P(("row", "col"), None),
        P(("row", "col"), None),
        P(("row", "col")),
        P(("row", "col"), None),
        P("row", "col"),
    )
    out_specs = (P(None, "row", "col"), P(None, "row", "col"))
    return jax.shard_map(
        per_device, mesh=mesh, in_specs=in_specs, out_specs=out_specs, check_vma=False
    )
```

```python
import math

import jax
import jax.numpy as jnp
import numpy as np
from jax import lax
from jax.experimental import pallas as pl
from jax.experimental.pallas import tpu as pltpu
from jax.sharding import PartitionSpec as P

PATCH = 160
STRIDE = 40
TY = 12
TX = 8
SWEEPS = 3
HALF = PATCH // 2
FREQ = HALF + 1
WIN = 3
GROUPS = 6
ROWS = PATCH
PAIR_H = 208
TILE_H = 40
TILE_W = 80
SPLIT = 128 - TILE_W
LANES = 32
SLOT_H = 56
FRAME_H = 608
FORM_H = 488
EDGE_H = 64
TOP = 56

VMEM_SPEC = pl.BlockSpec(memory_space=pltpu.VMEM)

stiffness = 1.0
tiny = 1e-06


def trig():
    k = np.arange(FREQ)
    n = np.arange(PATCH)
    phase = (k[:, None] * n[None, :] % PATCH).astype(np.float64) * (2.0 * math.pi / PATCH)
    cosine, sine = np.cos(phase), np.sin(phase)
    sine[0] = 0.0
    sine[HALF] = 0.0
    return cosine, sine


def tables():
    cosine, sine = trig()
    first = np.zeros((256, 512))
    for w in range(WIN):
        rows = slice(STRIDE * w, STRIDE * w + PATCH)
        first[rows, FREQ * w : FREQ * (w + 1)] = cosine.T
        first[rows, 256 + FREQ * w : 256 + FREQ * (w + 1)] = sine.T
    mixed = np.concatenate([cosine[HALF:], sine[1:HALF], cosine[:HALF]])
    second = np.zeros((2, ROWS, PAIR_H))
    for parity in range(2):
        second[parity, :, STRIDE * parity : STRIDE * parity + PATCH] = mixed
    second = second.reshape(2 * ROWS, PAIR_H)
    half = np.ones((FREQ, 1))
    half[0] = half[HALF] = 0.5
    shift = np.where(np.arange(PATCH) < HALF, np.arange(PATCH), np.arange(PATCH) - PATCH) * (16.0 / PATCH)
    shift[HALF] = 0.0
    rounded = lambda x: x.astype(jnp.bfloat16).astype(np.float64)
    mix = 2.0 * half * ((rounded(cosine) * shift) @ rounded(sine).T)
    sign = half[:, 0] * cosine[:, HALF]
    mix_rows = np.zeros((HALF + 8, ROWS))
    mix_rows[:FREQ, 1:HALF] = mix[:, 1:HALF]
    mix_rows[FREQ, HALF:] = sign[:HALF]
    mix_rows[FREQ, 0] = sign[HALF]
    mix_cols = np.zeros((256, 256))
    sign_cols = np.zeros((16, 256))
    for w in range(WIN):
        mix_cols[FREQ * w : FREQ * (w + 1), FREQ * w : FREQ * (w + 1)] = mix.T
        sign_cols[w, FREQ * w : FREQ * (w + 1)] = sign
    select = np.zeros((1280, 128))
    for w in range(WIN):
        lanes = np.arange(FREQ) + FREQ * w
        select[lanes, w] = half[:, 0]
        select[256 + lanes, w] = 1.0
        select[512 + lanes, 32 + w] = 1.0
        select[768 + lanes, 64 + w] = half[:, 0]
        select[1024 + lanes, 64 + w] = 1.0
    window = np.zeros((256, 128))
    for w in range(WIN):
        for kind in range(3):
            window[STRIDE * w : STRIDE * w + PATCH, 32 * kind + w] = 1.0
    as_bf16 = lambda x: jnp.asarray(x.astype(jnp.bfloat16))
    return tuple(as_bf16(x) for x in (first, second, mix_rows, mix_cols, sign_cols, select, window))


def dot(a, b):
    return lax.dot_general(a, b, (((1,), (0,)), ((), ())), preferred_element_type=jnp.float32)


def dot_exact(a, b):
    parts = []
    for _ in range(3):
        parts.append(a.astype(jnp.bfloat16))
        a = a - parts[-1].astype(jnp.float32)
    rows = a.shape[0]
    both = dot(jnp.concatenate(parts, axis=0), b)
    return both[:rows] + (both[rows : 2 * rows] + both[2 * rows :])


EDGE_GROUPS = (0, 4, 5)
INNER_GROUPS = (1, 2, 3)
INNER_LO = 64
INNER_HI = 528


def spread_groups(sums, groups):
    lane = lax.broadcasted_iota(jnp.int32, (16, 128), 1) % 32
    total = jnp.zeros((16, 128), jnp.float32)
    for piece, g in zip(sums, groups):
        piece = piece if g < GROUPS - 1 else jnp.where(lane == 0, piece, 0.0)
        total = total + (pltpu.roll(piece, WIN * g, axis=1) if g else piece)
    return total


def cell_squares(grp, sec, n, cells, lo, hi, base):
    for c in range(lo, hi):
        at = STRIDE * c - base
        near = at // 16 * 16
        values = grp[sec, n, near : near + 48, :].astype(jnp.float32)[at - near : at - near + STRIDE]
        squares = (values * values).reshape(5, 8, 256).sum(axis=0)
        cells[sec, c : c + 1, 256 * n : 256 * n + 256] = jnp.sum(squares, axis=0, keepdims=True)


def window_means(cells, sec, window, groups):
    sums = cells[sec, 0:16, :] + cells[sec, 1:17, :] + cells[sec, 2:18, :] + cells[sec, 3:19, :]
    stacked = jnp.concatenate([sums[:, 256 * n : 256 * n + 256] for n in range(WIN)], axis=0)
    total = dot_exact(stacked, window).reshape(WIN, 16, 128)
    return spread_groups([total[n] for n in range(WIN)], groups) / (PATCH * PATCH) + tiny


def group_pixels(tile, sec, g):
    c = 3 * (g // 2) + g % 2
    offset = 20 + 40 * (g % 2)
    pieces = []
    left = 240
    while left > 0 and c < 10:
        values = tile(c)
        width = min(TILE_W - offset, left)
        if sec == 0:
            pieces.append(values[:, offset : offset + width])
        else:
            if offset < SPLIT:
                pieces.append(values[:, TILE_W + offset : TILE_W + min(SPLIT, offset + width)])
            if offset + width > SPLIT:
                pieces.append(values[:, max(0, offset - SPLIT) : offset + width - SPLIT])
        left -= width
        offset = 0
        c += 1
    rows = pieces[0].shape[0]
    pieces.append(jnp.zeros((rows, 256 - 240 + left), pieces[0].dtype))
    return jnp.concatenate(pieces, axis=1)


def frame_column(form, top, bottom, frame, sec, c, upper, lower):
    t = c - 1
    if upper == lower:
        frame[sec, c, TOP : TOP + FORM_H, :] = form[t, sec]
    else:
        frame[sec, c, TOP:upper, :] = form[t, sec, 0 : upper - TOP, :]
        frame[sec, c, lower : TOP + FORM_H, :] = form[t, sec, lower - TOP :, :]
    frame[sec, c, 0:TOP, :] = top[t, sec, 0:TOP, :]
    frame[sec, c, 544:600, :] = bottom[t, sec, 8:EDGE_H, :]
    frame[sec, c, 600:608, :] = jnp.zeros((8, 128), jnp.bfloat16)
    for dst, own, other in (
        (TOP, form[t, sec, 0:8, :], top[t, sec, TOP:EDGE_H, :]),
        (536, form[t, sec, 480:488, :], bottom[t, sec, 0:8, :]),
    ):
        both = own.astype(jnp.float32) + other.astype(jnp.float32)
        frame[sec, c, dst : dst + 8, :] = both.astype(jnp.bfloat16)


def run_steps(step_of, pairs, base, fa, fb, second, mix_rows, mix_cols, sign_cols, raw, raw_end, work):
    spec, cross, flow_rows, flow_cols = work
    sub = lax.broadcasted_iota(jnp.int32, (8, 256), 0)
    top = sub == 0
    top_half = jnp.where(top, 0.5, 1.0)
    lane128 = lax.broadcasted_iota(jnp.int32, (8, 128), 1)
    k_lane = lax.broadcasted_iota(jnp.int32, (8, ROWS), 1)
    end_weight = jnp.where((k_lane == 0) | (k_lane == HALF), -4.0, -8.0)

    def spectra(pair, buf):
        n, q = step_of(pair)
        start = 80 * q - base
        if not isinstance(start, int):
            start = pl.multiple_of(start, 16)
        for sec, src in ((0, fa), (1, fb)):
            spec[buf, sec] = dot(second[...], src[n, pl.ds(start, PAIR_H), :])

    def products(pair, buf, parity):
        n, q = step_of(pair)
        shift = ROWS * parity
        totals = []
        top16 = lax.broadcasted_iota(jnp.int32, (16, 128), 0) == 0
        for lane in (0, 128):
            low = high = None
            for r in range(0, HALF, 16):
                sides = [
                    [
                        spec[buf, sec, shift + at + r : shift + at + r + 16, lo + lane : lo + lane + 128]
                        for at in (HALF, 0)
                        for lo in (0, 256)
                    ]
                    for sec in range(2)
                ]
                (a1, a2, a3, a4), (b1, b2, b3, b4) = [
                    (cc - ss, sc + cs, cc + ss, sc - cs) for cc, cs, sc, ss in sides
                ]
                plus_r = a1 * b1 + a2 * b2
                plus_i = a1 * b2 - a2 * b1
                minus_r = a3 * b3 + a4 * b4
                minus_i = a3 * b4 - a4 * b3
                dcc = plus_r + minus_r
                dss = minus_r - plus_r
                dsc = plus_i + minus_i
                dcs = plus_i - minus_i
                if r == 0:
                    (ac, asn, ae, aes), (bc, bsn, be, bes) = sides
                    dcc = jnp.where(top16, 2.0 * (ac * bc + asn * bsn), dcc)
                    dcs = jnp.where(top16, 2.0 * (ac * bsn - asn * bc), dcs)
                    dsc = jnp.where(top16, 2.0 * (ae * be + aes * bes), dsc)
                    dss = jnp.where(top16, 2.0 * (ae * bes - aes * be), dss)
                cross[buf, shift + r : shift + r + 16, lane : lane + 128] = dsc.astype(jnp.bfloat16)
                cross[buf, shift + r : shift + r + 16, 256 + lane : 384 + lane] = dss.astype(jnp.bfloat16)
                cross[buf, shift + HALF + r : shift + HALF + r + 16, lane : lane + 128] = dcc.astype(jnp.bfloat16)
                cross[buf, shift + HALF + r : shift + HALF + r + 16, 256 + lane : 384 + lane] = dcs.astype(jnp.bfloat16)
                near = dcc * dcc + dsc * dsc
                far = dcs * dcs + dss * dss
                if r == 0:
                    near = jnp.where(top16, 0.5 * near, near)
                    far = jnp.where(top16, 0.5 * far, far)
                low = near[:8] + near[8:] if low is None else low + (near[:8] + near[8:])
                high = far[:8] + far[8:] if high is None else high + (far[:8] + far[8:])
            totals.append((low, high))
        total = jnp.concatenate([totals[0][0], totals[1][0], totals[0][1], totals[1][1]], axis=1)
        raw[n, pl.ds(2 * q + parity, 1), 768:1280] = jnp.sum(total, axis=0, keepdims=True)

    def flows(pair, buf):
        n, q = step_of(pair)
        flow_cols[buf] = dot(cross[buf, :, 256:512], mix_cols[...])
        for parity in range(2):
            rows = slice(ROWS * parity, ROWS * parity + ROWS)
            flow_rows[buf, parity] = dot(mix_rows[...], cross[buf, rows, :])
            end = lax.dot_general(
                sign_cols[...], cross[buf, rows, 0:256], (((1,), (1,)), ((), ())), preferred_element_type=jnp.float32
            )[:8]
            end = jnp.sum(end * end * end_weight, axis=1, keepdims=True)
            raw_end[n] = jnp.where(lane128 == 2 * q + parity, end, raw_end[n])

    def flow_sums(pair, buf, parity):
        n, q = step_of(pair)
        shift = ROWS * parity
        where = pl.ds(2 * q + parity, 1)
        cosines = cross[buf, shift + HALF : shift + ROWS, :].astype(jnp.float32).reshape(10, 8, 512)
        mixed = flow_rows[buf, parity].reshape(11, 8, 512)
        flow_y = cosines[0] * mixed[0]
        for t in range(1, 10):
            flow_y = flow_y + cosines[t] * mixed[t]
        last = cross[buf, shift : shift + 16, :].astype(jnp.float32)[:1]
        end = last * mixed[10, 0:1] - 8.0 * mixed[10, 1:2] * mixed[10, 1:2]
        raw[n, where, 0:512] = jnp.sum(flow_y, axis=0, keepdims=True) + end
        cosines = cross[buf, shift : shift + ROWS, 0:256].astype(jnp.float32).reshape(20, 8, 256)
        mixed = flow_cols[buf, shift : shift + ROWS].reshape(20, 8, 256)
        flow_x = (cosines[0] * mixed[0] + cosines[10] * mixed[10]) * top_half
        for t in range(1, 20):
            if t != 10:
                flow_x = flow_x + cosines[t] * mixed[t]
        raw[n, where, 512:768] = jnp.sum(flow_x, axis=0, keepdims=True)

    def body(t, buf, stages):
        if 3 in stages:
            for parity in range(2):
                flow_sums(t - 3, 1 - buf, parity)
        if 2 in stages:
            flows(t - 2, buf)
        if 1 in stages:
            for parity in range(2):
                products(t - 1, 1 - buf, parity)
        if 0 in stages:
            spectra(t, buf)

    def some(t):
        body(t, t % 2, [k for k in range(4) if 0 <= t - k < pairs])

    begin = 3 + (pairs - 3) % 2
    for t in range(begin):
        some(t)

    def step(k, carry):
        body(begin + 2 * k, begin % 2, range(4))
        body(begin + 2 * k + 1, 1 - begin % 2, range(4))
        return carry

    lax.fori_loop(0, (pairs - begin) // 2, step, 0)
    for t in range(pairs, pairs + 3):
        some(t)


def finish(raw, raw_end, cells, select, window, groups):
    window = window[...]
    scale = (1.0 / (PATCH * PATCH)) / (
        window_means(cells, 0, window, groups) * window_means(cells, 1, window, groups)
    )
    sums = dot_exact(raw[...].reshape(WIN * 16, 1280), select[...]).reshape(WIN, 16, 128)
    pad = jnp.zeros((120, 128), jnp.float32)
    ends = [
        pltpu.roll(jnp.concatenate([raw_end[n], pad], axis=0).T[:16], 32, axis=1) for n in range(WIN)
    ]
    total = spread_groups([sums[n] + ends[n] for n in range(WIN)], groups)
    unit = (2.0 / (PATCH * PATCH)) ** 2 * HALF / (PATCH * PATCH)
    total = total * (scale * unit)
    lane_all = lax.broadcasted_iota(jnp.int32, (16, 128), 1)
    weight = jnp.where(lane_all >= 64, total * HALF, 0.0)
    down = 1.0 + weight + pltpu.roll(weight, 96, axis=1) + pltpu.roll(weight, 64, axis=1)
    return jnp.where(lane_all >= 64, weight, total) / down


def clear_sums(raw, raw_end):
    raw[:, 12:16, :] = jnp.zeros((WIN, 4, 1280), jnp.float32)
    raw_end[...] = jnp.zeros((WIN, 8, 128), jnp.float32)


def early_step(pair):
    return pair // 4, 1 + pair % 4


def tail_step(pair):
    return 2, 1 + pair


def edge_step(pair):
    return pair // 6, pair % 6


def late_step(pair):
    return pair // 2, 5 * (pair % 2)


def inner_rows(
    members, step_of, pairs, form, first, second, mix_rows, mix_cols, sign_cols, select, window,
    grp, fa, fb, cells, raw, raw_end, *work,
):
    lo, hi = INNER_LO - TOP, INNER_HI - TOP
    raw[...] = jnp.zeros((WIN, 16, 1280), jnp.float32)
    raw_end[...] = jnp.zeros((WIN, 8, 128), jnp.float32)
    for sec, dst in ((0, fa), (1, fb)):
        cells[sec] = jnp.zeros((24, 256 * WIN), jnp.float32)
        for n in members:
            pixels = group_pixels(lambda c: form[c - 1, sec, lo:hi, :], sec, INNER_GROUPS[n])
            grp[sec, n] = pixels
            dst[n] = dot(pixels, first[...]).astype(jnp.bfloat16)
            cell_squares(grp, sec, n, cells, 2, 13, INNER_LO)
    run_steps(step_of, pairs, INNER_LO, fa, fb, second, mix_rows, mix_cols, sign_cols, raw, raw_end, work)
    return finish(raw, raw_end, cells, select, window, INNER_GROUPS)


def early_kernel(*refs):
    out = refs[8]
    out[...] = inner_rows((0, 1), early_step, 8, *refs[:8], *refs[9:])


def tail_kernel(early, late, edge, valid, *refs):
    out, fields = refs[8:10]
    row = lax.broadcasted_iota(jnp.int32, (16, 128), 0)
    lane = lax.broadcasted_iota(jnp.int32, (16, 128), 1) % 32
    own = inner_rows((2,), tail_step, 4, *refs[:8], *refs[10:])
    own = jnp.where(lane < 9, early[...], own)
    own = jnp.where((row >= 2) & (row < 10), own, late[...])
    result = jnp.where((lane >= 3) & (lane < 12), own, edge[...])
    out[...] = result
    fields[...] = mesh_fields(result, valid)[0]


def mesh_fields(result, valid):
    row = lax.broadcasted_iota(jnp.int32, (16, 128), 0)
    lane = lax.broadcasted_iota(jnp.int32, (16, 128), 1)
    column = lane % 32
    inside = (row < 12) & (lane < 96) & (column >= SWEEPS) & (column < SWEEPS + 16)
    flags = jnp.concatenate([valid[...].astype(jnp.float32), jnp.zeros((12, 112), jnp.float32)], axis=1)
    flags = jnp.concatenate([flags, jnp.zeros((4, 128), jnp.float32)], axis=0)
    flags = sum(pltpu.roll(flags, SWEEPS + 32 * kind, axis=1) for kind in range(3))
    fields = flags * pltpu.roll(jnp.where(row < 12, result, 0.0), SWEEPS, axis=1)
    fields = fields + jnp.where(lane >= 64, 4.0 * stiffness, 0.0)
    return jnp.where(inside, fields, 0.0), column


def edge_kernel(
    form, top, bottom, left, right, valid, first, second, mix_rows, mix_cols, sign_cols, select, window,
    out, to_right, to_left, frame, grp, fa, fb, cells, raw, raw_end, *work,
):
    clear_sums(raw, raw_end)
    for sec, dst in ((0, fa), (1, fb)):
        frame[sec, 0] = left[sec]
        frame[sec, 9] = right[sec]
        for c in (1, 2, 3, 6, 7, 8):
            frame_column(form, top, bottom, frame, sec, c, FRAME_H, FRAME_H)
        for n, g in enumerate(EDGE_GROUPS):
            pixels = group_pixels(lambda c: frame[sec, c], sec, g)
            grp[sec, n] = pixels
            dst[n] = dot(pixels, first[...]).astype(jnp.bfloat16)
            cell_squares(grp, sec, n, cells, 0, 15, 0)
        cells[sec, 15:24, :] = jnp.zeros((9, 256 * WIN), jnp.float32)
    run_steps(edge_step, 18, 0, fa, fb, second, mix_rows, mix_cols, sign_cols, raw, raw_end, work)
    result = finish(raw, raw_end, cells, select, window, EDGE_GROUPS)
    out[...] = result
    fields, column = mesh_fields(result, valid)
    last = jnp.where((column >= 16) & (column < 16 + SWEEPS), fields, 0.0)
    to_right[...] = pltpu.roll(last, 112, axis=1)
    head = jnp.where((column >= SWEEPS) & (column < 2 * SWEEPS), fields, 0.0)
    to_left[...] = pltpu.roll(head, 16, axis=1)


def late_kernel(
    form, top, bottom, first, second, mix_rows, mix_cols, sign_cols, select, window,
    out, frame, grp, fa, fb, cells, raw, raw_end, *work,
):
    upper, lower = 208, 400
    clear_sums(raw, raw_end)
    raw[:, 2:10, :] = jnp.zeros((WIN, 8, 1280), jnp.float32)
    for sec, dst in ((0, fa), (1, fb)):
        cells[sec] = jnp.zeros((24, 256 * WIN), jnp.float32)
        for c in range(1, 8):
            frame_column(form, top, bottom, frame, sec, c, upper, lower)
        for n, g in enumerate(INNER_GROUPS):
            for lo, hi in ((0, upper), (lower, FRAME_H)):
                pixels = group_pixels(lambda c: frame[sec, c, lo:hi, :], sec, g)
                grp[sec, n, lo:hi, :] = pixels
                dst[n, lo:hi, :] = dot(pixels, first[...]).astype(jnp.bfloat16)
            cell_squares(grp, sec, n, cells, 0, 5, 0)
            cell_squares(grp, sec, n, cells, 10, 15, 0)
    run_steps(late_step, 6, 0, fa, fb, second, mix_rows, mix_cols, sign_cols, raw, raw_end, work)
    out[...] = finish(raw, raw_end, cells, select, window, INNER_GROUPS)


def relax_kernel(result, fields, above, beneath, flow, mesh_out):
    frame = jnp.concatenate(
        [above[...][1:4], fields[...][:12], beneath[...][:SWEEPS], jnp.zeros((6, 128), jnp.float32)],
        axis=0,
    )
    lane = lax.broadcasted_iota(jnp.int32, (24, 128), 1)
    below = jnp.where(lane < 32, pltpu.roll(frame, 64, axis=1), pltpu.roll(frame, 96, axis=1))
    inside = (below > 0.0) & (lane < 64)
    rest = jnp.where(inside, 1.0 / jnp.where(inside, below, 1.0), 0.0)
    mesh = jnp.where(lane < 64, frame, 0.0)
    pull = mesh * jnp.where(inside, below - 4.0 * stiffness, 0.0)
    for _ in range(SWEEPS):
        around = (
            pltpu.roll(mesh, 1, axis=0)
            + pltpu.roll(mesh, 23, axis=0)
            + pltpu.roll(mesh, 1, axis=1)
            + pltpu.roll(mesh, 127, axis=1)
        )
        mesh = (pull + stiffness * around) * rest
    for kind in range(2):
        flow[:, kind, :] = result[0:12, 32 * kind : 32 * kind + 16]
        mesh_out[:, kind, :] = mesh[SWEEPS : SWEEPS + 12, 32 * kind + SWEEPS : 32 * kind + SWEEPS + 16]


def work_shapes():
    return [
        pltpu.VMEM((2, 2, 2 * ROWS, 512), jnp.float32),
        pltpu.VMEM((2, 2 * ROWS, 512), jnp.bfloat16),
        pltpu.VMEM((2, 2, HALF + 8, 512), jnp.float32),
        pltpu.VMEM((2, 2 * ROWS, 256), jnp.float32),
    ]


SUM_SHAPES = (
    ((2, 24, 256 * WIN), jnp.float32),
    ((WIN, 16, 1280), jnp.float32),
    ((WIN, 8, 128), jnp.float32),
)


def sum_shapes(make):
    return [make(*shape) for shape in SUM_SHAPES]


def grow_params(mib):
    return pltpu.CompilerParams(vmem_limit_bytes=mib << 20)


def frame_shapes():
    return [
        pltpu.VMEM((2, 10, FRAME_H, 128), jnp.bfloat16),
        pltpu.VMEM((2, WIN, FRAME_H, 256), jnp.bfloat16),
        pltpu.VMEM((WIN, FRAME_H, 512), jnp.bfloat16),
        pltpu.VMEM((WIN, FRAME_H, 512), jnp.bfloat16),
        *sum_shapes(pltpu.VMEM),
        *work_shapes(),
    ]


SMALL = jax.ShapeDtypeStruct((16, 128), jnp.float32)


def inner_shapes():
    height = INNER_HI - INNER_LO
    return [
        pltpu.VMEM((2, WIN, height, 256), jnp.bfloat16),
        pltpu.VMEM((WIN, height, 512), jnp.bfloat16),
        pltpu.VMEM((WIN, height, 512), jnp.bfloat16),
        *sum_shapes(pltpu.VMEM),
        *work_shapes(),
    ]


def correlate_early(form, consts):
    return pl.pallas_call(
        early_kernel,
        out_shape=SMALL,
        in_specs=[VMEM_SPEC] * 8,
        out_specs=VMEM_SPEC,
        scratch_shapes=inner_shapes(),
        compiler_params=grow_params(20),
    )(form, *consts)


def correlate_tail(early, late, edge, valid, form, consts):
    return pl.pallas_call(
        tail_kernel,
        out_shape=(SMALL,) * 2,
        in_specs=[VMEM_SPEC] * 12,
        out_specs=(VMEM_SPEC,) * 2,
        scratch_shapes=inner_shapes(),
        compiler_params=grow_params(20),
    )(early, late, edge, valid, form, *consts)


def correlate_edge(form, top, bottom, left, right, valid, consts):
    return pl.pallas_call(
        edge_kernel,
        out_shape=(SMALL,) * 3,
        in_specs=[VMEM_SPEC] * 13,
        out_specs=(VMEM_SPEC,) * 3,
        scratch_shapes=frame_shapes(),
        compiler_params=grow_params(24),
    )(form, top, bottom, left, right, valid, *consts)


def correlate_late(form, top, bottom, consts):
    return pl.pallas_call(
        late_kernel,
        out_shape=SMALL,
        in_specs=[VMEM_SPEC] * 10,
        out_specs=VMEM_SPEC,
        scratch_shapes=frame_shapes(),
        compiler_params=grow_params(24),
    )(form, top, bottom, *consts)


def relax(result, fields, above, beneath):
    field = jax.ShapeDtypeStruct((12, 2, 16), jnp.float32)
    flow, mesh = pl.pallas_call(
        relax_kernel,
        out_shape=(field, field),
        in_specs=[VMEM_SPEC] * 4,
        compiler_params=grow_params(8),
    )(result, fields, above, beneath)
    return flow.transpose(1, 0, 2), mesh.transpose(1, 0, 2)


def pack_kernel(*refs):
    sources, target, rows, held, arrived = refs[:6], refs[6], refs[7], refs[8:14], refs[14]
    out, sent_out = refs[15:]
    copies = [pltpu.make_async_copy(src, dst, arrived.at[n]) for n, (src, dst) in enumerate(zip(sources, held))]
    for copy in copies:
        copy.start()
    for copy in copies:
        copy.wait()
    a_tiles, b_tiles, a_owner, b_owner, a_offset, b_offset = held
    count = a_tiles.shape[0]
    owners = jnp.concatenate([a_owner[...], b_owner[...]], axis=1)
    slot = lax.broadcasted_iota(jnp.int32, (128, 2 * count), 0)
    select = jnp.where(slot == owners, 1.0, 0.0).astype(jnp.bfloat16)
    zero = lambda width: jnp.zeros((count, width), jnp.bfloat16)

    def position(offset):
        row = offset[0:1, :].astype(jnp.float32)
        col = offset[1:2, :].astype(jnp.float32)
        code = jnp.floor(row * (TX / TILE_H) + col * (1.0 / TILE_W) + 1.5)
        code = jnp.concatenate([code, jnp.zeros((1, 128 - count), jnp.float32)], axis=1)
        return jnp.broadcast_to(code, (128, 128)).T[:count]

    def piece(tiles, start, width):
        return tiles[:, start : start + width]

    lane = lax.broadcasted_iota(jnp.int32, (count, 128), 1)
    code_a = jnp.where(lane == 64, position(a_offset), 0.0).astype(jnp.bfloat16)
    code_b = jnp.where(lane == 96, position(b_offset), 0.0).astype(jnp.bfloat16)

    def send_row(y):
        if y < TILE_H:
            a_part = jnp.concatenate([piece(a_tiles, TILE_W * y, TILE_W), zero(SPLIT)], axis=1)
            b_part = jnp.concatenate([zero(TILE_W), piece(b_tiles, TILE_W * y, SPLIT)], axis=1)
        elif y < TILE_H + 8:
            u = y - TILE_H
            a_part = zero(128)
            b_part = jnp.concatenate(
                [piece(b_tiles, TILE_W * (8 * k + u) + SPLIT, LANES) for k in range(4)], axis=1
            )
        else:
            u = y - TILE_H - 8
            a_part = code_a
            b_part = jnp.concatenate(
                [piece(b_tiles, TILE_W * (32 + u) + SPLIT, LANES), zero(96)], axis=1
            )
            b_part = b_part + code_b
        return jnp.concatenate([a_part, b_part], axis=0)

    for y in range(0, SLOT_H, 2):
        both = jnp.concatenate([send_row(y), send_row(y + 1)], axis=1)
        sent = dot(select, both)
        rows[pl.ds(y, 128, stride=SLOT_H), :] = sent[:, :128]
        rows[pl.ds(y + 1, 128, stride=SLOT_H), :] = sent[:, 128:]

    def flush(n, carry):
        start = pl.multiple_of(8 * SLOT_H * n, 8)
        block = rows[pl.ds(start, 8 * SLOT_H), :].reshape(8, SLOT_H, 128)
        out[pl.ds(8 * n, 8)] = block.astype(jnp.bfloat16)
        return carry

    sends = []
    for part in range(4):
        lax.fori_loop(4 * part, 4 * part + 4, flush, 0)
        slots = pl.ds(32 * part, 32)
        sends.append(pltpu.make_async_copy(out.at[slots], target.at[slots], sent_out.at[part]))
        sends[-1].start()
    for send in sends:
        send.wait()


def place_kernel(got, form, up, down, low, high, rows, plane_a, plane_b):
    def widen(n, carry):
        start = pl.multiple_of(8 * SLOT_H * n, 8)
        block = got[pl.ds(8 * n, 8)].astype(jnp.float32)
        rows[pl.ds(start, 8 * SLOT_H), :] = block.reshape(8 * SLOT_H, 128)
        return carry

    lax.fori_loop(0, 16, widen, 0)
    codes = rows[pl.ds(TILE_H + 8, 128, stride=SLOT_H), :]
    wanted = lax.broadcasted_iota(jnp.int32, (128, 128), 1).astype(jnp.float32) + 1.0
    pick = lambda col: jnp.where(codes[:, col : col + 1] == wanted, 1.0, 0.0).T[:96]
    select_a = pick(64)
    select_b = pick(96)
    select = jnp.concatenate([select_a, select_b], axis=0).astype(jnp.bfloat16)
    select_b = select_b.astype(jnp.bfloat16)

    def slot_row(y):
        return rows[pl.ds(y, 128, stride=SLOT_H), :].astype(jnp.bfloat16)

    for plane in (plane_a, plane_b):
        for t in range(TX):
            plane[FORM_H * t : FORM_H * t + 8, :] = jnp.zeros((8, 128), jnp.float32)
            plane[FORM_H * t + 480 : FORM_H * t + 488, :] = jnp.zeros((8, 128), jnp.float32)
    lane = lax.broadcasted_iota(jnp.int32, (96, 128), 1)
    tail = lane < LANES

    for u in range(0, 8, 2):
        tails = jnp.concatenate([slot_row(TILE_H + u + v + w) for v in range(2) for w in (0, 8)], axis=1)
        tails = dot(select_b, tails)
        for k in range(5):
            y = 8 * k + u
            main = dot(select, jnp.concatenate([slot_row(y), slot_row(y + 1)], axis=1))
            for v in range(2):
                part_a = main[:96, 128 * v : 128 * v + 128]
                part_b = main[96:, 128 * v : 128 * v + 128]
                rest = tails[:, 256 * v : 256 * v + 128] if k < 4 else tails[:, 256 * v + 128 : 256 * v + 256]
                if 0 < k < 4:
                    rest = pltpu.roll(rest, 128 - LANES * k, axis=1)
                part_b = jnp.where(tail, rest, part_b)
                for ty in range(TY):
                    where = pl.ds(TILE_H * ty + y + v + 4, TX, stride=FORM_H)
                    plane_a[where, :] = part_a[TX * ty : TX * ty + TX]
                    plane_b[where, :] = part_b[TX * ty : TX * ty + TX]

    for sec, plane in ((0, plane_a), (1, plane_b)):
        for t in range(TX):
            block = plane[FORM_H * t : FORM_H * t + FORM_H, :].astype(jnp.bfloat16)
            form[t, sec] = block
            for side, at in ((low, 0), (high, TX - 1)):
                if t == at:
                    side[sec, 0:TOP, :] = jnp.zeros((TOP, 128), jnp.bfloat16)
                    side[sec, TOP : TOP + FORM_H, :] = block
                    side[sec, TOP + FORM_H :, :] = jnp.zeros((FRAME_H - TOP - FORM_H, 128), jnp.bfloat16)
            up[t, sec] = plane[FORM_H * t : FORM_H * t + EDGE_H, :].astype(jnp.bfloat16)
            down[t, sec] = plane[FORM_H * t + 424 : FORM_H * t + 488, :].astype(jnp.bfloat16)


def pack(*arrays):
    return pl.pallas_call(
        pack_kernel,
        out_shape=jax.ShapeDtypeStruct((128, SLOT_H, 128), jnp.bfloat16),
        in_specs=[pl.BlockSpec(memory_space=pltpu.HBM)] * 6,
        out_specs=pl.BlockSpec(memory_space=pltpu.HBM),
        scratch_shapes=[
            pltpu.VMEM((128 * SLOT_H, 128), jnp.float32),
            *[pltpu.VMEM(x.shape, x.dtype) for x in arrays],
            pltpu.SemaphoreType.DMA((6,)),
            pltpu.VMEM((128, SLOT_H, 128), jnp.bfloat16),
            pltpu.SemaphoreType.DMA((4,)),
        ],
        compiler_params=pltpu.CompilerParams(vmem_limit_bytes=60 << 20),
    )(*arrays)


def place(got):
    edge = jax.ShapeDtypeStruct((TX, 2, EDGE_H, 128), jnp.bfloat16)
    side = jax.ShapeDtypeStruct((2, FRAME_H, 128), jnp.bfloat16)
    return pl.pallas_call(
        place_kernel,
        out_shape=(jax.ShapeDtypeStruct((TX, 2, FORM_H, 128), jnp.bfloat16), edge, edge, side, side),
        scratch_shapes=[
            pltpu.VMEM((128 * SLOT_H, 128), jnp.float32),
            pltpu.VMEM((TX * FORM_H, 128), jnp.float32),
            pltpu.VMEM((TX * FORM_H, 128), jnp.float32),
        ],
        in_specs=[VMEM_SPEC],
        out_specs=(VMEM_SPEC,) * 5,
        compiler_params=pltpu.CompilerParams(vmem_limit_bytes=24 << 20),
    )(got)


def shifted(block, axis, step):
    count = lax.axis_size(axis)
    pairs = [(i, i + step) for i in range(count) if 0 <= i + step < count]
    return lax.ppermute(block, axis, pairs)


def column(side, top, bottom, t):
    grow = lambda x, low, high: jnp.pad(x[t], ((0, 0), (low, high), (0, 0)))
    return side + grow(top, 0, FRAME_H - EDGE_H) + grow(bottom, 536, FRAME_H - 536 - EDGE_H)


def per_device(a_tiles, a_owner, a_offset, b_tiles, b_owner, b_offset, patch_valid):
    packed = pack(a_tiles, b_tiles, a_owner[None], b_owner[None], a_offset.T, b_offset.T)
    got = lax.all_to_all(packed, ("row", "col"), split_axis=0, concat_axis=0, tiled=True)
    form, up, down, low, high = place(got)
    consts = tables()
    top = shifted(down, "row", 1)
    bottom = shifted(up, "row", -1)
    early = correlate_early(form, consts)
    left = shifted(column(high, top, bottom, TX - 1), "col", 1)
    right = shifted(column(low, top, bottom, 0), "col", -1)
    late = correlate_late(form, top, bottom, consts)
    edge, to_right, to_left = correlate_edge(form, top, bottom, left, right, patch_valid, consts)
    from_left = shifted(to_right, "col", 1)
    from_right = shifted(to_left, "col", -1)
    result, fields = correlate_tail(early, late, edge, patch_valid, form, consts)
    fields = fields + from_left + from_right
    above = shifted(fields[8:16], "row", 1)
    beneath = shifted(fields[0:8], "row", -1)
    return relax(result, fields, above, beneath)


def solution(mesh):
    in_specs = (
        P(("row", "col"), None),
        P(("row", "col")),
        P(("row", "col"), None),
        P(("row", "col"), None),
        P(("row", "col")),
        P(("row", "col"), None),
        P("row", "col"),
    )
    out_specs = (P(None, "row", "col"), P(None, "row", "col"))
    return jax.shard_map(
        per_device, mesh=mesh, in_specs=in_specs, out_specs=out_specs, check_vma=False
    )
```
